128 devices in a mesh: seq: 8 (over z, core), tp: 16 (over y, x).
Axes of the slice: x: 4, y: 4, z: 4, core: 2. Of those that a mesh axis runs over, the one named last changes fastest.
Arguments:
- inputs: bfloat16 [8192, 4096], P('seq'), may hold values from -6 to 6
- cotangent: bfloat16 [8192, 4096], P('seq'), may hold values from -6 to 6
- w_in: bfloat16 [4096, 5120], P(None, 'tp'), may hold values from -0.125 to 0.125
- conv_w: float32 [3, 5120], P(None, 'tp'), may hold values from -3.5 to 3.5
- norm_gain: float32 [4096], P('tp'), may hold values from 0.25 to 1.75
- w_out: bfloat16 [4096, 4096], P('tp'), may hold values from -0.125 to 0.125
- keep_flags: int32 [32], P('tp'), may hold values 0 or 1
Outputs:
- layer_out: bfloat16 [8192, 4096], P('seq', 'tp')
- input_grad: bfloat16 [8192, 4096], P('seq', 'tp')
The draws below stay inside these ranges and needn't reach their ends.
All inputs are finite; a program needn't handle non-finite values. No bound on the sum of `keep_flags` on one device may be relied on, other than what follows from the above.
Results may differ from the reference program's by a relative error of at most 0.0071.
Values may be sent and summed in bfloat16 or wider, within the bound.
A program may use at most 192 MiB of HBM per device.

```python
from functools import partial
import jax
import jax.numpy as jnp
import numpy as np
from jax import lax

D = 4096
H = 32
FEAT = 16
DV = 128
EXP = 153
TOK_DEV = 1024
TOKENS = 8192
N_SEQ = 8


def set_ends(drawn, rng, smallest, high):
    index_at = [jax.random.randint(jax.random.fold_in(rng, axis), (), 0, length) for axis, length in enumerate(drawn.shape)]
    main_axis = drawn.shape.index(max(drawn.shape))
    next_to = index_at[:main_axis] + [(index_at[main_axis] + 1) % drawn.shape[main_axis]] + index_at[main_axis + 1:]
    return drawn.at[tuple(index_at)].set(smallest).at[tuple(next_to)].set(high)


def with_spikes(drawn, own_key, source, target, parts, factor):
    owner, partner = [(jnp.arange(drawn.shape[axis_at]) // (drawn.shape[axis_at] // parts)).reshape([-1 if axis == axis_at else 1 for axis in range(drawn.ndim)]) for axis_at in (source, target)]
    chosen = jax.random.permutation(own_key, parts)[partner]
    strong = (owner == chosen) | (owner == (partner + parts // 2) % parts)
    return jnp.where(strong, factor * drawn, drawn)


def block_levels(rng, dims, split, least, top_value):
    def one(axis_at, parts):
        draws = jax.random.uniform(jax.random.fold_in(jax.random.fold_in(rng, 6), axis_at), (parts,), jnp.float32, least / len(split), top_value / len(split))
        return jnp.repeat(jnp.exp(draws), dims[axis_at] // parts).reshape((-1,) + (1,) * (len(dims) - axis_at - 1))

    factor_of = one(*split[0])
    for cut in split[1:]:
        factor_of = factor_of * one(*cut)
    return factor_of


def normal_values(key, dims, width, bound, shards=(), kind=jnp.bfloat16):
    values = jax.random.normal(key, dims, jnp.float32) * width
    if len(shards) > 0:
        values = block_levels(key, dims, shards, -0.22, 0.18) * values
    return jnp.clip(values, min=-bound, max=bound).astype(kind)


def heavy_noise(own_key, shape, spread, bound, shards, heavy, kind=jnp.bfloat16):
    array = spread * jax.random.normal(own_key, shape, jnp.float32)
    if shards:
        array = array * block_levels(own_key, shape, shards, -0.22, 0.18)
    return jnp.clip(with_spikes(array, jax.random.fold_in(own_key, 3), *heavy), -bound, bound).astype(kind)


def setup_inputs(seed: int = 0) -> dict:
    key_of = jax.random.split(jax.random.key(seed), 8)
    return {
        "inputs": normal_values(key_of[0], (TOKENS, D), 1.0, 6.0, ((0, 8),)),
        "cotangent": normal_values(key_of[1], (TOKENS, D), 1.0, 6.0, ((0, 8),)),
        "w_in": heavy_noise(key_of[2], (D, H * (2 * FEAT + DV)), D ** -0.5, 0.125, ((1, 16),), (1, 0, 16, 2.0)),
        "conv_w": normal_values(key_of[3], (3, H * (2 * FEAT + DV)), 3 ** -0.5, 3.5, ((1, 16),), jnp.float32),
        "norm_gain": jnp.clip(1.0 + 0.15 * jax.random.normal(key_of[4], (H * DV,), jnp.float32), 0.25, 1.75),
        "w_out": heavy_noise(key_of[5], (H * DV, D), (H * DV) ** -0.5, 0.125, ((0, 16),), (0, 1, 16, 2.0)),
        "keep_flags": set_ends((jax.random.randint(key_of[6], (H,), 0, 4) < 3).astype(jnp.int32), jax.random.fold_in(key_of[6], 1), 0, 1),
    }


epsilon = 1e-06
highest = lax.Precision.HIGHEST

def pair_table(feature_dim):
    selector = np.zeros((feature_dim * feature_dim, feature_dim * (feature_dim + 1) // 2), np.float32)
    column = 0
    for row_index in range(feature_dim):
        for col_index in range(row_index, feature_dim):
            selector[row_index * feature_dim + col_index, column] = 0.7071067811865476 if row_index == col_index else 1.0
            column = column + 1
    return selector

def taylor_features(scaled, selector):
    outer_prod = scaled[..., :, None] * scaled[..., None, :]
    flattened = outer_prod.reshape(scaled.shape[:-1] + (scaled.shape[-1] * scaled.shape[-1],))
    pair_terms = jnp.einsum('thp,pm->thm', flattened, selector, precision=highest)
    constant = jnp.ones(scaled.shape[:-1] + (1,), scaled.dtype)
    return jnp.concatenate([constant, scaled, pair_terms], -1)

def causal_mask(row_total):
    return jnp.arange(row_total)[:, None] >= jnp.arange(row_total)[None, :]

def conv_forward(extended, conv_w):
    widened = extended.astype(jnp.float32)
    mixed = conv_w[0] * widened[2:] + conv_w[1] * widened[1:-1] + conv_w[2] * widened[:-2]
    return mixed.astype(jnp.bfloat16)

def conv_backward(extended_grad, conv_w):
    mixed = conv_w[0] * extended_grad[:-2] + conv_w[1] * extended_grad[1:-1] + conv_w[2] * extended_grad[2:]
    return mixed.astype(jnp.bfloat16)

def split_heads(convolved, head_count):
    widened = convolved.astype(jnp.float32).reshape(convolved.shape[0], head_count, 2 * FEAT + DV)
    return (widened[:, :, :FEAT], widened[:, :, FEAT:2 * FEAT], widened[:, :, 2 * FEAT:])

def block_forward(queries, key_part, values, selector):
    quarter_root = FEAT ** (-0.25)
    logits = jnp.einsum('thf,shf->hts', queries, key_part, precision=highest) * (quarter_root * quarter_root)
    causal = causal_mask(queries.shape[0])
    weights = jnp.where(causal[None], 1.0 + logits + 0.5 * logits * logits, 0.0)
    query_features = taylor_features(queries * quarter_root, selector)
    key_features = taylor_features(key_part * quarter_root, selector)
    local_state = jnp.einsum('the,thv->hev', key_features, values, precision=highest)
    local_mix = jnp.einsum('hts,shv->thv', weights, values, precision=highest)
    return (logits, weights, query_features, key_features, local_state, local_mix)

def head_norm(numerator, head_gains, keep_scale):
    radius = jnp.sqrt(lax.optimization_barrier(jnp.mean(numerator * numerator, -1, keepdims=True)) + epsilon)
    normed = numerator / radius
    output = (normed * head_gains[None] * keep_scale[None, :, None]).astype(jnp.bfloat16)
    return (radius, normed, output)

def norm_backward(grad_heads, normed, radius, head_gains, keep_scale):
    scaled_grad = grad_heads * head_gains[None] * keep_scale[None, :, None]
    return (scaled_grad - normed * lax.optimization_barrier(jnp.mean(scaled_grad * normed, -1, keepdims=True))) / radius

def block_backward(queries, key_part, values, logits, weights, query_features, key_features, prefix_state, suffix_state, d_numer, selector):
    quarter_root = FEAT ** (-0.25)
    d_values = jnp.einsum('hts,thv->shv', weights, d_numer, precision=highest)
    d_values = d_values + jnp.einsum('she,hev->shv', key_features, suffix_state, precision=highest)
    d_weights = jnp.einsum('thv,shv->hts', d_numer, values, precision=highest)
    causal = causal_mask(queries.shape[0])
    d_logits = jnp.where(causal[None], d_weights * (1.0 + logits), 0.0) * (quarter_root * quarter_root)
    d_queries = jnp.einsum('hts,shf->thf', d_logits, key_part, precision=highest)
    d_keys = jnp.einsum('hts,thf->shf', d_logits, queries, precision=highest)
    d_query_features = jnp.einsum('thv,hev->the', d_numer, prefix_state, precision=highest)
    d_key_features = jnp.einsum('shv,hev->she', values, suffix_state, precision=highest)
    pull_query = jax.vjp(partial(taylor_features, selector=selector), queries * quarter_root)[1]
    pull_key = jax.vjp(partial(taylor_features, selector=selector), key_part * quarter_root)[1]
    d_queries = d_queries + pull_query(d_query_features)[0] * quarter_root
    d_keys = d_keys + pull_key(d_key_features)[0] * quarter_root
    merged = jnp.concatenate([d_queries, d_keys, d_values], -1)
    return merged.reshape(merged.shape[0], -1)

def reference(inputs, cotangent, w_in, conv_w, norm_gain, w_out, keep_flags):
    selector = jnp.asarray(pair_table(FEAT)).astype(jnp.float32)
    width_all = H * (2 * FEAT + DV)
    projected = jnp.dot(inputs, w_in, preferred_element_type=jnp.float32).astype(jnp.bfloat16)
    extended = jnp.concatenate([jnp.zeros((2, width_all), jnp.bfloat16), projected], 0)
    convolved = conv_forward(extended, conv_w)
    blocked = convolved.reshape(N_SEQ, TOK_DEV, width_all)
    head_gains = norm_gain.reshape(H, DV)
    keep_scale = keep_flags.astype(jnp.float32)

    def forward_step(carried_state, block_rows):
        queries, key_part, values = split_heads(block_rows, H)
        logits, weights, query_features, key_features, local_state, local_mix = block_forward(queries, key_part, values, selector)
        numerator = local_mix + jnp.einsum('the,hev->thv', query_features, carried_state, precision=highest)
        radius, normed, output = head_norm(numerator, head_gains, keep_scale)
        return (carried_state + local_state, (carried_state, radius, normed, output))
    initial = jnp.zeros((H, EXP, DV), jnp.float32)
    final_state, saved_values = lax.scan(forward_step, initial, blocked)
    prefixes, all_radius, normals, outputs = saved_values
    flat_output = outputs.reshape(TOKENS, H * DV)
    layer_out = (inputs.astype(jnp.float32) + jnp.dot(flat_output, w_out, preferred_element_type=jnp.float32)).astype(jnp.bfloat16)
    grad_heads = jnp.dot(cotangent, w_out.T, preferred_element_type=jnp.float32).reshape(N_SEQ, TOK_DEV, H, DV)
    d_numers = norm_backward(grad_heads, normals, all_radius, head_gains, keep_scale)

    def backward_step(suffix_state, packed):
        block_rows, prefix_state, d_numer = packed
        queries, key_part, values = split_heads(block_rows, H)
        logits, weights, query_features, key_features, local_state, local_mix = block_forward(queries, key_part, values, selector)
        d_block = block_backward(queries, key_part, values, logits, weights, query_features, key_features, prefix_state, suffix_state, d_numer, selector)
        grad_term = jnp.einsum('the,thv->hev', query_features, d_numer, precision=highest)
        return (suffix_state + grad_term, d_block)
    suffix_final, d_blocks = lax.scan(backward_step, initial, (blocked, prefixes, d_numers), reverse=True)
    d_convolved = d_blocks.reshape(TOKENS, width_all)
    extended_grad = jnp.concatenate([d_convolved, jnp.zeros((2, width_all), jnp.float32)], 0)
    d_projected = conv_backward(extended_grad, conv_w)
    input_grad = (cotangent.astype(jnp.float32) + jnp.dot(d_projected, w_in.T, preferred_element_type=jnp.float32)).astype(jnp.bfloat16)
    return (layer_out, input_grad)
```

```python
from functools import partial

import jax
import jax.numpy as jnp
import numpy as np
from jax import lax
from jax.experimental import pallas as pl
from jax.experimental.pallas import tpu as pltpu
from jax.sharding import PartitionSpec as P

FEAT = 16
DV = 128


epsilon = 1e-06
highest = lax.Precision.HIGHEST


def passed_along(array, axis, by):
    count = lax.axis_size(axis)
    pairs = [(i, i + by) for i in range(count) if 0 <= i + by < count]
    return lax.ppermute(array, axis, pairs)


def entering(part, axis, combine, identity, reverse):
    count = lax.axis_size(axis)
    place = lax.axis_index(axis)
    ahead = count - 1 - place if reverse else place
    gathered = lax.all_gather(part, axis)
    state = jnp.zeros_like(part) + jnp.asarray(identity, part.dtype)

    def one(turn, state):
        source = count - 1 - turn if reverse else turn
        return combine(state, lax.dynamic_index_in_dim(gathered, source, 0, False))

    return lax.fori_loop(0, ahead, one, state)


def pair_table(feature_dim):
    selector = np.zeros(
        (feature_dim * feature_dim, feature_dim * (feature_dim + 1) // 2), np.float32
    )
    column = 0
    for row_index in range(feature_dim):
        for col_index in range(row_index, feature_dim):
            selector[row_index * feature_dim + col_index, column] = (
                0.7071067811865476 if row_index == col_index else 1.0
            )
            column = column + 1
    return selector


def taylor_features(scaled, selector):
    outer_prod = scaled[..., :, None] * scaled[..., None, :]
    flattened = outer_prod.reshape(scaled.shape[:-1] + (scaled.shape[-1] * scaled.shape[-1],))
    pair_terms = jnp.einsum("thp,pm->thm", flattened, selector, precision=highest)
    constant = jnp.ones(scaled.shape[:-1] + (1,), scaled.dtype)
    return jnp.concatenate([constant, scaled, pair_terms], -1)


def causal_mask(row_total):
    return jnp.arange(row_total)[:, None] >= jnp.arange(row_total)[None, :]


def conv_forward(extended, conv_w):
    widened = extended.astype(jnp.float32)
    mixed = conv_w[0] * widened[2:] + conv_w[1] * widened[1:-1] + conv_w[2] * widened[:-2]
    return mixed.astype(jnp.bfloat16)


def conv_backward(extended_grad, conv_w):
    mixed = (
        conv_w[0] * extended_grad[:-2]
        + conv_w[1] * extended_grad[1:-1]
        + conv_w[2] * extended_grad[2:]
    )
    return mixed.astype(jnp.bfloat16)


def split_heads(convolved, head_count):
    widened = convolved.astype(jnp.float32).reshape(convolved.shape[0], head_count, 2 * FEAT + DV)
    return (widened[:, :, :FEAT], widened[:, :, FEAT : 2 * FEAT], widened[:, :, 2 * FEAT :])


def block_forward(queries, key_part, values, selector):
    quarter_root = FEAT ** (-0.25)
    logits = jnp.einsum("thf,shf->hts", queries, key_part, precision=highest) * (
        quarter_root * quarter_root
    )
    causal = causal_mask(queries.shape[0])
    weights = jnp.where(causal[None], 1.0 + logits + 0.5 * logits * logits, 0.0)
    query_features = taylor_features(queries * quarter_root, selector)
    key_features = taylor_features(key_part * quarter_root, selector)
    local_state = jnp.einsum("the,thv->hev", key_features, values, precision=highest)
    local_mix = jnp.einsum("hts,shv->thv", weights, values, precision=highest)
    return (logits, weights, query_features, key_features, local_state, local_mix)


def head_norm(numerator, head_gains, keep_scale):
    radius = jnp.sqrt(jnp.mean(numerator * numerator, -1, keepdims=True) + epsilon)
    normed = numerator / radius
    output = (normed * head_gains[None] * keep_scale[None, :, None]).astype(jnp.bfloat16)
    return (radius, normed, output)


def norm_backward(grad_heads, normed, radius, head_gains, keep_scale):
    scaled_grad = grad_heads * head_gains[None] * keep_scale[None, :, None]
    return (scaled_grad - normed * jnp.mean(scaled_grad * normed, -1, keepdims=True)) / radius


def block_backward(
    queries,
    key_part,
    values,
    logits,
    weights,
    key_features,
    prefix_state,
    suffix_state,
    d_numer,
    selector,
):
    quarter_root = FEAT ** (-0.25)
    d_values = jnp.einsum("hts,thv->shv", weights, d_numer, precision=highest)
    d_values = d_values + jnp.einsum("she,hev->shv", key_features, suffix_state, precision=highest)
    d_weights = jnp.einsum("thv,shv->hts", d_numer, values, precision=highest)
    causal = causal_mask(queries.shape[0])
    d_logits = jnp.where(causal[None], d_weights * (1.0 + logits), 0.0) * (
        quarter_root * quarter_root
    )
    d_queries = jnp.einsum("hts,shf->thf", d_logits, key_part, precision=highest)
    d_keys = jnp.einsum("hts,thf->shf", d_logits, queries, precision=highest)
    d_query_features = jnp.einsum("thv,hev->the", d_numer, prefix_state, precision=highest)
    d_key_features = jnp.einsum("shv,hev->she", values, suffix_state, precision=highest)
    pull_query = jax.vjp(partial(taylor_features, selector=selector), queries * quarter_root)[1]
    pull_key = jax.vjp(partial(taylor_features, selector=selector), key_part * quarter_root)[1]
    d_queries = d_queries + pull_query(d_query_features)[0] * quarter_root
    d_keys = d_keys + pull_key(d_key_features)[0] * quarter_root
    merged = jnp.concatenate([d_queries, d_keys, d_values], -1)
    return merged.reshape(merged.shape[0], -1)


def add_states(earlier, later_part):
    return earlier + later_part


CH = 256
NCH = 4
MESH = pl.DeviceIdType.MESH
NT = (((1,), (1,)), ((), ()))
NN = (((1,), (0,)), ((), ()))
f32 = jnp.float32
bf16 = jnp.bfloat16


def neighbour(along, step):
    place = lax.axis_index("tp")
    column, row = lax.rem(place, 4), lax.div(place, 4)
    if along == "x":
        return row * 4 + lax.rem(column + step, 4)
    return lax.rem(row + step, 4) * 4 + column


def block_at(a_along, a_step, r_along, r_step):
    place = lax.axis_index("tp")
    column, row = lax.rem(place, 4), lax.div(place, 4)
    x_step = a_step if a_along == "x" else r_step
    y_step = a_step if a_along == "y" else r_step
    return lax.rem(row + y_step, 4) * 4 + lax.rem(column + x_step, 4)


def to_device(src, dst, send_sem, recv_sem, place):
    return pltpu.make_async_remote_copy(
        src_ref=src,
        dst_ref=dst,
        send_sem=send_sem,
        recv_sem=recv_sem,
        device_id={"tp": place},
        device_id_type=MESH,
    )


def rows_of(c):
    return pl.ds(pl.multiple_of(c * CH, CH), CH)


def way(c):
    return jnp.where(c < NCH // 2, 1, 3)


class Ring:
    def __init__(self, a, r, held, weight, own, dims, part, landed, relay, keep, res, out, sems):
        self.a, self.r = a, r
        self.held, self.weight, self.own, self.dims = held, weight, own, dims
        self.part, self.landed, self.relay = part, landed, relay
        self.keep, self.res, self.out = keep, res, out
        (self.gs, self.gr, self.ts, self.tr, self.ps, self.pr, self.ws, self.wr, self.wo) = sems

    def weight_copies(self, w_block):
        copies = []
        for d in range(1, 4):
            for k in range(4):
                src = w_block(block_at(self.a, d, self.r, k))
                copies.append(
                    to_device(
                        src,
                        self.weight.at[k, d],
                        self.ws.at[d - 1, k],
                        self.wr.at[d - 1, k],
                        neighbour(self.a, d),
                    )
                )
        return copies

    def own_copies(self, w_block):
        return [
            pltpu.make_async_copy(
                w_block(block_at(self.a, 0, self.r, k)), self.weight.at[k, 0], self.wo.at[k]
            )
            for k in range(4)
        ]

    def direct(self, c, d):
        return to_device(
            self.held.at[0, rows_of(c)],
            self.held.at[d, rows_of(c)],
            self.gs.at[d - 1, c],
            self.gr.at[d - 1, c],
            neighbour(self.a, d),
        )

    def passed_on(self, c):
        return to_device(
            self.held.at[way(c), rows_of(c)],
            self.held.at[2, rows_of(c)],
            self.gs.at[1, c],
            self.gr.at[1, c],
            neighbour(self.a, way(c)),
        )

    def send_own(self, c):
        self.direct(c, 1).start()
        self.direct(c, 3).start()

    def forward(self, c):
        self.direct(c, 1).wait_recv()
        self.direct(c, 3).wait_recv()
        self.passed_on(c).start()

    def tie(self, c):
        return to_device(
            self.part.at[2, rows_of(c)],
            self.relay.at[rows_of(c)],
            self.ts.at[c],
            self.tr.at[c],
            neighbour(self.r, way(c)),
        )

    def side(self, c, d):
        return to_device(
            self.part.at[d, rows_of(c)],
            self.landed.at[d // 2, rows_of(c)],
            self.ps.at[d // 2, c],
            self.pr.at[d // 2, c],
            neighbour(self.r, d),
        )

    def product(self, c, k):
        total = None
        for o in range(4):
            term = lax.dot_general(
                self.held[o, rows_of(c)], self.weight[k, o], self.dims, preferred_element_type=f32
            )
            total = term if total is None else total + term
        return total

    def multiply(self, c):
        self.passed_on(c).wait_recv()
        near, far = way(c), 4 - way(c)
        self.part[2, rows_of(c)] = self.product(c, 2).astype(bf16)
        self.tie(c).start()
        self.part[far, rows_of(c)] = self.product(c, far).astype(bf16)
        self.side(c, far).start()
        self.keep[1, rows_of(c)] = self.product(c, near)
        self.keep[0, rows_of(c)] = self.product(c, 0) + self.res[rows_of(c)].astype(f32)

    def relayed(self, c):
        self.tie(c).wait_recv()
        near = way(c)
        total = self.keep[1, rows_of(c)] + self.relay[rows_of(c)].astype(f32)
        self.part[near, rows_of(c)] = total.astype(bf16)
        self.side(c, near).start()

    def finish(self, c):
        self.side(c, 1).wait_recv()
        self.side(c, 3).wait_recv()
        total = self.keep[0, rows_of(c)] + (
            self.landed[0, rows_of(c)].astype(f32) + self.landed[1, rows_of(c)].astype(f32)
        )
        self.out[rows_of(c)] = total.astype(bf16)

    def drain(self, c):
        self.direct(c, 1).wait_send()
        self.direct(c, 3).wait_send()
        self.passed_on(c).wait_send()
        self.tie(c).wait_send()
        self.side(c, 1).wait_send()
        self.side(c, 3).wait_send()


def ring_semaphores():
    dma = pltpu.SemaphoreType.DMA
    return [
        dma((3, NCH)),
        dma((3, NCH)),
        dma((NCH,)),
        dma((NCH,)),
        dma((2, NCH)),
        dma((2, NCH)),
        dma((3, 4)),
        dma((3, 4)),
        dma((4,)),
    ]


def ring_buffers(rows, width, weight_shape):
    return [
        pltpu.VMEM((4, rows, width), bf16),
        pltpu.VMEM((4, 4) + weight_shape, bf16),
        pltpu.VMEM((4, rows, 256), bf16),
        pltpu.VMEM((2, rows, 256), bf16),
        pltpu.VMEM((rows, 256), bf16),
        pltpu.VMEM((2, rows, 256), f32),
        pltpu.VMEM((rows, 256), bf16),
    ]


def combine_kernel(heads, d_proj, w_out, w_in, inputs, cotangent, layer_out, input_grad, *scratch):
    fwd_bufs, bwd_bufs = scratch[:7], scratch[7:14]
    fwd_sems, bwd_sems = scratch[14:23], scratch[23:32]
    in_sem = scratch[32]
    h_held, h_weight, h_part, h_landed, h_relay, h_keep, h_res = fwd_bufs
    g_held, g_weight, g_part, g_landed, g_relay, g_keep, g_res = bwd_bufs
    fwd = Ring("x", "y", h_held, h_weight, None, NN, h_part, h_landed, h_relay, h_keep, h_res, layer_out, fwd_sems)
    bwd = Ring("y", "x", g_held, g_weight, None, NT, g_part, g_landed, g_relay, g_keep, g_res, input_grad, bwd_sems)

    def out_block(t):
        return w_out.at[:, pl.ds(pl.multiple_of(t * 256, 256), 256)]

    def in_block(t):
        return w_in.at[pl.ds(pl.multiple_of(t * 256, 256), 256)]

    mine = pl.ds(pl.multiple_of(lax.axis_index("tp") * 256, 256), 256)
    local = [
        pltpu.make_async_copy(heads, h_held.at[0], in_sem.at[0]),
        pltpu.make_async_copy(d_proj, g_held.at[0], in_sem.at[1]),
        pltpu.make_async_copy(inputs.at[:, mine], h_res, in_sem.at[2]),
        pltpu.make_async_copy(cotangent.at[:, mine], g_res, in_sem.at[3]),
    ]
    local += fwd.own_copies(out_block) + bwd.own_copies(in_block)
    for copy in local:
        copy.start()
    barrier = pltpu.get_barrier_semaphore()
    for along in ("x", "y"):
        for d in (1, 2, 3):
            pl.semaphore_signal(
                barrier, inc=1, device_id={"tp": neighbour(along, d)}, device_id_type=MESH
            )
    pl.semaphore_wait(barrier, 6)
    weights = fwd.weight_copies(out_block) + bwd.weight_copies(in_block)
    for copy in weights:
        copy.start()
    for copy in local:
        copy.wait()

    @pl.loop(0, NCH)
    def _(c):
        fwd.send_own(c)
        bwd.send_own(c)

    for copy in weights:
        copy.wait()

    @pl.loop(0, NCH + 3)
    def _(i):
        for ring in (fwd, bwd):

            @pl.when(i < NCH)
            def _():
                ring.forward(i)

        for ring in (fwd, bwd):

            @pl.when((i >= 1) & (i < NCH + 1))
            def _():
                ring.multiply(i - 1)

        for ring in (fwd, bwd):

            @pl.when((i >= 2) & (i < NCH + 2))
            def _():
                ring.relayed(i - 2)

        for ring in (fwd, bwd):

            @pl.when(i >= 3)
            def _():
                ring.finish(i - 3)

    @pl.loop(0, NCH)
    def _(c):
        fwd.drain(c)
        bwd.drain(c)


def combine(heads, d_proj, w_out, w_in, inputs, cotangent):
    rows = heads.shape[0]
    whole = pl.BlockSpec(memory_space=pl.ANY)
    result = jax.ShapeDtypeStruct((rows, 256), bf16)
    return pl.pallas_call(
        combine_kernel,
        out_shape=(result, result),
        in_specs=[whole] * 6,
        out_specs=(pl.BlockSpec(memory_space=pltpu.VMEM),) * 2,
        scratch_shapes=ring_buffers(rows, 256, (256, 256))
        + ring_buffers(rows, 320, (256, 320))
        + ring_semaphores()
        + ring_semaphores()
        + [pltpu.SemaphoreType.DMA((4,))],
        compiler_params=pltpu.CompilerParams(
            collective_id=0, has_side_effects=True, vmem_limit_bytes=56 << 20
        ),
    )(heads, d_proj, w_out, w_in, inputs, cotangent)


def per_device(inputs, cotangent, w_in, conv_w, norm_gain, w_out, keep_flags):
    selector = jnp.asarray(pair_table(FEAT)).astype(jnp.float32)
    head_count = keep_flags.shape[0]
    row_count = inputs.shape[0]
    head_gains = norm_gain.reshape(head_count, DV)
    keep_scale = keep_flags.astype(jnp.float32)
    projected = jnp.dot(inputs, w_in, preferred_element_type=jnp.float32).astype(jnp.bfloat16)
    prev_rows = passed_along(projected[-2:], "seq", 1)
    convolved = conv_forward(jnp.concatenate([prev_rows, projected], 0), conv_w)
    queries, key_part, values = split_heads(convolved, head_count)
    logits, weights, query_features, key_features, local_state, local_mix = block_forward(
        queries, key_part, values, selector
    )
    prefix_state = entering(local_state, "seq", add_states, jnp.zeros_like(local_state), False)
    numerator = local_mix + jnp.einsum(
        "the,hev->thv", query_features, prefix_state, precision=highest
    )
    radius, normed, output = head_norm(numerator, head_gains, keep_scale)
    flat_output = output.reshape(row_count, -1)
    grad_heads = jnp.einsum(
        "td,cd->tc", cotangent, w_out, preferred_element_type=jnp.float32
    ).reshape(row_count, head_count, DV)
    d_numer = norm_backward(grad_heads, normed, radius, head_gains, keep_scale)
    grad_term = jnp.einsum("the,thv->hev", query_features, d_numer, precision=highest)
    suffix_state = entering(grad_term, "seq", add_states, jnp.zeros_like(grad_term), True)
    d_convolved = block_backward(
        queries,
        key_part,
        values,
        logits,
        weights,
        key_features,
        prefix_state,
        suffix_state,
        d_numer,
        selector,
    )
    next_rows = passed_along(d_convolved[:2], "seq", -1)
    d_projected = conv_backward(jnp.concatenate([d_convolved, next_rows], 0), conv_w)
    return combine(flat_output, d_projected, w_out, w_in, inputs, cotangent)


def solution(mesh):
    placed = (
        P("seq", None),
        P("seq", None),
        P(None, "tp"),
        P(None, "tp"),
        P("tp"),
        P("tp", None),
        P("tp"),
    )
    return jax.shard_map(
        per_device,
        mesh=mesh,
        in_specs=placed,
        out_specs=(P("seq", "tp"), P("seq", "tp")),
        check_vma=False,
    )
```

```python
from functools import partial

import jax
import jax.numpy as jnp
import numpy as np
from jax import lax
from jax.experimental import pallas as pl
from jax.experimental.pallas import tpu as pltpu
from jax.sharding import PartitionSpec as P

FEAT = 16
DV = 128
LANES = 384
EXP = 256
HEADS = 2
epsilon = 1e-06

CH = 256
NCH = 4
MESH = pl.DeviceIdType.MESH
NT = (((1,), (1,)), ((), ()))
NN = (((1,), (0,)), ((), ()))
TN = (((0,), (0,)), ((), ()))
f32 = jnp.float32
bf16 = jnp.bfloat16


def neighbour(along, step):
    place = lax.axis_index("tp")
    column, row = lax.rem(place, 4), lax.div(place, 4)
    if along == "x":
        return row * 4 + lax.rem(column + step, 4)
    return lax.rem(row + step, 4) * 4 + column


def block_at(a_along, a_step, r_along, r_step):
    place = lax.axis_index("tp")
    column, row = lax.rem(place, 4), lax.div(place, 4)
    x_step = a_step if a_along == "x" else r_step
    y_step = a_step if a_along == "y" else r_step
    return lax.rem(row + y_step, 4) * 4 + lax.rem(column + x_step, 4)


def to_device(src, dst, send_sem, recv_sem, place):
    return pltpu.make_async_remote_copy(
        src_ref=src,
        dst_ref=dst,
        send_sem=send_sem,
        recv_sem=recv_sem,
        device_id={"tp": place},
        device_id_type=MESH,
    )


def rows_of(c):
    return pl.ds(pl.multiple_of(c * CH, CH), CH)


def way(c):
    return jnp.where(c < NCH // 2, 1, 3)


class Ring:
    def __init__(self, a, r, held, weight, own, dims, part, landed, relay, keep, res, out, sems):
        self.a, self.r = a, r
        self.held, self.weight, self.own, self.dims = held, weight, own, dims
        self.part, self.landed, self.relay = part, landed, relay
        self.keep, self.res, self.out = keep, res, out
        (self.gs, self.gr, self.ts, self.tr, self.ps, self.pr, self.ws, self.wr, self.wo) = sems

    def weight_copies(self, w_block):
        copies = []
        for d in range(1, 4):
            for k in range(4):
                src = w_block(block_at(self.a, d, self.r, k))
                copies.append(
                    to_device(
                        src,
                        self.weight.at[k, d],
                        self.ws.at[d - 1, k],
                        self.wr.at[d - 1, k],
                        neighbour(self.a, d),
                    )
                )
        return copies

    def own_copies(self, w_block):
        return [
            pltpu.make_async_copy(
                w_block(block_at(self.a, 0, self.r, k)), self.weight.at[k, 0], self.wo.at[k]
            )
            for k in range(4)
        ]

    def direct(self, c, d):
        return to_device(
            self.held.at[0, rows_of(c)],
            self.held.at[d, rows_of(c)],
            self.gs.at[d - 1, c],
            self.gr.at[d - 1, c],
            neighbour(self.a, d),
        )

    def passed_on(self, c):
        return to_device(
            self.held.at[way(c), rows_of(c)],
            self.held.at[2, rows_of(c)],
            self.gs.at[1, c],
            self.gr.at[1, c],
            neighbour(self.a, way(c)),
        )

    def send_own(self, c):
        self.direct(c, 1).start()
        self.direct(c, 3).start()

    def forward(self, c):
        self.direct(c, 1).wait_recv()
        self.direct(c, 3).wait_recv()
        self.passed_on(c).start()

    def tie(self, c):
        return to_device(
            self.part.at[2, rows_of(c)],
            self.relay.at[rows_of(c)],
            self.ts.at[c],
            self.tr.at[c],
            neighbour(self.r, way(c)),
        )

    def side(self, c, d):
        return to_device(
            self.part.at[d, rows_of(c)],
            self.landed.at[d // 2, rows_of(c)],
            self.ps.at[d // 2, c],
            self.pr.at[d // 2, c],
            neighbour(self.r, d),
        )

    def product(self, c, k):
        total = None
        for o in range(4):
            term = lax.dot_general(
                self.held[o, rows_of(c)], self.weight[k, o], self.dims, preferred_element_type=f32
            )
            total = term if total is None else total + term
        return total

    def multiply(self, c):
        self.passed_on(c).wait_recv()
        near, far = way(c), 4 - way(c)
        self.part[2, rows_of(c)] = self.product(c, 2).astype(bf16)
        self.tie(c).start()
        self.part[far, rows_of(c)] = self.product(c, far).astype(bf16)
        self.side(c, far).start()
        self.keep[1, rows_of(c)] = self.product(c, near)
        self.keep[0, rows_of(c)] = self.product(c, 0) + self.res[rows_of(c)].astype(f32)

    def relayed(self, c):
        self.tie(c).wait_recv()
        near = way(c)
        total = self.keep[1, rows_of(c)] + self.relay[rows_of(c)].astype(f32)
        self.part[near, rows_of(c)] = total.astype(bf16)
        self.side(c, near).start()

    def finish(self, c):
        self.side(c, 1).wait_recv()
        self.side(c, 3).wait_recv()
        total = self.keep[0, rows_of(c)] + (
            self.landed[0, rows_of(c)].astype(f32) + self.landed[1, rows_of(c)].astype(f32)
        )
        self.out[rows_of(c)] = total.astype(bf16)

    def drain(self, c):
        self.direct(c, 1).wait_send()
        self.direct(c, 3).wait_send()
        self.passed_on(c).wait_send()
        self.tie(c).wait_send()
        self.side(c, 1).wait_send()
        self.side(c, 3).wait_send()


def ring_semaphores():
    dma = pltpu.SemaphoreType.DMA
    return [
        dma((3, NCH)),
        dma((3, NCH)),
        dma((NCH,)),
        dma((NCH,)),
        dma((2, NCH)),
        dma((2, NCH)),
        dma((3, 4)),
        dma((3, 4)),
        dma((4,)),
    ]


def ring_buffers(rows, width, weight_shape):
    return [
        pltpu.VMEM((4, rows, width), bf16),
        pltpu.VMEM((4, 4) + weight_shape, bf16),
        pltpu.VMEM((4, rows, 256), bf16),
        pltpu.VMEM((2, rows, 256), bf16),
        pltpu.VMEM((rows, 256), bf16),
        pltpu.VMEM((2, rows, 256), f32),
        pltpu.VMEM((rows, 256), bf16),
    ]


def selectors():
    first = np.zeros((4, 128, EXP), np.float32)
    second = np.zeros((4, 128, EXP), np.float32)
    rows = np.zeros((8, EXP), np.float32)
    rows[0, 0] = rows[1, 0] = rows[2, 0] = 1.0
    for group in range(4):
        base = group * FEAT
        for i in range(FEAT):
            first[group, base + i, 1 + i] = 1.0
            rows[1, 1 + i] = 1.0
            rows[2, 1 + i] = 0.25
        e = 1 + FEAT
        for i in range(FEAT):
            for j in range(i, FEAT):
                first[group, base + i, e] = 1.0
                second[group, base + j, e] = 1.0
                rows[2, e] = 1 / 32 if i == j else 1 / 16
                e += 1
    moves = np.zeros((4, 128, 128), np.float32)
    for h in range(HEADS):
        for i in range(FEAT):
            q, k = 2 * h * FEAT + i, (2 * h + 1) * FEAT + i
            moves[2 * h, q, k] = 1.0
            moves[2 * h + 1, k, q] = 1.0
    return first, second, rows, moves


def dot(a, b, dims=NN):
    return lax.dot_general(a, b, dims, preferred_element_type=f32)


def one_if(condition):
    return jnp.where(condition, 1.0, 0.0).astype(f32)


def to_seq(src, dst, send_sem, recv_sem, place):
    return pltpu.make_async_remote_copy(
        src_ref=src,
        dst_ref=dst,
        send_sem=send_sem,
        recv_sem=recv_sem,
        device_id={"seq": place},
        device_id_type=MESH,
    )


class Carry:
    def __init__(self, earlier, local, state, bufs, sems):
        self.earlier, self.local, self.state = earlier, local, state
        self.sa, self.ra, self.sb, self.rb, self.sc, self.rc = bufs
        self.pair_sems, self.zs, self.zr = sems
        place = lax.axis_index("seq")
        self.core, self.z = lax.rem(place, 2), lax.div(place, 2)
        self.partner = self.z * 2 + (1 - self.core)

    def swap(self):
        return to_seq(self.sa, self.ra, self.pair_sems.at[0], self.pair_sems.at[1], self.partner)

    def give(self):
        return to_seq(self.sc, self.rc, self.pair_sems.at[2], self.pair_sems.at[3], self.partner)

    def along(self, step):
        there = lax.rem(self.z + step, 4) * 2 + self.core
        return to_seq(
            self.sb, self.rb.at[step - 1], self.zs.at[step - 1], self.zr.at[step - 1], there
        )

    def start(self):
        self.sa[...] = self.local[1 - self.core].astype(bf16)
        self.swap().start()

    def middle(self):
        self.swap().wait_recv()
        self.sb[...] = (self.local[self.core] + self.ra[...].astype(f32)).astype(bf16)
        for step in (1, 2, 3):
            self.along(step).start()

    def late(self):
        total = jnp.zeros(self.sb.shape, f32)
        for step in (1, 2, 3):
            self.along(step).wait_recv()
            counts = one_if(self.z >= step if self.earlier else self.z < step)
            total = total + self.rb[step - 1].astype(f32) * counts
        takes = self.core if self.earlier else 1 - self.core
        self.sc[...] = (total + self.local[self.core] * one_if(takes == 0)).astype(bf16)
        self.give().start()
        self.state[self.core] = total + self.ra[...].astype(f32) * one_if(takes == 1)

    def end(self):
        self.give().wait_recv()
        self.state[1 - self.core] = self.rc[...].astype(f32)

    def drain(self):
        self.swap().wait_send()
        self.give().wait_send()
        for step in (1, 2, 3):
            self.along(step).wait_send()


def layer_kernel(
    inputs, cotangent, w_t, w_out, taps, gains, first, second, rows, moves,
    layer_out, input_grad, *scratch,
):
    take = list(scratch)

    def pop(n):
        got = take[:n]
        del take[:n]
        return got

    fwd_bufs, bwd_bufs = pop(7), pop(7)
    fwd_sems, bwd_sems = pop(9), pop(9)
    early_bufs, late_bufs = pop(6), pop(6)
    early_sems, late_sems = pop(3), pop(3)
    (xin, cot, weights_t, weights_o) = pop(4)
    (pp, cv, mix, gh, dn, phi_q, phi_k, states, grads, scaled, dconv) = pop(11)
    (state_in, state_out, local_in, local_out, halo_in, halo_out) = pop(6)
    (x_sem, c_sem, w_sem, o_sem, r_sem, h_sem) = pop(6)

    tp, place = lax.axis_index("tp"), lax.axis_index("seq")

    def ring(a, r, bufs, sems, out):
        held, weight, part, landed, relay, keep, res = bufs
        return Ring(a, r, held, weight, None, NN, part, landed, relay, keep, res, out, sems)

    fwd = ring("x", "y", fwd_bufs, fwd_sems, layer_out)
    bwd = ring("y", "x", bwd_bufs, bwd_sems, input_grad)
    early = Carry(True, local_in, state_in, early_bufs, early_sems)
    later = Carry(False, local_out, state_out, late_bufs, late_sems)
    heads, d_proj = fwd.held.at[0], bwd.held.at[0]

    def columns(t):
        return pl.ds(pl.multiple_of(t * 256, 256), 256)

    def out_block(t):
        return w_out.at[:, columns(t)]

    def in_block(t):
        return weights_t.at[pl.ds(0, 320), columns(t)]

    pieces = ((32, 128, 0), (192, 128, 128), (0, 32, 256), (160, 32, 288))
    w_loads = [
        pltpu.make_async_copy(
            w_t.at[pl.ds(src, size)], weights_t.at[pl.ds(dst, size)], w_sem.at[n]
        )
        for n, (src, size, dst) in enumerate(pieces)
    ]
    for copy in w_loads:
        copy.start()

    def x_load(c):
        return pltpu.make_async_copy(inputs.at[rows_of(c)], xin.at[rows_of(c)], x_sem.at[c])

    def c_load(c):
        return pltpu.make_async_copy(cotangent.at[rows_of(c)], cot.at[rows_of(c)], c_sem.at[c])

    for c in (3, 0, 1, 2):
        x_load(c).start()
    o_load = pltpu.make_async_copy(w_out, weights_o, o_sem.at[0])
    o_load.start()
    for c in range(NCH):
        c_load(c).start()
    res_loads = [
        pltpu.make_async_copy(inputs.at[:, columns(tp)], fwd.res, r_sem.at[0]),
        pltpu.make_async_copy(cotangent.at[:, columns(tp)], bwd.res, r_sem.at[1]),
    ]
    fwd_own = fwd.own_copies(out_block)
    for copy in res_loads + fwd_own:
        copy.start()

    barrier = pltpu.get_barrier_semaphore()
    for along in ("x", "y"):
        for d in (1, 2, 3):
            pl.semaphore_signal(
                barrier, inc=1, device_id={"tp": neighbour(along, d)}, device_id_type=MESH
            )
    for d in (1, 2, 4, 6, 7):
        pl.semaphore_signal(
            barrier, inc=1, device_id={"seq": lax.rem(place + d, 8)}, device_id_type=MESH
        )
    weights_t[pl.ds(320, 64)] = jnp.zeros((64, weights_t.shape[1]), bf16)
    pl.semaphore_wait(barrier, 11)
    fwd_weights = fwd.weight_copies(out_block)
    for copy in fwd_weights:
        copy.start()
    for copy in w_loads:
        copy.wait()
    bwd_own = bwd.own_copies(in_block)
    bwd_weights = bwd.weight_copies(in_block)
    for copy in bwd_weights + bwd_own:
        copy.start()

    ahead = to_seq(
        pp.at[pl.ds(NCH * CH, 8)], halo_in, h_sem.at[0], h_sem.at[1], lax.rem(place + 1, 8)
    )
    behind = to_seq(
        dconv.at[pl.ds(0, 8)], halo_out, h_sem.at[2], h_sem.at[3], lax.rem(place + 7, 8)
    )

    @pl.loop(0, NCH)
    def _(i):
        c = lax.rem(i + NCH - 1, NCH)
        x_load(c).wait()
        projected = dot(xin[rows_of(c)], weights_t[...], NT).astype(bf16).astype(f32)
        pp[pl.ds(pl.multiple_of(c * CH + 8, 8), CH)] = projected

        @pl.when(i == 0)
        def _():
            ahead.start()

    ahead.wait()
    pp[pl.ds(0, 8)] = halo_in[...] * one_if(place > 0)

    t0, t1, t2 = taps[0:1], taps[1:2], taps[2:3]
    bias_a, bias_b, scale = rows[0:1], rows[1:2], rows[2:3]

    def factors(qk, group):
        return dot(qk, first[group]) + bias_a, dot(qk, second[group]) + bias_b

    def lanes(h):
        return slice(h * DV, (h + 1) * DV)

    def qk_of(c):
        return cv[rows_of(c), 2 * DV : LANES]

    local_in[...] = jnp.zeros(local_in.shape, f32)

    @pl.loop(0, NCH)
    def _(c):
        window = pp[pl.ds(pl.multiple_of(c * CH, CH), CH + 8)]
        mixed = t0 * window[8:] + (
            t1 * pltpu.roll(window, 1, 0)[8:] + t2 * pltpu.roll(window, 2, 0)[8:]
        )
        cv[rows_of(c)] = mixed.astype(bf16)
        qk = qk_of(c)
        for h in range(HEADS):
            a, b = factors(qk, 2 * h + 1)
            features = (a * b).astype(bf16)
            phi_k[h, rows_of(c)] = features
            local = dot(cv[rows_of(c), lanes(h)], features, TN)
            states[c, h] = local
            local_in[h] = local_in[h] + local

    early.start()

    causal = lax.broadcasted_iota(jnp.int32, (CH, CH), 0) >= lax.broadcasted_iota(
        jnp.int32, (CH, CH), 1
    )

    @pl.loop(0, NCH)
    def _(c):
        qk = qk_of(c)
        for h in range(HEADS):
            logits = dot(dot(qk, moves[2 * h]).astype(bf16), qk, NT) * 0.25
            weight = jnp.where(causal, 1.0 + logits + 0.5 * logits * logits, 0.0)
            mix[rows_of(c), lanes(h)] = dot(weight.astype(bf16), cv[rows_of(c), lanes(h)])

        @pl.when(c == 1)
        def _():
            early.middle()

    o_load.wait()
    gain = gains[0:1]

    @pl.loop(0, NCH)
    def _(c):
        c_load(c).wait()
        gh[rows_of(c)] = dot(cot[rows_of(c)], weights_o[...], NT) * gain

    early.late()

    @pl.loop(0, NCH)
    def _(c):
        qk = qk_of(c)
        for h in range(HEADS):
            a, b = factors(qk, 2 * h)
            phi_q[h, rows_of(c)] = (a * b).astype(bf16)

    early.end()
    local_out[...] = jnp.zeros(local_out.shape, f32)

    @pl.loop(0, NCH)
    def _(c):
        for h in range(HEADS):
            entering = state_in[h]
            state_in[h] = entering + states[c, h]
            scaled[c, h] = (entering * scale).astype(bf16)
            numerator = mix[rows_of(c), lanes(h)] + dot(phi_q[h, rows_of(c)], scaled[c, h], NT)
            inverse = 1.0 / jnp.sqrt(jnp.mean(numerator * numerator, -1, keepdims=True) + epsilon)
            normed = numerator * inverse
            heads[rows_of(c), lanes(h)] = (normed * gain[:, lanes(h)]).astype(bf16)
            grad = gh[rows_of(c), lanes(h)]
            d_numer = (grad - normed * jnp.mean(grad * normed, -1, keepdims=True)) * inverse
            rounded = d_numer.astype(bf16)
            dn[rows_of(c), lanes(h)] = rounded
            local = dot(rounded, phi_q[h, rows_of(c)], TN)
            grads[c, h] = local
            local_out[h] = local_out[h] + local
        fwd.send_own(c)

    later.start()

    @pl.loop(0, NCH)
    def _(c):
        qk = qk_of(c)
        d_qk = jnp.zeros((CH, 128), f32)
        for h in range(HEADS):
            moved = dot(qk, moves[2 * h]).astype(bf16)
            logits = dot(moved, qk, NT) * 0.25
            weight = jnp.where(causal, 1.0 + logits + 0.5 * logits * logits, 0.0)
            rounded = dn[rows_of(c), lanes(h)]
            dconv[rows_of(c), lanes(h)] = dot(weight.astype(bf16), rounded, TN)
            d_weight = dot(rounded, cv[rows_of(c), lanes(h)], NT)
            d_logits = jnp.where(causal, d_weight * (1.0 + logits), 0.0) * 0.25
            d_logits = d_logits.astype(bf16)
            d_qk = d_qk + dot(d_logits, dot(qk, moves[2 * h + 1]).astype(bf16))
            d_qk = d_qk + dot(d_logits, moved, TN)
            a, b = factors(qk, 2 * h)
            d_phi = dot(rounded, scaled[c, h])
            d_qk = d_qk + dot((d_phi * b).astype(bf16), first[2 * h], NT)
            d_qk = d_qk + dot((d_phi * a).astype(bf16), second[2 * h], NT)
        dconv[rows_of(c), 2 * DV : LANES] = d_qk

        @pl.when(c == 1)
        def _():
            later.middle()

        @pl.when(c == 3)
        def _():
            later.late()

        fwd.forward(c)

    for copy in fwd_weights + fwd_own + res_loads:
        copy.wait()
    later.end()
    state_out[...] = state_out[...] + local_out[...]

    def project_back(c):
        window = dconv[pl.ds(pl.multiple_of(c * CH, CH), CH + 8)]
        mixed = t0 * window[:CH] + (
            t1 * pltpu.roll(window, CH + 7, 0)[:CH] + t2 * pltpu.roll(window, CH + 6, 0)[:CH]
        )
        d_proj[rows_of(c)] = mixed[:, :320].astype(bf16)
        bwd.send_own(c)

    @pl.loop(0, NCH)
    def _(c):
        qk = qk_of(c)
        d_qk = dconv[rows_of(c), 2 * DV : LANES]
        for h in range(HEADS):
            remaining = state_out[h] - grads[c, h]
            state_out[h] = remaining
            suffix = (remaining * scale).astype(bf16)
            dconv[rows_of(c), lanes(h)] = dconv[rows_of(c), lanes(h)] + dot(
                phi_k[h, rows_of(c)], suffix, NT
            )
            a, b = factors(qk, 2 * h + 1)
            d_phi = dot(cv[rows_of(c), lanes(h)], suffix)
            d_qk = d_qk + dot((d_phi * b).astype(bf16), first[2 * h + 1], NT)
            d_qk = d_qk + dot((d_phi * a).astype(bf16), second[2 * h + 1], NT)
        dconv[rows_of(c), 2 * DV : LANES] = d_qk

        @pl.when(c == 0)
        def _():
            behind.start()

        @pl.when(c > 0)
        def _():
            project_back(c - 1)

        fwd.multiply(c)

    behind.wait()
    dconv[pl.ds(NCH * CH, 8)] = halo_out[...] * one_if(place < 7)
    project_back(NCH - 1)
    for copy in bwd_weights + bwd_own:
        copy.wait()

    @pl.loop(0, NCH + 3)
    def _(i):
        @pl.when(i < NCH)
        def _():
            bwd.forward(i)
            fwd.relayed(i)

        @pl.when((i >= 1) & (i < NCH + 1))
        def _():
            bwd.multiply(i - 1)

        @pl.when((i >= 2) & (i < NCH + 2))
        def _():
            bwd.relayed(i - 2)
            fwd.finish(i - 2)

        @pl.when(i >= 3)
        def _():
            bwd.finish(i - 3)

    @pl.loop(0, NCH)
    def _(c):
        fwd.drain(c)
        bwd.drain(c)

    early.drain()
    later.drain()


def permuted(array):
    parts = [array[..., 32:160], array[..., 192:320], array[..., 0:32], array[..., 160:192]]
    return jnp.concatenate(parts + [jnp.zeros(array.shape[:-1] + (64,), array.dtype)], -1)


def per_device(inputs, cotangent, w_in, conv_w, norm_gain, w_out, keep_flags):
    count, width = inputs.shape
    taps = jnp.pad(permuted(conv_w), ((0, 5), (0, 0)))
    gains = (norm_gain.reshape(HEADS, DV) * keep_flags.astype(f32)[:, None]).reshape(1, HEADS * DV)
    first, second, rows, moves = selectors()
    consts = [jnp.asarray(first, bf16), jnp.asarray(second, bf16), jnp.asarray(rows), jnp.asarray(moves, bf16)]
    whole, near = pl.BlockSpec(memory_space=pl.ANY), pl.BlockSpec(memory_space=pltpu.VMEM)
    result = jax.ShapeDtypeStruct((count, 256), bf16)
    dma = pltpu.SemaphoreType.DMA
    state = (DV, EXP)
    carry_bufs = [pltpu.VMEM((n,) + state if n > 1 else state, bf16) for n in (1, 1, 1, 3, 1, 1)]
    carry_sems = [dma((4,)), dma((3,)), dma((3,))]
    return pl.pallas_call(
        layer_kernel,
        out_shape=(result, result),
        in_specs=[whole] * 4 + [near] * 6,
        out_specs=(near, near),
        scratch_shapes=ring_buffers(count, 256, (256, 256))
        + ring_buffers(count, 320, (320, 256))
        + ring_semaphores()
        + ring_semaphores()
        + carry_bufs
        + carry_bufs
        + carry_sems
        + carry_sems
        + [
            pltpu.VMEM((count, width), bf16),
            pltpu.VMEM((count, width), bf16),
            pltpu.VMEM((LANES, width), bf16),
            pltpu.VMEM((256, width), bf16),
            pltpu.VMEM((count + 8, LANES), f32),
            pltpu.VMEM((count, LANES), bf16),
            pltpu.VMEM((count, 256), f32),
            pltpu.VMEM((count, 256), f32),
            pltpu.VMEM((count, 256), bf16),
            pltpu.VMEM((HEADS, count, EXP), bf16),
            pltpu.VMEM((HEADS, count, EXP), bf16),
            pltpu.VMEM((NCH, HEADS) + state, f32),
            pltpu.VMEM((NCH, HEADS) + state, f32),
            pltpu.VMEM((NCH, HEADS) + state, bf16),
            pltpu.VMEM((count + 8, LANES), f32),
            pltpu.VMEM((HEADS,) + state, f32),
            pltpu.VMEM((HEADS,) + state, f32),
            pltpu.VMEM((HEADS,) + state, f32),
            pltpu.VMEM((HEADS,) + state, f32),
            pltpu.VMEM((8, LANES), f32),
            pltpu.VMEM((8, LANES), f32),
            dma((NCH,)),
            dma((NCH,)),
            dma((4,)),
            dma((1,)),
            dma((2,)),
            dma((4,)),
        ],
        compiler_params=pltpu.CompilerParams(
            collective_id=0, has_side_effects=True, vmem_limit_bytes=62 << 20
        ),
    )(inputs, cotangent, w_in.T, w_out, taps, gains, *consts)


def solution(mesh):
    placed = (
        P("seq", None),
        P("seq", None),
        P(None, "tp"),
        P(None, "tp"),
        P("tp"),
        P("tp", None),
        P("tp"),
    )
    return jax.shard_map(
        per_device,
        mesh=mesh,
        in_specs=placed,
        out_specs=(P("seq", "tp"), P("seq", "tp")),
        check_vma=False,
    )
```

```python
from functools import partial

import jax
import jax.numpy as jnp
import numpy as np
from jax import lax
from jax.experimental import pallas as pl
from jax.experimental.pallas import tpu as pltpu
from jax.sharding import PartitionSpec as P

FEAT = 16
DV = 128
LANES = 384
EXP = 256
HEADS = 2
epsilon = 1e-06

CH = 256
NCH = 4
MESH = pl.DeviceIdType.MESH
NT = (((1,), (1,)), ((), ()))
NN = (((1,), (0,)), ((), ()))
TN = (((0,), (0,)), ((), ()))
f32 = jnp.float32
bf16 = jnp.bfloat16


def neighbour(along, step):
    place = lax.axis_index("tp")
    column, row = lax.rem(place, 4), lax.div(place, 4)
    if along == "x":
        return row * 4 + lax.rem(column + step, 4)
    return lax.rem(row + step, 4) * 4 + column


def block_at(a_along, a_step, r_along, r_step):
    place = lax.axis_index("tp")
    column, row = lax.rem(place, 4), lax.div(place, 4)
    x_step = a_step if a_along == "x" else r_step
    y_step = a_step if a_along == "y" else r_step
    return lax.rem(row + y_step, 4) * 4 + lax.rem(column + x_step, 4)


def to_device(src, dst, send_sem, recv_sem, place):
    return pltpu.make_async_remote_copy(
        src_ref=src,
        dst_ref=dst,
        send_sem=send_sem,
        recv_sem=recv_sem,
        device_id={"tp": place},
        device_id_type=MESH,
    )


def to_seq(src, dst, send_sem, recv_sem, place):
    return pltpu.make_async_remote_copy(
        src_ref=src,
        dst_ref=dst,
        send_sem=send_sem,
        recv_sem=recv_sem,
        device_id={"seq": place},
        device_id_type=MESH,
    )


def rows_of(c):
    return pl.ds(pl.multiple_of(c * CH, CH), CH)


def way(c):
    return jnp.where(c < NCH // 2, 1, 3)


class Ring:
    def __init__(self, a, r, held, weight, own, dims, part, landed, relay, keep, res, out, sems):
        self.a, self.r = a, r
        self.held, self.weight, self.own, self.dims = held, weight, own, dims
        self.part, self.landed, self.relay = part, landed, relay
        self.keep, self.res, self.out = keep, res, out
        (self.gs, self.gr, self.ts, self.tr, self.ps, self.pr) = sems[:6]
        (self.ws, self.wr, self.us, self.ur, self.wo, self.os) = sems[6:]

    def weight_copies(self, w_block):
        core = lax.rem(lax.axis_index("seq"), 2)
        copies = []
        for d in range(1, 4):
            for j in range(2):
                k = core * 2 + j
                copies.append(
                    to_device(
                        w_block(block_at(self.a, d, self.r, k)),
                        self.weight.at[k, d],
                        self.ws.at[d - 1, j],
                        self.wr.at[d - 1, j],
                        neighbour(self.a, d),
                    )
                )
        return copies

    def swap_copies(self):
        place = lax.axis_index("seq")
        core = lax.rem(place, 2)
        copies = []
        for d in range(1, 4):
            for j in range(2):
                block = self.weight.at[core * 2 + j, d]
                copies.append(
                    to_seq(
                        block,
                        block,
                        self.us.at[d - 1, j],
                        self.ur.at[d - 1, j],
                        place + 1 - 2 * core,
                    )
                )
        return copies

    def own_copies(self, w_block):
        return [
            pltpu.make_async_copy(
                w_block(block_at(self.a, 0, self.r, k)), self.weight.at[k, 0], self.wo.at[k]
            )
            for k in range(4)
        ]

    def direct(self, c, d):
        return to_device(
            self.held.at[0, rows_of(c)],
            self.held.at[d, rows_of(c)],
            self.gs.at[d - 1, c],
            self.gr.at[d - 1, c],
            neighbour(self.a, d),
        )

    def passed_on(self, c):
        return to_device(
            self.held.at[way(c), rows_of(c)],
            self.held.at[2, rows_of(c)],
            self.gs.at[1, c],
            self.gr.at[1, c],
            neighbour(self.a, way(c)),
        )

    def send_own(self, c):
        self.direct(c, 1).start()
        self.direct(c, 3).start()

    def forward(self, c):
        self.direct(c, 1).wait_recv()
        self.direct(c, 3).wait_recv()
        self.passed_on(c).start()

    def tie(self, c):
        return to_device(
            self.part.at[2, rows_of(c)],
            self.relay.at[rows_of(c)],
            self.ts.at[c],
            self.tr.at[c],
            neighbour(self.r, way(c)),
        )

    def side(self, c, d):
        return to_device(
            self.part.at[d, rows_of(c)],
            self.landed.at[d // 2, rows_of(c)],
            self.ps.at[d // 2, c],
            self.pr.at[d // 2, c],
            neighbour(self.r, d),
        )

    def product(self, c, k):
        total = None
        for o in range(4):
            term = lax.dot_general(
                self.held[o, rows_of(c)], self.weight[k, o], self.dims, preferred_element_type=f32
            )
            total = term if total is None else total + term
        return total

    def multiply(self, c):
        self.passed_on(c).wait_recv()
        near, far = way(c), 4 - way(c)
        self.part[2, rows_of(c)] = self.product(c, 2).astype(bf16)
        self.tie(c).start()
        self.part[far, rows_of(c)] = self.product(c, far).astype(bf16)
        self.side(c, far).start()
        self.keep[1, rows_of(c)] = self.product(c, near)
        self.keep[0, rows_of(c)] = self.product(c, 0) + self.res[rows_of(c)].astype(f32)

    def relayed(self, c):
        self.tie(c).wait_recv()
        near = way(c)
        total = self.keep[1, rows_of(c)] + self.relay[rows_of(c)].astype(f32)
        self.part[near, rows_of(c)] = total.astype(bf16)
        self.side(c, near).start()

    def finish(self, c):
        self.side(c, 1).wait_recv()
        self.side(c, 3).wait_recv()
        total = self.keep[0, rows_of(c)] + (
            self.landed[0, rows_of(c)].astype(f32) + self.landed[1, rows_of(c)].astype(f32)
        )
        self.part[0, rows_of(c)] = total.astype(bf16)
        self.leave(c).start()

    def leave(self, c):
        return pltpu.make_async_copy(
            self.part.at[0, rows_of(c)], self.out.at[rows_of(c)], self.os.at[c]
        )

    def drain(self, c):
        self.direct(c, 1).wait_send()
        self.direct(c, 3).wait_send()
        self.passed_on(c).wait_send()
        self.tie(c).wait_send()
        self.side(c, 1).wait_send()
        self.side(c, 3).wait_send()
        self.leave(c).wait()


def ring_semaphores():
    dma = pltpu.SemaphoreType.DMA
    return [
        dma((3, NCH)),
        dma((3, NCH)),
        dma((NCH,)),
        dma((NCH,)),
        dma((2, NCH)),
        dma((2, NCH)),
        dma((3, 2)),
        dma((3, 2)),
        dma((3, 2)),
        dma((3, 2)),
        dma((4,)),
        dma((NCH,)),
    ]


def ring_buffers(rows, width, weight_shape):
    return [
        pltpu.VMEM((4, rows, width), bf16),
        pltpu.VMEM((4, 4) + weight_shape, bf16),
        pltpu.VMEM((4, rows, 256), bf16),
        pltpu.VMEM((2, rows, 256), bf16),
        pltpu.VMEM((rows, 256), bf16),
        pltpu.VMEM((2, rows, 256), f32),
        pltpu.VMEM((rows, 256), bf16),
    ]


def selectors():
    first = np.zeros((4, 128, EXP), np.float32)
    second = np.zeros((4, 128, EXP), np.float32)
    rows = np.zeros((8, EXP), np.float32)
    rows[0, 0] = rows[1, 0] = rows[2, 0] = 1.0
    for group in range(4):
        base = group * FEAT
        for i in range(FEAT):
            first[group, base + i, 1 + i] = 1.0
            rows[1, 1 + i] = 1.0
            rows[2, 1 + i] = 0.25
        e = 1 + FEAT
        for i in range(FEAT):
            for j in range(i, FEAT):
                first[group, base + i, e] = 1.0
                second[group, base + j, e] = 1.0
                rows[2, e] = 1 / 32 if i == j else 1 / 16
                e += 1
    moves = np.zeros((4, 128, 128), np.float32)
    for h in range(HEADS):
        for i in range(FEAT):
            q, k = 2 * h * FEAT + i, (2 * h + 1) * FEAT + i
            moves[2 * h, q, k] = 1.0
            moves[2 * h + 1, k, q] = 1.0
    return first, second, rows, moves


def dot(a, b, dims=NN):
    return lax.dot_general(a, b, dims, preferred_element_type=f32)


def one_if(condition):
    return jnp.where(condition, 1.0, 0.0).astype(f32)


class Carry:
    def __init__(self, earlier, local, state, bufs, sems):
        self.earlier, self.local, self.state = earlier, local, state
        self.sa, self.ra, self.sb, self.rb, self.sc, self.rc = bufs
        self.pair_sems, self.zs, self.zr = sems
        place = lax.axis_index("seq")
        self.core, self.z = lax.rem(place, 2), lax.div(place, 2)
        self.partner = self.z * 2 + (1 - self.core)

    def swap(self):
        return to_seq(self.sa, self.ra, self.pair_sems.at[0], self.pair_sems.at[1], self.partner)

    def give(self):
        return to_seq(self.sc, self.rc, self.pair_sems.at[2], self.pair_sems.at[3], self.partner)

    def along(self, step):
        there = lax.rem(self.z + step, 4) * 2 + self.core
        return to_seq(
            self.sb, self.rb.at[step - 1], self.zs.at[step - 1], self.zr.at[step - 1], there
        )

    def start(self):
        self.sa[...] = self.local[1 - self.core].astype(bf16)
        self.swap().start()

    def middle(self):
        self.swap().wait_recv()
        self.sb[...] = (self.local[self.core] + self.ra[...].astype(f32)).astype(bf16)
        for step in (1, 2, 3):
            self.along(step).start()

    def late(self):
        total = jnp.zeros(self.sb.shape, f32)
        for step in (1, 2, 3):
            self.along(step).wait_recv()
            counts = one_if(self.z >= step if self.earlier else self.z < step)
            total = total + self.rb[step - 1].astype(f32) * counts
        takes = self.core if self.earlier else 1 - self.core
        self.sc[...] = (total + self.local[self.core] * one_if(takes == 0)).astype(bf16)
        self.give().start()
        self.state[self.core] = total + self.ra[...].astype(f32) * one_if(takes == 1)

    def end(self):
        self.give().wait_recv()
        self.state[1 - self.core] = self.rc[...].astype(f32)

    def drain(self):
        self.swap().wait_send()
        self.give().wait_send()
        for step in (1, 2, 3):
            self.along(step).wait_send()


def layer_kernel(
    inputs, cotangent, w_t, w_out, first_any, second_any, moves_any, conv, gains, rows, keep,
    layer_out, input_grad, *scratch,
):
    take = list(scratch)

    def pop(n):
        got = take[:n]
        del take[:n]
        return got

    fwd_bufs, bwd_bufs = pop(7), pop(7)
    fwd_sems, bwd_sems = pop(12), pop(12)
    early_bufs, late_bufs = pop(6), pop(6)
    early_sems, late_sems = pop(3), pop(3)
    (xin, cot, weights_t, weights_o) = pop(4)
    (pp, cv, mix, gh, dn, phi_q, phi_k, states, grads, scaled, dconv) = pop(11)
    (state_in, state_out, local_in, local_out, halo_in, halo_out) = pop(6)
    (first, second, moves) = pop(3)
    (x_sem, c_sem, w_sem, o_sem, r_sem, h_sem, k_sem) = pop(7)

    tp, place = lax.axis_index("tp"), lax.axis_index("seq")

    def ring(a, r, bufs, sems, out):
        held, weight, part, landed, relay, keep, res = bufs
        return Ring(a, r, held, weight, None, NN, part, landed, relay, keep, res, out, sems)

    fwd = ring("x", "y", fwd_bufs, fwd_sems, layer_out)
    bwd = ring("x", "y", bwd_bufs, bwd_sems, input_grad)
    early = Carry(True, local_in, state_in, early_bufs, early_sems)
    later = Carry(False, local_out, state_out, late_bufs, late_sems)
    heads, d_proj = fwd.held.at[0], bwd.held.at[0]

    def columns(t):
        return pl.ds(pl.multiple_of(t * 256, 256), 256)

    def out_block(t):
        return w_out.at[:, columns(t)]

    def in_block(t):
        return weights_t.at[pl.ds(0, 320), columns(t)]

    pieces = ((32, 128, 0), (192, 128, 128), (0, 32, 256), (160, 32, 288))
    w_loads = [
        pltpu.make_async_copy(
            w_t.at[pl.ds(src, size)], weights_t.at[pl.ds(dst, size)], w_sem.at[n]
        )
        for n, (src, size, dst) in enumerate(pieces)
    ]
    for copy in w_loads:
        copy.start()

    def x_load(c):
        return pltpu.make_async_copy(inputs.at[rows_of(c)], xin.at[rows_of(c)], x_sem.at[c])

    def c_load(c):
        return pltpu.make_async_copy(cotangent.at[rows_of(c)], cot.at[rows_of(c)], c_sem.at[c])

    x_load(3).start()
    barrier = pltpu.get_barrier_semaphore()
    for d in (1, 2, 3):
        for along in ("x", "y"):
            pl.semaphore_signal(
                barrier, inc=1, device_id={"tp": neighbour(along, d)}, device_id_type=MESH
            )
    for d in (1, 2, 4, 6, 7):
        pl.semaphore_signal(
            barrier, inc=1, device_id={"seq": lax.rem(place + d, 8)}, device_id_type=MESH
        )
    weights_t[pl.ds(320, 64)] = jnp.zeros((64, weights_t.shape[1]), bf16)
    const_loads = [
        pltpu.make_async_copy(src, dst, k_sem.at[n])
        for n, (src, dst) in enumerate(
            ((first_any, first), (second_any, second), (moves_any, moves))
        )
    ]
    o_load = pltpu.make_async_copy(w_out, weights_o, o_sem.at[0])
    res_loads = [
        pltpu.make_async_copy(inputs.at[:, columns(tp)], fwd.res, r_sem.at[0]),
        pltpu.make_async_copy(cotangent.at[:, columns(tp)], bwd.res, r_sem.at[1]),
    ]
    fwd_own, bwd_own = fwd.own_copies(out_block), bwd.own_copies(in_block)
    fwd_weights, bwd_weights = fwd.weight_copies(out_block), bwd.weight_copies(in_block)
    fwd_swaps, bwd_swaps = fwd.swap_copies(), bwd.swap_copies()

    src = lax.broadcasted_iota(jnp.int32, (320, LANES), 0)
    dst = lax.broadcasted_iota(jnp.int32, (320, LANES), 1)
    from_high = jnp.where(dst < 288, dst - 256, jnp.where(dst < 320, dst - 128, -1))
    source = jnp.where(dst < 128, dst + 32, jnp.where(dst < 256, dst + 64, from_high))
    taps = lax.dot_general(
        conv[...],
        jnp.where(src == source, 1.0, 0.0).astype(f32),
        NN,
        precision=lax.Precision.HIGHEST,
        preferred_element_type=f32,
    )
    lane = lax.broadcasted_iota(jnp.int32, (1, HEADS * DV), 1)
    gain = gains[...] * jnp.where(lane < DV, keep[0].astype(f32), keep[1].astype(f32))

    for copy in w_loads:
        copy.wait()
    for c in (0, 1, 2):
        x_load(c).start()
    for copy in const_loads + [o_load] + res_loads + fwd_own + bwd_own:
        copy.start()

    ahead = to_seq(
        pp.at[pl.ds(NCH * CH, 8)], halo_in, h_sem.at[0], h_sem.at[1], lax.rem(place + 1, 8)
    )
    behind = to_seq(
        dconv.at[pl.ds(0, 8)], halo_out, h_sem.at[2], h_sem.at[3], lax.rem(place + 7, 8)
    )

    @pl.loop(0, NCH)
    def _(i):
        c = lax.rem(i + NCH - 1, NCH)
        x_load(c).wait()
        c_load(c).start()
        projected = dot(xin[rows_of(c)], weights_t[...], NT).astype(bf16).astype(f32)
        pp[pl.ds(pl.multiple_of(c * CH + 8, 8), CH)] = projected

        @pl.when(i == 0)
        def _():
            pl.semaphore_wait(barrier, 11)
            ahead.start()
            for copy in fwd_weights + bwd_weights:
                copy.start()

    for copy in const_loads:
        copy.wait()
    ahead.wait()
    pp[pl.ds(0, 8)] = halo_in[...] * one_if(place > 0)

    t0, t1, t2 = taps[0:1], taps[1:2], taps[2:3]
    bias_a, bias_b, scale = rows[0:1], rows[1:2], rows[2:3]

    def factors(qk, group):
        return dot(qk, first[group]) + bias_a, dot(qk, second[group]) + bias_b

    def lanes(h):
        return slice(h * DV, (h + 1) * DV)

    def qk_of(c):
        return cv[rows_of(c), 2 * DV : LANES]

    local_in[...] = jnp.zeros(local_in.shape, f32)

    @pl.loop(0, NCH)
    def _(c):
        window = pp[pl.ds(pl.multiple_of(c * CH, CH), CH + 8)]
        mixed = t0 * window[8:] + (
            t1 * pltpu.roll(window, 1, 0)[8:] + t2 * pltpu.roll(window, 2, 0)[8:]
        )
        cv[rows_of(c)] = mixed.astype(bf16)
        qk = qk_of(c)
        for h in range(HEADS):
            a, b = factors(qk, 2 * h + 1)
            features = (a * b).astype(bf16)
            phi_k[h, rows_of(c)] = features
            local = dot(cv[rows_of(c), lanes(h)], features, TN)
            states[c, h] = local
            local_in[h] = local_in[h] + local

    early.start()

    causal = lax.broadcasted_iota(jnp.int32, (CH, CH), 0) >= lax.broadcasted_iota(
        jnp.int32, (CH, CH), 1
    )

    @pl.loop(0, NCH)
    def _(c):
        qk = qk_of(c)
        for h in range(HEADS):
            logits = dot(dot(qk, moves[2 * h]).astype(bf16), qk, NT) * 0.25
            weight = jnp.where(causal, 1.0 + logits + 0.5 * logits * logits, 0.0)
            mix[rows_of(c), lanes(h)] = dot(weight.astype(bf16), cv[rows_of(c), lanes(h)])

        @pl.when(c == 1)
        def _():
            early.middle()

    o_load.wait()

    @pl.loop(0, NCH)
    def _(c):
        c_load(c).wait()
        gh[rows_of(c)] = dot(cot[rows_of(c)], weights_o[...], NT) * gain

    @pl.loop(0, NCH)
    def _(c):
        qk = qk_of(c)
        for h in range(HEADS):
            a, b = factors(qk, 2 * h)
            phi_q[h, rows_of(c)] = (a * b).astype(bf16)

    early.late()
    early.end()
    local_out[...] = jnp.zeros(local_out.shape, f32)

    @pl.loop(0, NCH)
    def _(c):
        for h in range(HEADS):
            entering = state_in[h]
            state_in[h] = entering + states[c, h]
            scaled[c, h] = (entering * scale).astype(bf16)
            numerator = mix[rows_of(c), lanes(h)] + dot(phi_q[h, rows_of(c)], scaled[c, h], NT)
            inverse = 1.0 / jnp.sqrt(jnp.mean(numerator * numerator, -1, keepdims=True) + epsilon)
            normed = numerator * inverse
            heads[rows_of(c), lanes(h)] = (normed * gain[:, lanes(h)]).astype(bf16)
            grad = gh[rows_of(c), lanes(h)]
            d_numer = (grad - normed * jnp.mean(grad * normed, -1, keepdims=True)) * inverse
            rounded = d_numer.astype(bf16)
            dn[rows_of(c), lanes(h)] = rounded
            local = dot(rounded, phi_q[h, rows_of(c)], TN)
            grads[c, h] = local
            local_out[h] = local_out[h] + local
        fwd.send_own(c)

    later.start()
    for copy in fwd_weights:
        copy.wait()
    for copy in fwd_swaps:
        copy.start()

    @pl.loop(0, NCH)
    def _(c):
        qk = qk_of(c)
        d_qk = jnp.zeros((CH, 128), f32)
        for h in range(HEADS):
            moved = dot(qk, moves[2 * h]).astype(bf16)
            logits = dot(moved, qk, NT) * 0.25
            weight = jnp.where(causal, 1.0 + logits + 0.5 * logits * logits, 0.0)
            rounded = dn[rows_of(c), lanes(h)]
            dconv[rows_of(c), lanes(h)] = dot(weight.astype(bf16), rounded, TN)
            d_weight = dot(rounded, cv[rows_of(c), lanes(h)], NT)
            d_logits = jnp.where(causal, d_weight * (1.0 + logits), 0.0) * 0.25
            d_logits = d_logits.astype(bf16)
            d_qk = d_qk + dot(d_logits, dot(qk, moves[2 * h + 1]).astype(bf16))
            d_qk = d_qk + dot(d_logits, moved, TN)
            a, b = factors(qk, 2 * h)
            d_phi = dot(rounded, scaled[c, h])
            d_qk = d_qk + dot((d_phi * b).astype(bf16), first[2 * h], NT)
            d_qk = d_qk + dot((d_phi * a).astype(bf16), second[2 * h], NT)
        dconv[rows_of(c), 2 * DV : LANES] = d_qk

        @pl.when(c == 1)
        def _():
            later.middle()

        @pl.when(c == 3)
        def _():
            later.late()

        fwd.forward(c)

    later.end()
    state_out[...] = state_out[...] + local_out[...]

    def project_back(c):
        window = dconv[pl.ds(pl.multiple_of(c * CH, CH), CH + 8)]
        mixed = t0 * window[:CH] + (
            t1 * pltpu.roll(window, CH + 7, 0)[:CH] + t2 * pltpu.roll(window, CH + 6, 0)[:CH]
        )
        d_proj[rows_of(c)] = mixed[:, :320].astype(bf16)
        bwd.send_own(c)

    @pl.loop(0, NCH)
    def _(c):
        qk = qk_of(c)
        d_qk = dconv[rows_of(c), 2 * DV : LANES]
        for h in range(HEADS):
            remaining = state_out[h] - grads[c, h]
            state_out[h] = remaining
            suffix = (remaining * scale).astype(bf16)
            dconv[rows_of(c), lanes(h)] = dconv[rows_of(c), lanes(h)] + dot(
                phi_k[h, rows_of(c)], suffix, NT
            )
            a, b = factors(qk, 2 * h + 1)
            d_phi = dot(cv[rows_of(c), lanes(h)], suffix)
            d_qk = d_qk + dot((d_phi * b).astype(bf16), first[2 * h + 1], NT)
            d_qk = d_qk + dot((d_phi * a).astype(bf16), second[2 * h + 1], NT)
        dconv[rows_of(c), 2 * DV : LANES] = d_qk

        @pl.when(c == 0)
        def _():
            behind.start()

        @pl.when(c > 0)
        def _():
            project_back(c - 1)

    behind.wait()
    dconv[pl.ds(NCH * CH, 8)] = halo_out[...] * one_if(place < 7)
    project_back(NCH - 1)
    for copy in bwd_weights:
        copy.wait()
    for copy in bwd_swaps:
        copy.start()
    for copy in fwd_swaps + fwd_own + bwd_own + res_loads:
        copy.wait()

    @pl.loop(0, NCH)
    def _(i):
        fwd.multiply(i)
        bwd.forward(i)

        @pl.when(i >= 1)
        def _():
            fwd.relayed(i - 1)

    for copy in bwd_swaps:
        copy.wait()

    @pl.loop(0, NCH + 2)
    def _(i):
        @pl.when(i < NCH)
        def _():
            bwd.multiply(i)

        @pl.when(i == 0)
        def _():
            fwd.relayed(NCH - 1)

        @pl.when((i >= 1) & (i < NCH + 1))
        def _():
            bwd.relayed(i - 1)
            fwd.finish(i - 1)

        @pl.when(i >= 2)
        def _():
            bwd.finish(i - 2)

    @pl.loop(0, NCH)
    def _(c):
        fwd.drain(c)
        bwd.drain(c)

    early.drain()
    later.drain()


def settle_kernel(first, second, first_out, second_out, held, in_sem, out_sem):
    pairs = ((first, first_out), (second, second_out))
    ins = [pltpu.make_async_copy(p[0], held.at[n], in_sem.at[n]) for n, p in enumerate(pairs)]
    outs = [pltpu.make_async_copy(held.at[n], p[1], out_sem.at[n]) for n, p in enumerate(pairs)]
    for copy in ins:
        copy.start()
    for n in range(2):
        ins[n].wait()
        outs[n].start()
    for copy in outs:
        copy.wait()


def settle(first, second):
    whole = pl.BlockSpec(memory_space=pl.ANY)
    result = jax.ShapeDtypeStruct(first.shape, first.dtype)
    dma = pltpu.SemaphoreType.DMA
    return pl.pallas_call(
        settle_kernel,
        out_shape=(result, result),
        in_specs=[whole] * 2,
        out_specs=(whole, whole),
        scratch_shapes=[pltpu.VMEM((2,) + first.shape, first.dtype), dma((2,)), dma((2,))],
    )(first, second)


def per_device(inputs, cotangent, w_in, conv_w, norm_gain, w_out, keep_flags):
    count, width = inputs.shape
    first, second, rows, moves = selectors()
    consts = [jnp.asarray(part, bf16) for part in (first, second, moves)]
    whole, near = pl.BlockSpec(memory_space=pl.ANY), pl.BlockSpec(memory_space=pltpu.VMEM)
    result = jax.ShapeDtypeStruct((count, 256), bf16)
    dma = pltpu.SemaphoreType.DMA
    state = (DV, EXP)
    carry_bufs = [pltpu.VMEM((n,) + state if n > 1 else state, bf16) for n in (1, 1, 1, 3, 1, 1)]
    carry_sems = [dma((4,)), dma((3,)), dma((3,))]
    results = pl.pallas_call(
        layer_kernel,
        out_shape=(result, result),
        in_specs=[whole] * 7 + [near] * 3 + [pl.BlockSpec(memory_space=pltpu.SMEM)],
        out_specs=(whole, whole),
        scratch_shapes=ring_buffers(count, 256, (256, 256))
        + ring_buffers(count, 320, (320, 256))
        + ring_semaphores()
        + ring_semaphores()
        + carry_bufs
        + carry_bufs
        + carry_sems
        + carry_sems
        + [
            pltpu.VMEM((count, width), bf16),
            pltpu.VMEM((count, width), bf16),
            pltpu.VMEM((LANES, width), bf16),
            pltpu.VMEM((256, width), bf16),
            pltpu.VMEM((count + 8, LANES), f32),
            pltpu.VMEM((count, LANES), bf16),
            pltpu.VMEM((count, 256), f32),
            pltpu.VMEM((count, 256), f32),
            pltpu.VMEM((count, 256), bf16),
            pltpu.VMEM((HEADS, count, EXP), bf16),
            pltpu.VMEM((HEADS, count, EXP), bf16),
            pltpu.VMEM((NCH, HEADS) + state, f32),
            pltpu.VMEM((NCH, HEADS) + state, f32),
            pltpu.VMEM((NCH, HEADS) + state, bf16),
            pltpu.VMEM((count + 8, LANES), f32),
            pltpu.VMEM((HEADS,) + state, f32),
            pltpu.VMEM((HEADS,) + state, f32),
            pltpu.VMEM((HEADS,) + state, f32),
            pltpu.VMEM((HEADS,) + state, f32),
            pltpu.VMEM((8, LANES), f32),
            pltpu.VMEM((8, LANES), f32),
            pltpu.VMEM((4, 128, EXP), bf16),
            pltpu.VMEM((4, 128, EXP), bf16),
            pltpu.VMEM((4, 128, 128), bf16),
            dma((NCH,)),
            dma((NCH,)),
            dma((4,)),
            dma((1,)),
            dma((2,)),
            dma((4,)),
            dma((3,)),
        ],
        compiler_params=pltpu.CompilerParams(
            collective_id=0, has_side_effects=True, vmem_limit_bytes=62 << 20
        ),
    )(
        inputs,
        cotangent,
        w_in.T,
        w_out,
        *consts,
        conv_w,
        norm_gain.reshape(1, HEADS * DV),
        jnp.asarray(rows),
        keep_flags,
    )
    return settle(*results)


def solution(mesh):
    placed = (
        P("seq", None),
        P("seq", None),
        P(None, "tp"),
        P(None, "tp"),
        P("tp"),
        P("tp", None),
        P("tp"),
    )
    return jax.shard_map(
        per_device,
        mesh=mesh,
        in_specs=placed,
        out_specs=(P("seq", "tp"), P("seq", "tp")),
        check_vma=False,
    )
```

```python
from functools import partial

import jax
import jax.numpy as jnp
import numpy as np
from jax import lax
from jax.experimental import pallas as pl
from jax.experimental.pallas import tpu as pltpu
from jax.sharding import PartitionSpec as P

FEAT = 16
DV = 128
LANES = 384
EXP = 256
HEADS = 2
epsilon = 1e-06

CH = 256
NCH = 4
MESH = pl.DeviceIdType.MESH
NT = (((1,), (1,)), ((), ()))
NN = (((1,), (0,)), ((), ()))
TN = (((0,), (0,)), ((), ()))
f32 = jnp.float32
bf16 = jnp.bfloat16


def neighbour(along, step):
    place = lax.axis_index("tp")
    column, row = lax.rem(place, 4), lax.div(place, 4)
    if along == "x":
        return row * 4 + lax.rem(column + step, 4)
    return lax.rem(row + step, 4) * 4 + column


def block_at(a_along, a_step, r_along, r_step):
    place = lax.axis_index("tp")
    column, row = lax.rem(place, 4), lax.div(place, 4)
    x_step = a_step if a_along == "x" else r_step
    y_step = a_step if a_along == "y" else r_step
    return lax.rem(row + y_step, 4) * 4 + lax.rem(column + x_step, 4)


def to_device(src, dst, send_sem, recv_sem, place):
    return pltpu.make_async_remote_copy(
        src_ref=src,
        dst_ref=dst,
        send_sem=send_sem,
        recv_sem=recv_sem,
        device_id={"tp": place},
        device_id_type=MESH,
    )


def to_seq(src, dst, send_sem, recv_sem, place):
    return pltpu.make_async_remote_copy(
        src_ref=src,
        dst_ref=dst,
        send_sem=send_sem,
        recv_sem=recv_sem,
        device_id={"seq": place},
        device_id_type=MESH,
    )


def dot(a, b, dims=NN):
    return lax.dot_general(a, b, dims, preferred_element_type=f32)


def rows_of(c, size=CH):
    return pl.ds(pl.multiple_of(c * size, size), size)


def way(c):
    return jnp.where(c < NCH // 2, 1, 3)


class Ring:
    def __init__(self, a, r, streams, weight, part, landed, relay, keep, res, out, sems):
        self.a, self.r, self.streams, self.weight = a, r, streams, weight
        self.part, self.landed, self.relay = part, landed, relay
        self.keep, self.res, self.out = keep, res, out
        (self.ts, self.tr, self.ps, self.pr, self.os) = sems

    def direct(self, c, d):
        return [
            to_device(
                held.at[0, rows_of(c, size)],
                held.at[d, rows_of(c, size)],
                send.at[d - 1, c],
                recv.at[d - 1, c],
                neighbour(self.a, d),
            )
            for held, size, send, recv in self.streams
        ]

    def passed_on(self, c):
        return [
            to_device(
                held.at[way(c), rows_of(c, size)],
                held.at[2, rows_of(c, size)],
                send.at[1, c],
                recv.at[1, c],
                neighbour(self.a, way(c)),
            )
            for held, size, send, recv in self.streams
        ]

    def send_own(self, c):
        for d in (1, 3):
            for copy in self.direct(c, d):
                copy.start()

    def forward(self, c):
        for d in (1, 3):
            for copy in self.direct(c, d):
                copy.wait_recv()
        for copy in self.passed_on(c):
            copy.start()

    def tie(self, c):
        return to_device(
            self.part.at[2, rows_of(c)],
            self.relay.at[rows_of(c)],
            self.ts.at[c],
            self.tr.at[c],
            neighbour(self.r, way(c)),
        )

    def side(self, c, d):
        return to_device(
            self.part.at[d, rows_of(c)],
            self.landed.at[d // 2, rows_of(c)],
            self.ps.at[d // 2, c],
            self.pr.at[d // 2, c],
            neighbour(self.r, d),
        )

    def prepare(self, c):
        pass

    def product(self, c, k):
        held = self.streams[0][0]
        total = None
        for o in range(4):
            term = dot(held[o, rows_of(c)], self.weight[k, o])
            total = term if total is None else total + term
        return total

    def multiply(self, c):
        for copy in self.passed_on(c):
            copy.wait_recv()
        self.prepare(c)
        near, far = way(c), 4 - way(c)
        self.part[2, rows_of(c)] = self.product(c, 2).astype(bf16)
        self.tie(c).start()
        self.part[far, rows_of(c)] = self.product(c, far).astype(bf16)
        self.side(c, far).start()
        self.keep[1, rows_of(c)] = self.product(c, near)
        self.keep[0, rows_of(c)] = self.product(c, 0) + self.res[rows_of(c)].astype(f32)

    def relayed(self, c):
        self.tie(c).wait_recv()
        near = way(c)
        total = self.keep[1, rows_of(c)] + self.relay[rows_of(c)].astype(f32)
        self.part[near, rows_of(c)] = total.astype(bf16)
        self.side(c, near).start()

    def finish(self, c):
        self.side(c, 1).wait_recv()
        self.side(c, 3).wait_recv()
        total = self.keep[0, rows_of(c)] + (
            self.landed[0, rows_of(c)].astype(f32) + self.landed[1, rows_of(c)].astype(f32)
        )
        self.part[0, rows_of(c)] = total.astype(bf16)
        self.leave(c).start()

    def leave(self, c):
        return pltpu.make_async_copy(
            self.part.at[0, rows_of(c)], self.out.at[rows_of(c)], self.os.at[c]
        )

    def drain(self, c):
        for copy in self.direct(c, 1) + self.direct(c, 3) + self.passed_on(c):
            copy.wait_send()
        self.tie(c).wait_send()
        self.side(c, 1).wait_send()
        self.side(c, 3).wait_send()
        self.leave(c).wait()


class SplitRing(Ring):
    def prepare(self, c):
        packed = self.streams[1][0]
        low = lax.broadcasted_iota(jnp.int32, (CH // 2, 128), 1) < 64
        for pair in range(2):
            one = packed[2 * pair, rows_of(c, CH // 2)].astype(f32)
            two = packed[2 * pair + 1, rows_of(c, CH // 2)].astype(f32)
            top = jnp.where(low, one, pltpu.roll(two, 64, 1))
            bottom = jnp.where(low, pltpu.roll(one, 64, 1), two)
            lanes = slice(pair * 128, pair * 128 + 128)
            self.flat[0 : CH // 2, lanes] = top.astype(bf16)
            self.flat[CH // 2 : CH, lanes] = bottom.astype(bf16)

    def product(self, c, k):
        return super().product(c, k) + dot(self.flat[...], self.weight_qk[k].reshape(256, 256))


def ring_semaphores():
    dma = pltpu.SemaphoreType.DMA
    return [dma((NCH,)), dma((NCH,)), dma((2, NCH)), dma((2, NCH)), dma((NCH,))]


def ring_buffers(rows):
    return [
        pltpu.VMEM((4, 4, 256, 256), bf16),
        pltpu.VMEM((4, rows, 256), bf16),
        pltpu.VMEM((2, rows, 256), bf16),
        pltpu.VMEM((rows, 256), bf16),
        pltpu.VMEM((2, rows, 256), f32),
        pltpu.VMEM((rows, 256), bf16),
    ]


def selectors():
    first = np.zeros((4, 128, EXP), np.float32)
    second = np.zeros((4, 128, EXP), np.float32)
    rows = np.zeros((8, EXP), np.float32)
    rows[0, 0] = rows[1, 0] = rows[2, 0] = 1.0
    for group in range(4):
        base = group * FEAT
        for i in range(FEAT):
            first[group, base + i, 1 + i] = 1.0
            rows[1, 1 + i] = 1.0
            rows[2, 1 + i] = 0.25
        e = 1 + FEAT
        for i in range(FEAT):
            for j in range(i, FEAT):
                first[group, base + i, e] = 1.0
                second[group, base + j, e] = 1.0
                rows[2, e] = 1 / 32 if i == j else 1 / 16
                e += 1
    moves = np.zeros((4, 128, 128), np.float32)
    for h in range(HEADS):
        for i in range(FEAT):
            q, k = 2 * h * FEAT + i, (2 * h + 1) * FEAT + i
            moves[2 * h, q, k] = 1.0
            moves[2 * h + 1, k, q] = 1.0
    return first, second, rows, moves


def one_if(condition):
    return jnp.where(condition, 1.0, 0.0).astype(f32)


class Carry:
    def __init__(self, earlier, local, state, bufs, sems):
        self.earlier, self.local, self.state = earlier, local, state
        self.sa, self.ra, self.sb, self.rb, self.sc, self.rc = bufs
        self.pair_sems, self.zs, self.zr = sems
        place = lax.axis_index("seq")
        self.core, self.z = lax.rem(place, 2), lax.div(place, 2)
        self.partner = self.z * 2 + (1 - self.core)

    def swap(self):
        return to_seq(self.sa, self.ra, self.pair_sems.at[0], self.pair_sems.at[1], self.partner)

    def give(self):
        return to_seq(self.sc, self.rc, self.pair_sems.at[2], self.pair_sems.at[3], self.partner)

    def along(self, step):
        there = lax.rem(self.z + step, 4) * 2 + self.core
        return to_seq(
            self.sb, self.rb.at[step - 1], self.zs.at[step - 1], self.zr.at[step - 1], there
        )

    def start(self):
        self.sa[...] = self.local[1 - self.core].astype(bf16)
        self.swap().start()

    def middle(self):
        self.swap().wait_recv()
        self.sb[...] = (self.local[self.core] + self.ra[...].astype(f32)).astype(bf16)
        for step in (1, 2, 3):
            self.along(step).start()

    def late(self):
        total = jnp.zeros(self.sb.shape, f32)
        for step in (1, 2, 3):
            self.along(step).wait_recv()
            counts = one_if(self.z >= step if self.earlier else self.z < step)
            total = total + self.rb[step - 1].astype(f32) * counts
        takes = self.core if self.earlier else 1 - self.core
        self.sc[...] = (total + self.local[self.core] * one_if(takes == 0)).astype(bf16)
        self.give().start()
        self.state[self.core] = total + self.ra[...].astype(f32) * one_if(takes == 1)

    def end(self):
        self.give().wait_recv()
        self.state[1 - self.core] = self.rc[...].astype(f32)

    def drain(self):
        self.swap().wait_send()
        self.give().wait_send()
        for step in (1, 2, 3):
            self.along(step).wait_send()


def layer_kernel(
    inputs, cotangent, w_t, w_out, first_any, second_any, moves_any, conv, gains, rows, keep,
    layer_out, input_grad, *scratch,
):
    take = list(scratch)

    def pop(n):
        got = take[:n]
        del take[:n]
        return got

    fwd_bufs, bwd_bufs = pop(6), pop(6)
    fwd_sems, bwd_sems = pop(5), pop(5)
    (held_h, held_v, held_qk, weight_qk, flat, saved_w, saved_l, moved_q) = pop(8)
    (gs_h, gr_h, gs_v, gr_v, gs_q, gr_q) = pop(6)
    (ws, wr, us, ur, w_own, q_own) = pop(6)
    (fs, fr, zcs, zcr, ss, sr) = pop(6)
    early_bufs, late_bufs = pop(6), pop(6)
    early_sems, late_sems = pop(3), pop(3)
    (xin, cot, weights_t, weights_o) = pop(4)
    (pp, cv, mix, gh, dn, phi_q, phi_k, states, grads, scaled, dconv) = pop(11)
    (state_in, state_out, local_in, local_out, halo_in, halo_out) = pop(6)
    (first, second, moves) = pop(3)
    (x_sem, c_sem, w_sem, o_sem, r_sem, h_sem, k_sem) = pop(7)

    tp, place = lax.axis_index("tp"), lax.axis_index("seq")

    core, z = lax.rem(place, 2), lax.div(place, 2)
    fwd = Ring("x", "y", [(held_h, CH, gs_h, gr_h)], *fwd_bufs, layer_out, fwd_sems)
    streams = [(held_v, CH, gs_v, gr_v), (held_qk, CH // 2, gs_q, gr_q)]
    bwd = SplitRing("x", "y", streams, *bwd_bufs, input_grad, bwd_sems)
    bwd.flat, bwd.weight_qk = flat, weight_qk
    early = Carry(True, local_in, state_in, early_bufs, early_sems)
    later = Carry(False, local_out, state_out, late_bufs, late_sems)
    heads = held_h.at[0]

    def columns(t):
        return pl.ds(pl.multiple_of(t * 256, 256), 256)

    def out_block(t):
        return w_out.at[:, columns(t)]

    def swap_device():
        return place + 1 - 2 * core

    fwd_weights, fwd_swaps = [], []
    for d in (1, 2, 3):
        for j in range(2):
            k = core * 2 + j
            block = fwd.weight.at[k, d]
            at = (d - 1, j)
            fwd_weights.append(
                to_device(
                    out_block(block_at("x", d, "y", k)), block, ws.at[at], wr.at[at], neighbour("x", d)
                )
            )
            fwd_swaps.append(to_seq(block, block, us.at[at], ur.at[at], swap_device()))

    sides = ((bwd.weight, 128, 0), (weight_qk, 32, 256))
    bwd_weights, spreads, bwd_swaps = [], [], []
    for n, (array, size, start) in enumerate(sides):
        half = rows_of(core, size)
        theirs = pl.ds(pl.multiple_of(start + core * size, size), size)
        for d in (1, 2, 3):
            at = (n, d - 1)
            bwd_weights.append(
                to_device(
                    weights_t.at[theirs, columns(block_at("x", d, "y", z))],
                    array.at[z, d, half],
                    fs.at[at],
                    fr.at[at],
                    neighbour("x", d),
                )
            )
            mine = array.at[z, pl.ds(1, 3), half]
            there = lax.rem(z + d, 4) * 2 + core
            spreads.append(to_seq(mine, mine, zcs.at[at], zcr.at[at], there))
        ours = array.at[:, pl.ds(1, 3), half]
        bwd_swaps.append(to_seq(ours, ours, ss.at[n], sr.at[n], swap_device()))

    fwd_own, bwd_own = [], []
    for k in range(4):
        t = block_at("x", 0, "y", k)
        fwd_own.append(pltpu.make_async_copy(out_block(t), fwd.weight.at[k, 0], w_own.at[0, k]))
        for n, (array, size, start) in enumerate(sides):
            bwd_own.append(
                pltpu.make_async_copy(
                    weights_t.at[pl.ds(start, 2 * size), columns(t)], array.at[k, 0], q_own.at[n, k]
                )
            )

    pieces = ((32, 128, 0), (192, 128, 128), (0, 32, 256), (160, 32, 288))
    w_loads = [
        pltpu.make_async_copy(
            w_t.at[pl.ds(src, size)], weights_t.at[pl.ds(dst, size)], w_sem.at[n]
        )
        for n, (src, size, dst) in enumerate(pieces)
    ]
    for copy in w_loads:
        copy.start()

    def x_load(c):
        return pltpu.make_async_copy(inputs.at[rows_of(c)], xin.at[rows_of(c)], x_sem.at[c])

    def c_load(c):
        return pltpu.make_async_copy(cotangent.at[rows_of(c)], cot.at[rows_of(c)], c_sem.at[c])

    x_load(3).start()
    barrier = pltpu.get_barrier_semaphore()
    for d in (1, 2, 3):
        for along in ("x", "y"):
            pl.semaphore_signal(
                barrier, inc=1, device_id={"tp": neighbour(along, d)}, device_id_type=MESH
            )
    for d in (1, 2, 4, 6, 7):
        pl.semaphore_signal(
            barrier, inc=1, device_id={"seq": lax.rem(place + d, 8)}, device_id_type=MESH
        )
    weights_t[pl.ds(320, 64)] = jnp.zeros((64, weights_t.shape[1]), bf16)
    const_loads = [
        pltpu.make_async_copy(src, dst, k_sem.at[n])
        for n, (src, dst) in enumerate(
            ((first_any, first), (second_any, second), (moves_any, moves))
        )
    ]
    o_load = pltpu.make_async_copy(w_out, weights_o, o_sem.at[0])
    res_loads = [
        pltpu.make_async_copy(inputs.at[:, columns(tp)], fwd.res, r_sem.at[0]),
        pltpu.make_async_copy(cotangent.at[:, columns(tp)], bwd.res, r_sem.at[1]),
    ]
    src = lax.broadcasted_iota(jnp.int32, (320, LANES), 0)
    dst = lax.broadcasted_iota(jnp.int32, (320, LANES), 1)
    from_high = jnp.where(dst < 288, dst - 256, jnp.where(dst < 320, dst - 128, -1))
    source = jnp.where(dst < 128, dst + 32, jnp.where(dst < 256, dst + 64, from_high))
    taps = lax.dot_general(
        conv[...],
        jnp.where(src == source, 1.0, 0.0).astype(f32),
        NN,
        precision=lax.Precision.HIGHEST,
        preferred_element_type=f32,
    )
    lane = lax.broadcasted_iota(jnp.int32, (1, HEADS * DV), 1)
    gain = gains[...] * jnp.where(lane < DV, keep[0].astype(f32), keep[1].astype(f32))

    for copy in w_loads:
        copy.wait()
    for c in (0, 1, 2):
        x_load(c).start()
    for copy in const_loads + [o_load] + res_loads + fwd_own + bwd_own:
        copy.start()

    ahead = to_seq(
        pp.at[pl.ds(NCH * CH, 8)], halo_in, h_sem.at[0], h_sem.at[1], lax.rem(place + 1, 8)
    )
    behind = to_seq(
        dconv.at[pl.ds(0, 8)], halo_out, h_sem.at[2], h_sem.at[3], lax.rem(place + 7, 8)
    )

    @pl.loop(0, NCH)
    def _(i):
        c = lax.rem(i + NCH - 1, NCH)
        x_load(c).wait()
        c_load(c).start()
        projected = dot(xin[rows_of(c)], weights_t[...], NT).astype(bf16).astype(f32)
        pp[pl.ds(pl.multiple_of(c * CH + 8, 8), CH)] = projected

        @pl.when(i == 0)
        def _():
            pl.semaphore_wait(barrier, 11)
            ahead.start()
            for copy in bwd_weights + fwd_weights:
                copy.start()

    for copy in const_loads:
        copy.wait()
    ahead.wait()
    pp[pl.ds(0, 8)] = halo_in[...] * one_if(place > 0)

    t0, t1, t2 = taps[0:1], taps[1:2], taps[2:3]
    bias_a, bias_b, scale = rows[0:1], rows[1:2], rows[2:3]

    def factors(qk, group):
        return dot(qk, first[group]) + bias_a, dot(qk, second[group]) + bias_b

    def lanes(h):
        return slice(h * DV, (h + 1) * DV)

    def qk_of(c):
        return cv[rows_of(c), 2 * DV : LANES]

    local_in[...] = jnp.zeros(local_in.shape, f32)

    @pl.loop(0, NCH)
    def _(c):
        window = pp[pl.ds(pl.multiple_of(c * CH, CH), CH + 8)]
        mixed = t0 * window[8:] + (
            t1 * pltpu.roll(window, 1, 0)[8:] + t2 * pltpu.roll(window, 2, 0)[8:]
        )
        cv[rows_of(c)] = mixed.astype(bf16)
        qk = qk_of(c)
        for h in range(HEADS):
            a, b = factors(qk, 2 * h + 1)
            features = (a * b).astype(bf16)
            phi_k[h, rows_of(c)] = features
            local = dot(cv[rows_of(c), lanes(h)], features, TN)
            states[c, h] = local
            local_in[h] = local_in[h] + local

    early.start()

    causal = lax.broadcasted_iota(jnp.int32, (CH, CH), 0) >= lax.broadcasted_iota(
        jnp.int32, (CH, CH), 1
    )

    @pl.loop(0, NCH)
    def _(c):
        qk = qk_of(c)
        for h in range(HEADS):
            moved = dot(qk, moves[2 * h]).astype(bf16)
            moved_q[h, rows_of(c)] = moved
            logits = dot(moved, qk, NT) * 0.25
            weight = jnp.where(causal, 1.0 + logits + 0.5 * logits * logits, 0.0).astype(bf16)
            saved_w[h, rows_of(c)] = weight
            saved_l[h, rows_of(c)] = jnp.where(causal, 0.25 + 0.25 * logits, 0.0)
            mix[rows_of(c), lanes(h)] = dot(weight, cv[rows_of(c), lanes(h)])

        @pl.when(c == 1)
        def _():
            early.middle()

    o_load.wait()

    @pl.loop(0, NCH)
    def _(c):
        c_load(c).wait()
        gh[rows_of(c)] = dot(cot[rows_of(c)], weights_o[...], NT) * gain

    @pl.loop(0, NCH)
    def _(c):
        qk = qk_of(c)
        for h in range(HEADS):
            a, b = factors(qk, 2 * h)
            phi_q[h, rows_of(c)] = (a * b).astype(bf16)

    early.late()
    for copy in bwd_weights:
        copy.wait()
    for copy in spreads:
        copy.start()
    early.end()
    local_out[...] = jnp.zeros(local_out.shape, f32)

    @pl.loop(0, NCH)
    def _(c):
        for h in range(HEADS):
            entering = state_in[h]
            state_in[h] = entering + states[c, h]
            scaled[c, h] = (entering * scale).astype(bf16)
            numerator = mix[rows_of(c), lanes(h)] + dot(phi_q[h, rows_of(c)], scaled[c, h], NT)
            inverse = 1.0 / jnp.sqrt(jnp.mean(numerator * numerator, -1, keepdims=True) + epsilon)
            normed = numerator * inverse
            heads[rows_of(c), lanes(h)] = (normed * gain[:, lanes(h)]).astype(bf16)
            grad = gh[rows_of(c), lanes(h)]
            d_numer = (grad - normed * jnp.mean(grad * normed, -1, keepdims=True)) * inverse
            rounded = d_numer.astype(bf16)
            dn[rows_of(c), lanes(h)] = rounded
            local = dot(rounded, phi_q[h, rows_of(c)], TN)
            grads[c, h] = local
            local_out[h] = local_out[h] + local
        fwd.send_own(c)

    later.start()
    for copy in fwd_weights:
        copy.wait()
    for copy in fwd_swaps:
        copy.start()

    @pl.loop(0, NCH)
    def _(c):
        qk = qk_of(c)
        d_qk = jnp.zeros((CH, 128), f32)
        for h in range(HEADS):
            rounded = dn[rows_of(c), lanes(h)]
            dconv[rows_of(c), lanes(h)] = dot(saved_w[h, rows_of(c)], rounded, TN)
            d_weight = dot(rounded, cv[rows_of(c), lanes(h)], NT)
            d_logits = (d_weight * saved_l[h, rows_of(c)]).astype(bf16)
            d_qk = d_qk + dot(d_logits, dot(qk, moves[2 * h + 1]).astype(bf16))
            d_qk = d_qk + dot(d_logits, moved_q[h, rows_of(c)], TN)
            a, b = factors(qk, 2 * h)
            d_phi = dot(rounded, scaled[c, h])
            d_qk = d_qk + dot((d_phi * b).astype(bf16), first[2 * h], NT)
            d_qk = d_qk + dot((d_phi * a).astype(bf16), second[2 * h], NT)
        dconv[rows_of(c), 2 * DV : LANES] = d_qk

        @pl.when(c == 1)
        def _():
            later.middle()

        @pl.when(c == 3)
        def _():
            later.late()

        fwd.forward(c)

    later.end()
    state_out[...] = state_out[...] + local_out[...]

    def project_back(c):
        window = dconv[pl.ds(pl.multiple_of(c * CH, CH), CH + 8)]
        mixed = t0 * window[:CH] + (
            t1 * pltpu.roll(window, CH + 7, 0)[:CH] + t2 * pltpu.roll(window, CH + 6, 0)[:CH]
        )
        held_v[0, rows_of(c)] = mixed[:, : 2 * DV].astype(bf16)
        packed = mixed[: CH // 2, 2 * DV :] + pltpu.roll(mixed[CH // 2 :, 2 * DV :], 64, 1)
        held_qk[0, rows_of(c, CH // 2)] = packed.astype(bf16)

    @pl.loop(0, NCH)
    def _(c):
        qk = qk_of(c)
        d_qk = dconv[rows_of(c), 2 * DV : LANES]
        for h in range(HEADS):
            remaining = state_out[h] - grads[c, h]
            state_out[h] = remaining
            suffix = (remaining * scale).astype(bf16)
            dconv[rows_of(c), lanes(h)] = dconv[rows_of(c), lanes(h)] + dot(
                phi_k[h, rows_of(c)], suffix, NT
            )
            a, b = factors(qk, 2 * h + 1)
            d_phi = dot(cv[rows_of(c), lanes(h)], suffix)
            d_qk = d_qk + dot((d_phi * b).astype(bf16), first[2 * h + 1], NT)
            d_qk = d_qk + dot((d_phi * a).astype(bf16), second[2 * h + 1], NT)
        dconv[rows_of(c), 2 * DV : LANES] = d_qk

        @pl.when(c == 0)
        def _():
            behind.start()

        @pl.when(c > 0)
        def _():
            project_back(c - 1)

        @pl.when((c == 1) | (c == 2))
        def _():
            bwd.send_own(c - 1)

    behind.wait()
    dconv[pl.ds(NCH * CH, 8)] = halo_out[...] * one_if(place < 7)
    project_back(NCH - 1)
    for copy in fwd_swaps + fwd_own + bwd_own + res_loads:
        copy.wait()

    @pl.loop(0, NCH + 3)
    def _(i):
        @pl.when(i == 1)
        def _():
            for copy in spreads:
                copy.wait()
            for copy in bwd_swaps:
                copy.start()

        @pl.when(i < NCH)
        def _():
            fwd.multiply(i)
            bwd.forward(i)

        @pl.when(i < NCH - 2)
        def _():
            bwd.send_own(i + 2)

        @pl.when(i == 1)
        def _():
            for copy in bwd_swaps:
                copy.wait()

        @pl.when((i >= 1) & (i < NCH + 1))
        def _():
            fwd.relayed(i - 1)
            bwd.multiply(i - 1)

        @pl.when((i >= 2) & (i < NCH + 2))
        def _():
            bwd.relayed(i - 2)
            fwd.finish(i - 2)

        @pl.when(i >= 3)
        def _():
            bwd.finish(i - 3)

    @pl.loop(0, NCH)
    def _(c):
        fwd.drain(c)
        bwd.drain(c)

    early.drain()
    later.drain()


def settle_kernel(first, second, first_out, second_out, held, in_sem, out_sem):
    pairs = ((first, first_out), (second, second_out))
    ins = [pltpu.make_async_copy(p[0], held.at[n], in_sem.at[n]) for n, p in enumerate(pairs)]
    outs = [pltpu.make_async_copy(held.at[n], p[1], out_sem.at[n]) for n, p in enumerate(pairs)]
    for copy in ins:
        copy.start()
    for n in range(2):
        ins[n].wait()
        outs[n].start()
    for copy in outs:
        copy.wait()


def settle(first, second):
    whole = pl.BlockSpec(memory_space=pl.ANY)
    result = jax.ShapeDtypeStruct(first.shape, first.dtype)
    dma = pltpu.SemaphoreType.DMA
    return pl.pallas_call(
        settle_kernel,
        out_shape=(result, result),
        in_specs=[whole] * 2,
        out_specs=(whole, whole),
        scratch_shapes=[pltpu.VMEM((2,) + first.shape, first.dtype), dma((2,)), dma((2,))],
    )(first, second)


def per_device(inputs, cotangent, w_in, conv_w, norm_gain, w_out, keep_flags):
    count, width = inputs.shape
    first, second, rows, moves = selectors()
    consts = [jnp.asarray(part, bf16) for part in (first, second, moves)]
    whole, near = pl.BlockSpec(memory_space=pl.ANY), pl.BlockSpec(memory_space=pltpu.VMEM)
    result = jax.ShapeDtypeStruct((count, 256), bf16)
    dma = pltpu.SemaphoreType.DMA
    state = (DV, EXP)
    carry_bufs = [pltpu.VMEM((n,) + state if n > 1 else state, bf16) for n in (1, 1, 1, 3, 1, 1)]
    carry_sems = [dma((4,)), dma((3,)), dma((3,))]
    results = pl.pallas_call(
        layer_kernel,
        out_shape=(result, result),
        in_specs=[whole] * 7 + [near] * 3 + [pl.BlockSpec(memory_space=pltpu.SMEM)],
        out_specs=(whole, whole),
        scratch_shapes=ring_buffers(count)
        + ring_buffers(count)
        + ring_semaphores()
        + ring_semaphores()
        + [
            pltpu.VMEM((4, count, 256), bf16),
            pltpu.VMEM((4, count, 256), bf16),
            pltpu.VMEM((4, count // 2, 128), bf16),
            pltpu.VMEM((4, 4, 64, 256), bf16),
            pltpu.VMEM((CH, 256), bf16),
            pltpu.VMEM((HEADS, count, CH), bf16),
            pltpu.VMEM((HEADS, count, CH), f32),
            pltpu.VMEM((HEADS, count, 128), bf16),
        ]
        + [dma((3, NCH))] * 6
        + [dma((3, 2))] * 4
        + [dma((1, 4)), dma((2, 4))]
        + [dma((2, 3))] * 4
        + [dma((2,))] * 2
        + carry_bufs
        + carry_bufs
        + carry_sems
        + carry_sems
        + [
            pltpu.VMEM((count, width), bf16),
            pltpu.VMEM((count, width), bf16),
            pltpu.VMEM((LANES, width), bf16),
            pltpu.VMEM((256, width), bf16),
            pltpu.VMEM((count + 8, LANES), f32),
            pltpu.VMEM((count, LANES), bf16),
            pltpu.VMEM((count, 256), f32),
            pltpu.VMEM((count, 256), f32),
            pltpu.VMEM((count, 256), bf16),
            pltpu.VMEM((HEADS, count, EXP), bf16),
            pltpu.VMEM((HEADS, count, EXP), bf16),
            pltpu.VMEM((NCH, HEADS) + state, f32),
            pltpu.VMEM((NCH, HEADS) + state, f32),
            pltpu.VMEM((NCH, HEADS) + state, bf16),
            pltpu.VMEM((count + 8, LANES), f32),
            pltpu.VMEM((HEADS,) + state, f32),
            pltpu.VMEM((HEADS,) + state, f32),
            pltpu.VMEM((HEADS,) + state, f32),
            pltpu.VMEM((HEADS,) + state, f32),
            pltpu.VMEM((8, LANES), f32),
            pltpu.VMEM((8, LANES), f32),
            pltpu.VMEM((4, 128, EXP), bf16),
            pltpu.VMEM((4, 128, EXP), bf16),
            pltpu.VMEM((4, 128, 128), bf16),
            dma((NCH,)),
            dma((NCH,)),
            dma((4,)),
            dma((1,)),
            dma((2,)),
            dma((4,)),
            dma((3,)),
        ],
        compiler_params=pltpu.CompilerParams(
            collective_id=0, has_side_effects=True, vmem_limit_bytes=62 << 20
        ),
    )(
        inputs,
        cotangent,
        w_in.T,
        w_out,
        *consts,
        conv_w,
        norm_gain.reshape(1, HEADS * DV),
        jnp.asarray(rows),
        keep_flags,
    )
    return settle(*results)


def solution(mesh):
    placed = (
        P("seq", None),
        P("seq", None),
        P(None, "tp"),
        P(None, "tp"),
        P("tp"),
        P("tp", None),
        P("tp"),
    )
    return jax.shard_map(
        per_device,
        mesh=mesh,
        in_specs=placed,
        out_specs=(P("seq", "tp"), P("seq", "tp")),
        check_vma=False,
    )
```

```python
from functools import partial

import jax
import jax.numpy as jnp
import numpy as np
from jax import lax
from jax.experimental import pallas as pl
from jax.experimental.pallas import tpu as pltpu
from jax.sharding import PartitionSpec as P

FEAT = 16
DV = 128
LANES = 384
EXP = 256
HEADS = 2
epsilon = 1e-06

CH = 256
NCH = 4
MESH = pl.DeviceIdType.MESH
NT = (((1,), (1,)), ((), ()))
NN = (((1,), (0,)), ((), ()))
TN = (((0,), (0,)), ((), ()))
f32 = jnp.float32
bf16 = jnp.bfloat16


def neighbour(along, step):
    place = lax.axis_index("tp")
    column, row = lax.rem(place, 4), lax.div(place, 4)
    if along == "x":
        return row * 4 + lax.rem(column + step, 4)
    return lax.rem(row + step, 4) * 4 + column


def block_at(a_along, a_step, r_along, r_step):
    place = lax.axis_index("tp")
    column, row = lax.rem(place, 4), lax.div(place, 4)
    x_step = a_step if a_along == "x" else r_step
    y_step = a_step if a_along == "y" else r_step
    return lax.rem(row + y_step, 4) * 4 + lax.rem(column + x_step, 4)


def to_device(src, dst, send_sem, recv_sem, place):
    return pltpu.make_async_remote_copy(
        src_ref=src,
        dst_ref=dst,
        send_sem=send_sem,
        recv_sem=recv_sem,
        device_id={"tp": place},
        device_id_type=MESH,
    )


def to_seq(src, dst, send_sem, recv_sem, place):
    return pltpu.make_async_remote_copy(
        src_ref=src,
        dst_ref=dst,
        send_sem=send_sem,
        recv_sem=recv_sem,
        device_id={"seq": place},
        device_id_type=MESH,
    )


def dot(a, b, dims=NN):
    return lax.dot_general(a, b, dims, preferred_element_type=f32)


def rows_of(c, size=CH):
    return pl.ds(pl.multiple_of(c * size, size), size)


def way(c):
    return jnp.where(c < NCH // 2, 1, 3)


class Ring:
    def __init__(self, flip, streams, weight, part, landed, relay, keep, res, out, sems):
        self.flip, self.streams, self.weight = flip, streams, weight
        self.part, self.landed, self.relay = part, landed, relay
        self.keep, self.res, self.out = keep, res, out
        (self.ts, self.tr, self.ps, self.pr, self.os) = sems

    def turn(self, c):
        return lax.rem(c + self.flip, 2)

    def gather_to(self, c, d):
        return jnp.where(self.turn(c) == 0, neighbour("x", d), neighbour("y", d))

    def scatter_to(self, c, d):
        return jnp.where(self.turn(c) == 0, neighbour("y", d), neighbour("x", d))

    def direct(self, c, d):
        return [
            to_device(
                held.at[0, rows_of(c, size)],
                held.at[d, rows_of(c, size)],
                send.at[d - 1, c],
                recv.at[d - 1, c],
                self.gather_to(c, d),
            )
            for held, size, send, recv in self.streams
        ]

    def passed_on(self, c):
        return [
            to_device(
                held.at[way(c), rows_of(c, size)],
                held.at[2, rows_of(c, size)],
                send.at[1, c],
                recv.at[1, c],
                self.gather_to(c, way(c)),
            )
            for held, size, send, recv in self.streams
        ]

    def send_own(self, c):
        for d in (1, 3):
            for copy in self.direct(c, d):
                copy.start()

    def forward(self, c):
        for d in (1, 3):
            for copy in self.direct(c, d):
                copy.wait_recv()
        for copy in self.passed_on(c):
            copy.start()

    def tie(self, c):
        return to_device(
            self.part.at[2, rows_of(c)],
            self.relay.at[rows_of(c)],
            self.ts.at[c],
            self.tr.at[c],
            self.scatter_to(c, way(c)),
        )

    def side(self, c, d):
        return to_device(
            self.part.at[d, rows_of(c)],
            self.landed.at[d // 2, rows_of(c)],
            self.ps.at[d // 2, c],
            self.pr.at[d // 2, c],
            self.scatter_to(c, d),
        )

    def prepare(self, c):
        pass

    def product(self, c, k):
        held = self.streams[0][0]
        total = None
        for o in range(4):
            term = dot(held[o, rows_of(c)], self.weight[self.turn(c), k, o])
            total = term if total is None else total + term
        return total

    def compute(self, c):
        for copy in self.passed_on(c):
            copy.wait_recv()
        self.prepare(c)
        near, far = way(c), 4 - way(c)
        self.part[2, rows_of(c)] = self.product(c, 2).astype(bf16)
        self.part[far, rows_of(c)] = self.product(c, far).astype(bf16)
        self.keep[1, rows_of(c)] = self.product(c, near)
        self.keep[0, rows_of(c)] = self.product(c, 0) + self.res[rows_of(c)].astype(f32)

    def send(self, c):
        self.tie(c).start()
        self.side(c, 4 - way(c)).start()

    def multiply(self, c):
        for copy in self.passed_on(c):
            copy.wait_recv()
        self.prepare(c)
        near, far = way(c), 4 - way(c)
        self.part[2, rows_of(c)] = self.product(c, 2).astype(bf16)
        self.tie(c).start()
        self.keep[1, rows_of(c)] = self.product(c, near)
        self.part[far, rows_of(c)] = self.product(c, far).astype(bf16)
        self.side(c, far).start()
        self.keep[0, rows_of(c)] = self.product(c, 0) + self.res[rows_of(c)].astype(f32)

    def relayed(self, c):
        self.tie(c).wait_recv()
        near = way(c)
        total = self.keep[1, rows_of(c)] + self.relay[rows_of(c)].astype(f32)
        self.part[near, rows_of(c)] = total.astype(bf16)
        self.side(c, near).start()

    def finish(self, c):
        self.side(c, 1).wait_recv()
        self.side(c, 3).wait_recv()
        total = self.keep[0, rows_of(c)] + (
            self.landed[0, rows_of(c)].astype(f32) + self.landed[1, rows_of(c)].astype(f32)
        )
        self.part[0, rows_of(c)] = total.astype(bf16)
        self.leave(c).start()

    def leave(self, c):
        return pltpu.make_async_copy(
            self.part.at[0, rows_of(c)], self.out.at[rows_of(c)], self.os.at[c]
        )

    def drain(self, c):
        for copy in self.direct(c, 1) + self.direct(c, 3) + self.passed_on(c):
            copy.wait_send()
        self.tie(c).wait_send()
        self.side(c, 1).wait_send()
        self.side(c, 3).wait_send()
        self.leave(c).wait()


class SplitRing(Ring):
    def prepare(self, c):
        packed = self.streams[1][0]
        low = lax.broadcasted_iota(jnp.int32, (CH // 2, 128), 1) < 64
        for pair in range(2):
            one = packed[2 * pair, rows_of(c, CH // 2)].astype(f32)
            two = packed[2 * pair + 1, rows_of(c, CH // 2)].astype(f32)
            top = jnp.where(low, one, pltpu.roll(two, 64, 1))
            bottom = jnp.where(low, pltpu.roll(one, 64, 1), two)
            lanes = slice(pair * 128, pair * 128 + 128)
            self.flat[0 : CH // 2, lanes] = top.astype(bf16)
            self.flat[CH // 2 : CH, lanes] = bottom.astype(bf16)

    def product(self, c, k):
        return super().product(c, k) + dot(self.flat[...], self.weight_qk[self.turn(c), k].reshape(256, 256))


def ring_semaphores():
    dma = pltpu.SemaphoreType.DMA
    return [dma((NCH,)), dma((NCH,)), dma((2, NCH)), dma((2, NCH)), dma((NCH,))]


def ring_buffers(rows):
    return [
        pltpu.VMEM((2, 4, 4, 256, 256), bf16),
        pltpu.VMEM((4, rows, 256), bf16),
        pltpu.VMEM((2, rows, 256), bf16),
        pltpu.VMEM((rows, 256), bf16),
        pltpu.VMEM((2, rows, 256), f32),
        pltpu.VMEM((rows, 256), bf16),
    ]


def selectors():
    first = np.zeros((4, 128, EXP), np.float32)
    second = np.zeros((4, 128, EXP), np.float32)
    rows = np.zeros((8, EXP), np.float32)
    rows[0, 0] = rows[1, 0] = rows[2, 0] = 1.0
    for group in range(4):
        base = group * FEAT
        for i in range(FEAT):
            first[group, base + i, 1 + i] = 1.0
            rows[1, 1 + i] = 1.0
            rows[2, 1 + i] = 0.25
        e = 1 + FEAT
        for i in range(FEAT):
            for j in range(i, FEAT):
                first[group, base + i, e] = 1.0
                second[group, base + j, e] = 1.0
                rows[2, e] = 1 / 32 if i == j else 1 / 16
                e += 1
    moves = np.zeros((4, 128, 128), np.float32)
    for h in range(HEADS):
        for i in range(FEAT):
            q, k = 2 * h * FEAT + i, (2 * h + 1) * FEAT + i
            moves[2 * h, q, k] = 1.0
            moves[2 * h + 1, k, q] = 1.0
    return first, second, rows, moves


def one_if(condition):
    return jnp.where(condition, 1.0, 0.0).astype(f32)


def packed_state(state):
    rest = state[:32, DV:]
    for g in range(1, 4):
        rest = rest + pltpu.roll(state[32 * g : 32 * g + 32, DV:], 32 * g, 1)
    return jnp.concatenate([state[:, :DV], rest], 0)


def whole_state(packed):
    low = lax.broadcasted_iota(jnp.int32, (32, DV), 1) < 32
    rest = packed[DV:]
    parts = [rest] + [pltpu.roll(rest, DV - 32 * g, 1) for g in range(1, 4)]
    parts = [jnp.where(low, part, 0.0) for part in parts]
    return jnp.concatenate([packed[:DV], jnp.concatenate(parts, 0)], 1)


class Carry:
    def __init__(self, earlier, local, state, bufs, sems):
        self.earlier, self.local, self.state = earlier, local, state
        self.sa, self.ra, self.sb, self.rb, self.sc, self.rc = bufs
        self.pair_sems, self.zs, self.zr = sems
        place = lax.axis_index("seq")
        self.core, self.z = lax.rem(place, 2), lax.div(place, 2)
        self.partner = self.z * 2 + (1 - self.core)

    def swap(self):
        return to_seq(self.sa, self.ra, self.pair_sems.at[0], self.pair_sems.at[1], self.partner)

    def give(self):
        return to_seq(self.sc, self.rc, self.pair_sems.at[2], self.pair_sems.at[3], self.partner)

    def along(self, step):
        there = lax.rem(self.z + step, 4) * 2 + self.core
        return to_seq(
            self.sb, self.rb.at[step - 1], self.zs.at[step - 1], self.zr.at[step - 1], there
        )

    def start(self):
        self.sa[...] = packed_state(self.local[1 - self.core]).astype(bf16)
        self.swap().start()

    def middle(self):
        self.swap().wait_recv()
        self.sb[...] = (packed_state(self.local[self.core]) + self.ra[...].astype(f32)).astype(bf16)
        for step in (1, 2, 3):
            self.along(step).start()

    def late(self):
        total = jnp.zeros(self.sb.shape, f32)
        for step in (1, 2, 3):
            self.along(step).wait_recv()
            counts = one_if(self.z >= step if self.earlier else self.z < step)
            total = total + self.rb[step - 1].astype(f32) * counts
        takes = self.core if self.earlier else 1 - self.core
        own = packed_state(self.local[self.core]) * one_if(takes == 0)
        self.sc[...] = (total + own).astype(bf16)
        self.give().start()
        self.state[self.core] = whole_state(total + self.ra[...].astype(f32) * one_if(takes == 1))

    def end(self):
        self.give().wait_recv()
        self.state[1 - self.core] = whole_state(self.rc[...].astype(f32))

    def drain(self):
        self.swap().wait_send()
        self.give().wait_send()
        for step in (1, 2, 3):
            self.along(step).wait_send()


def layer_kernel(
    inputs, cotangent, w_t, w_out, first_any, second_any, moves_any, conv, gains, rows, keep,
    layer_out, input_grad, *scratch,
):
    take = list(scratch)

    def pop(n):
        got = take[:n]
        del take[:n]
        return got

    fwd_bufs, bwd_bufs = pop(6), pop(6)
    fwd_sems, bwd_sems = pop(5), pop(5)
    (held_h, held_v, held_qk, weight_qk, flat, saved_w, saved_l, moved_q) = pop(8)
    (gs_h, gr_h, gs_v, gr_v, gs_q, gr_q) = pop(6)
    (ws, wr, us, ur, w_own, q_own) = pop(6)
    (fs, fr, zcs, zcr, rys, ryr, ss, sr) = pop(8)
    early_bufs, late_bufs = pop(6), pop(6)
    early_sems, late_sems = pop(3), pop(3)
    (xin, cot, weights_t, weights_o) = pop(4)
    (pp, cv, mix, gh, dn, phi_q, phi_k, states, grads, scaled) = pop(10)
    dconv = pp
    (state_in, state_out, local_in, local_out, halo_in, halo_out) = pop(6)
    (first, second, moves) = pop(3)
    (x_sem, c_sem, w_sem, o_sem, r_sem, h_sem, k_sem) = pop(7)

    tp, place = lax.axis_index("tp"), lax.axis_index("seq")

    core, z = lax.rem(place, 2), lax.div(place, 2)
    fwd = Ring(1, [(held_h, CH, gs_h, gr_h)], *fwd_bufs, layer_out, fwd_sems)
    streams = [(held_v, CH, gs_v, gr_v), (held_qk, CH // 2, gs_q, gr_q)]
    bwd = SplitRing(0, streams, *bwd_bufs, input_grad, bwd_sems)
    bwd.flat, bwd.weight_qk = flat, weight_qk
    early = Carry(True, local_in, state_in, early_bufs, early_sems)
    later = Carry(False, local_out, state_out, late_bufs, late_sems)
    heads = held_h.at[0]

    def columns(t):
        return pl.ds(pl.multiple_of(t * 256, 256), 256)

    def out_block(t):
        return w_out.at[:, columns(t)]

    def swap_device():
        return place + 1 - 2 * core

    sides = ((bwd.weight, 128, 0), (weight_qk, 32, 256))
    fwd_weights, fwd_swaps, fwd_own, bwd_own = [], [], [], []
    bwd_weights, spreads, relays, bwd_swaps = [], ([], []), ([], []), ([], [])
    for p, (a, r) in enumerate((("x", "y"), ("y", "x"))):
        for d in (1, 2, 3):
            for j in range(2):
                k = core * 2 + j
                block = fwd.weight.at[p, k, d]
                at = (p, d - 1, j)
                wanted = out_block(block_at(a, d, r, k))
                fwd_weights.append(to_device(wanted, block, ws.at[at], wr.at[at], neighbour(a, d)))
                fwd_swaps.append(to_seq(block, block, us.at[at], ur.at[at], swap_device()))
        for n, (array, size, start) in enumerate(sides):
            half = rows_of(core, size)
            theirs = pl.ds(pl.multiple_of(start + core * size, size), size)
            for d in (1, 2, 3):
                at = (p, n, d - 1)
                wanted = weights_t.at[theirs, columns(block_at(a, d, r, z))]
                bwd_weights.append(
                    to_device(wanted, array.at[p, z, d, half], fs.at[at], fr.at[at], neighbour(a, d))
                )
            for n_way, step in enumerate((1, 3)):
                at = (p, n, n_way)
                there = lax.rem(z + step, 4) * 2 + core
                mine = array.at[p, z, pl.ds(1, 3), half]
                spreads[p].append(to_seq(mine, mine, zcs.at[at], zcr.at[at], there))
                near = lax.rem(z + 4 - step, 4)
                rows_in = pl.ds(
                    pl.multiple_of(core * size + n_way * (size // 2), size // 2), size // 2
                )
                passing = array.at[p, near, pl.ds(1, 3), rows_in]
                relays[p].append(to_seq(passing, passing, rys.at[at], ryr.at[at], there))
            ours = array.at[p, :, pl.ds(1, 3), half]
            bwd_swaps[p].append(to_seq(ours, ours, ss.at[p, n], sr.at[p, n], swap_device()))
        for k in range(4):
            t = block_at(a, 0, r, k)
            fwd_own.append(
                pltpu.make_async_copy(out_block(t), fwd.weight.at[p, k, 0], w_own.at[p, k])
            )
            for n, (array, size, start) in enumerate(sides):
                wanted = weights_t.at[pl.ds(start, 2 * size), columns(t)]
                bwd_own.append(
                    pltpu.make_async_copy(wanted, array.at[p, k, 0], q_own.at[p, n, k])
                )

    pieces = ((32, 128, 0), (192, 128, 128), (0, 32, 256), (160, 32, 288))
    w_loads = [
        pltpu.make_async_copy(
            w_t.at[pl.ds(src, size)], weights_t.at[pl.ds(dst, size)], w_sem.at[n]
        )
        for n, (src, size, dst) in enumerate(pieces)
    ]
    for copy in w_loads:
        copy.start()

    def x_load(c):
        return pltpu.make_async_copy(inputs.at[rows_of(c)], xin.at[rows_of(c)], x_sem.at[c])

    def c_load(c):
        return pltpu.make_async_copy(cotangent.at[rows_of(c)], cot.at[rows_of(c)], c_sem.at[c])

    x_load(3).start()
    barrier = pltpu.get_barrier_semaphore()
    for d in (1, 2, 3):
        for along in ("x", "y"):
            pl.semaphore_signal(
                barrier, inc=1, device_id={"tp": neighbour(along, d)}, device_id_type=MESH
            )
    for d in (1, 2, 4, 6, 7):
        pl.semaphore_signal(
            barrier, inc=1, device_id={"seq": lax.rem(place + d, 8)}, device_id_type=MESH
        )
    weights_t[pl.ds(320, 64)] = jnp.zeros((64, weights_t.shape[1]), bf16)
    const_loads = [
        pltpu.make_async_copy(src, dst, k_sem.at[n])
        for n, (src, dst) in enumerate(
            ((first_any, first), (second_any, second), (moves_any, moves))
        )
    ]
    o_load = pltpu.make_async_copy(w_out, weights_o, o_sem.at[0])
    res_loads = [
        pltpu.make_async_copy(inputs.at[:, columns(tp)], fwd.res, r_sem.at[0]),
        pltpu.make_async_copy(cotangent.at[:, columns(tp)], bwd.res, r_sem.at[1]),
    ]
    src = lax.broadcasted_iota(jnp.int32, (320, LANES), 0)
    dst = lax.broadcasted_iota(jnp.int32, (320, LANES), 1)
    from_high = jnp.where(dst < 288, dst - 256, jnp.where(dst < 320, dst - 128, -1))
    source = jnp.where(dst < 128, dst + 32, jnp.where(dst < 256, dst + 64, from_high))
    taps = lax.dot_general(
        conv[...],
        jnp.where(src == source, 1.0, 0.0).astype(f32),
        NN,
        precision=lax.Precision.HIGHEST,
        preferred_element_type=f32,
    )
    lane = lax.broadcasted_iota(jnp.int32, (1, HEADS * DV), 1)
    gain = gains[...] * jnp.where(lane < DV, keep[0].astype(f32), keep[1].astype(f32))

    for copy in w_loads:
        copy.wait()
    for c in (0, 1, 2):
        x_load(c).start()
    for copy in const_loads + [o_load] + res_loads + fwd_own + bwd_own:
        copy.start()

    ahead = to_seq(
        pp.at[pl.ds(NCH * CH, 8)], halo_in, h_sem.at[0], h_sem.at[1], lax.rem(place + 1, 8)
    )
    behind = to_seq(
        dconv.at[pl.ds(0, 8)], halo_out, h_sem.at[2], h_sem.at[3], lax.rem(place + 7, 8)
    )

    @pl.loop(0, NCH)
    def _(i):
        c = lax.rem(i + NCH - 1, NCH)
        x_load(c).wait()
        c_load(c).start()
        projected = dot(xin[rows_of(c)], weights_t[...], NT).astype(bf16).astype(f32)
        pp[pl.ds(pl.multiple_of(c * CH + 8, 8), CH)] = projected

        @pl.when(i == 0)
        def _():
            pl.semaphore_wait(barrier, 11)
            ahead.start()
            for copy in bwd_weights + fwd_weights:
                copy.start()

    for copy in const_loads:
        copy.wait()
    ahead.wait()
    pp[pl.ds(0, 8)] = halo_in[...] * one_if(place > 0)

    t0, t1, t2 = taps[0:1], taps[1:2], taps[2:3]
    bias_a, bias_b, scale = rows[0:1], rows[1:2], rows[2:3]

    def factors(qk, group):
        return dot(qk, first[group]) + bias_a, dot(qk, second[group]) + bias_b

    def lanes(h):
        return slice(h * DV, (h + 1) * DV)

    def qk_of(c):
        return cv[rows_of(c), 2 * DV : LANES]

    local_in[...] = jnp.zeros(local_in.shape, f32)

    @pl.loop(0, NCH)
    def _(c):
        window = pp[pl.ds(pl.multiple_of(c * CH, CH), CH + 8)]
        mixed = t0 * window[8:] + (
            t1 * pltpu.roll(window, 1, 0)[8:] + t2 * pltpu.roll(window, 2, 0)[8:]
        )
        cv[rows_of(c)] = mixed.astype(bf16)
        qk = qk_of(c)
        for h in range(HEADS):
            a, b = factors(qk, 2 * h + 1)
            features = (a * b).astype(bf16)
            phi_k[h, rows_of(c)] = features
            local = dot(cv[rows_of(c), lanes(h)], features, TN)
            states[c, h] = local
            local_in[h] = local_in[h] + local

    early.start()

    causal = lax.broadcasted_iota(jnp.int32, (CH, CH), 0) >= lax.broadcasted_iota(
        jnp.int32, (CH, CH), 1
    )

    @pl.loop(0, NCH)
    def _(c):
        qk = qk_of(c)
        for h in range(HEADS):
            moved = dot(qk, moves[2 * h]).astype(bf16)
            moved_q[h, rows_of(c)] = moved
            logits = dot(moved, qk, NT) * 0.25
            weight = jnp.where(causal, 1.0 + logits + 0.5 * logits * logits, 0.0).astype(bf16)
            saved_w[h, rows_of(c)] = weight
            saved_l[h, rows_of(c)] = jnp.where(causal, 0.25 + 0.25 * logits, 0.0)
            mix[rows_of(c), lanes(h)] = dot(weight, cv[rows_of(c), lanes(h)])

        @pl.when(c == 1)
        def _():
            early.middle()

    o_load.wait()

    @pl.loop(0, NCH)
    def _(c):
        c_load(c).wait()
        gh[rows_of(c)] = dot(cot[rows_of(c)], weights_o[...], NT) * gain

    @pl.loop(0, NCH)
    def _(c):
        qk = qk_of(c)
        for h in range(HEADS):
            a, b = factors(qk, 2 * h)
            phi_q[h, rows_of(c)] = (a * b).astype(bf16)

    early.late()
    for copy in bwd_weights:
        copy.wait()
    for copy in spreads[0]:
        copy.start()
    early.end()
    local_out[...] = jnp.zeros(local_out.shape, f32)

    @pl.loop(0, NCH)
    def _(c):
        for h in range(HEADS):
            entering = state_in[h]
            state_in[h] = entering + states[c, h]
            scaled[c, h] = (entering * scale).astype(bf16)
            numerator = mix[rows_of(c), lanes(h)] + dot(phi_q[h, rows_of(c)], scaled[c, h], NT)
            inverse = 1.0 / jnp.sqrt(jnp.mean(numerator * numerator, -1, keepdims=True) + epsilon)
            normed = numerator * inverse
            heads[rows_of(c), lanes(h)] = (normed * gain[:, lanes(h)]).astype(bf16)
            grad = gh[rows_of(c), lanes(h)]
            d_numer = (grad - normed * jnp.mean(grad * normed, -1, keepdims=True)) * inverse
            rounded = d_numer.astype(bf16)
            dn[rows_of(c), lanes(h)] = rounded
            local = dot(rounded, phi_q[h, rows_of(c)], TN)
            grads[c, h] = local
            local_out[h] = local_out[h] + local
        fwd.send_own(c)

    later.start()
    for copy in fwd_weights:
        copy.wait()
    for copy in fwd_swaps:
        copy.start()

    @pl.loop(0, NCH)
    def _(c):
        qk = qk_of(c)
        d_qk = jnp.zeros((CH, 128), f32)
        for h in range(HEADS):
            rounded = dn[rows_of(c), lanes(h)]
            dconv[rows_of(c), lanes(h)] = dot(saved_w[h, rows_of(c)], rounded, TN)
            d_weight = dot(rounded, cv[rows_of(c), lanes(h)], NT)
            d_logits = (d_weight * saved_l[h, rows_of(c)]).astype(bf16)
            d_qk = d_qk + dot(d_logits, dot(qk, moves[2 * h + 1]).astype(bf16))
            d_qk = d_qk + dot(d_logits, moved_q[h, rows_of(c)], TN)
            a, b = factors(qk, 2 * h)
            d_phi = dot(rounded, scaled[c, h])
            d_qk = d_qk + dot((d_phi * b).astype(bf16), first[2 * h], NT)
            d_qk = d_qk + dot((d_phi * a).astype(bf16), second[2 * h], NT)
        dconv[rows_of(c), 2 * DV : LANES] = d_qk

        @pl.when(c == 0)
        def _():
            later.middle()

        @pl.when(c >= 1)
        def _():
            fwd.forward(c - 1)

    fwd.forward(NCH - 1)
    for copy in spreads[0]:
        copy.wait()
    for copy in relays[0]:
        copy.start()
    later.late()
    later.end()
    state_out[...] = state_out[...] + local_out[...]

    def project_back(c):
        window = dconv[pl.ds(pl.multiple_of(c * CH, CH), CH + 8)]
        mixed = t0 * window[:CH] + (
            t1 * pltpu.roll(window, CH + 7, 0)[:CH] + t2 * pltpu.roll(window, CH + 6, 0)[:CH]
        )
        held_v[0, rows_of(c)] = mixed[:, : 2 * DV].astype(bf16)
        packed = mixed[: CH // 2, 2 * DV :] + pltpu.roll(mixed[CH // 2 :, 2 * DV :], 64, 1)
        held_qk[0, rows_of(c, CH // 2)] = packed.astype(bf16)

    @pl.loop(0, NCH)
    def _(c):
        qk = qk_of(c)
        d_qk = dconv[rows_of(c), 2 * DV : LANES]
        for h in range(HEADS):
            remaining = state_out[h] - grads[c, h]
            state_out[h] = remaining
            suffix = (remaining * scale).astype(bf16)
            dconv[rows_of(c), lanes(h)] = dconv[rows_of(c), lanes(h)] + dot(
                phi_k[h, rows_of(c)], suffix, NT
            )
            a, b = factors(qk, 2 * h + 1)
            d_phi = dot(cv[rows_of(c), lanes(h)], suffix)
            d_qk = d_qk + dot((d_phi * b).astype(bf16), first[2 * h + 1], NT)
            d_qk = d_qk + dot((d_phi * a).astype(bf16), second[2 * h + 1], NT)
        dconv[rows_of(c), 2 * DV : LANES] = d_qk

        @pl.when(c == 0)
        def _():
            behind.start()

        @pl.when(c == 1)
        def _():
            for copy in spreads[1]:
                copy.start()

        @pl.when(c > 0)
        def _():
            project_back(c - 1)

        @pl.when((c == 1) | (c == 2))
        def _():
            bwd.send_own(c - 1)

    behind.wait()
    dconv[pl.ds(NCH * CH, 8)] = halo_out[...] * one_if(place < 7)
    project_back(NCH - 1)

    for copy in relays[0]:
        copy.wait()
    for copy in bwd_swaps[0]:
        copy.start()
    for copy in fwd_swaps + fwd_own + bwd_own + res_loads:
        copy.wait()

    @pl.loop(0, NCH)
    def _(j):
        fwd.compute(j)

    @pl.loop(0, 2)
    def _(j):
        bwd.forward(j)
        bwd.send_own(j + 2)
        fwd.send(j)

    for copy in spreads[1]:
        copy.wait()
    for copy in relays[1]:
        copy.start()
    fwd.send(2)
    fwd.send(3)
    for copy in bwd_swaps[0]:
        copy.wait()

    @pl.loop(0, NCH + 1)
    def _(i):
        @pl.when(i < NCH)
        def _():
            bwd.multiply(i)

        @pl.when(i == 0)
        def _():
            for copy in relays[1]:
                copy.wait()
            for copy in bwd_swaps[1]:
                copy.start()

        @pl.when(i < 2)
        def _():
            bwd.forward(i + 2)

        @pl.when(i == 0)
        def _():
            for copy in bwd_swaps[1]:
                copy.wait()

        @pl.when(i >= 1)
        def _():
            fwd.relayed(i - 1)
            bwd.relayed(i - 1)

    @pl.loop(0, NCH)
    def _(i):
        fwd.finish(i)
        bwd.finish(i)

    @pl.loop(0, NCH)
    def _(c):
        fwd.drain(c)
        bwd.drain(c)

    early.drain()
    later.drain()


def settle_kernel(first, second, first_out, second_out, held, in_sem, out_sem):
    pairs = ((first, first_out), (second, second_out))
    ins = [pltpu.make_async_copy(p[0], held.at[n], in_sem.at[n]) for n, p in enumerate(pairs)]
    outs = [pltpu.make_async_copy(held.at[n], p[1], out_sem.at[n]) for n, p in enumerate(pairs)]
    for copy in ins:
        copy.start()
    for n in range(2):
        ins[n].wait()
        outs[n].start()
    for copy in outs:
        copy.wait()


def settle(first, second):
    whole = pl.BlockSpec(memory_space=pl.ANY)
    result = jax.ShapeDtypeStruct(first.shape, first.dtype)
    dma = pltpu.SemaphoreType.DMA
    return pl.pallas_call(
        settle_kernel,
        out_shape=(result, result),
        in_specs=[whole] * 2,
        out_specs=(whole, whole),
        scratch_shapes=[pltpu.VMEM((2,) + first.shape, first.dtype), dma((2,)), dma((2,))],
    )(first, second)


def per_device(inputs, cotangent, w_in, conv_w, norm_gain, w_out, keep_flags):
    count, width = inputs.shape
    first, second, rows, moves = selectors()
    consts = [jnp.asarray(part, bf16) for part in (first, second, moves)]
    whole, near = pl.BlockSpec(memory_space=pl.ANY), pl.BlockSpec(memory_space=pltpu.VMEM)
    result = jax.ShapeDtypeStruct((count, 256), bf16)
    dma = pltpu.SemaphoreType.DMA
    state = (DV, EXP)
    lump = (160, DV)
    carry_bufs = [pltpu.VMEM((n,) + lump if n > 1 else lump, bf16) for n in (1, 1, 1, 3, 1, 1)]
    carry_sems = [dma((4,)), dma((3,)), dma((3,))]
    results = pl.pallas_call(
        layer_kernel,
        out_shape=(result, result),
        in_specs=[whole] * 7 + [near] * 3 + [pl.BlockSpec(memory_space=pltpu.SMEM)],
        out_specs=(whole, whole),
        scratch_shapes=ring_buffers(count)
        + ring_buffers(count)
        + ring_semaphores()
        + ring_semaphores()
        + [
            pltpu.VMEM((4, count, 256), bf16),
            pltpu.VMEM((4, count, 256), bf16),
            pltpu.VMEM((4, count // 2, 128), bf16),
            pltpu.VMEM((2, 4, 4, 64, 256), bf16),
            pltpu.VMEM((CH, 256), bf16),
            pltpu.VMEM((HEADS, count, CH), bf16),
            pltpu.VMEM((HEADS, count, CH), f32),
            pltpu.VMEM((HEADS, count, 128), bf16),
        ]
        + [dma((3, NCH))] * 6
        + [dma((2, 3, 2))] * 4
        + [dma((2, 4)), dma((2, 2, 4))]
        + [dma((2, 2, 3))] * 2
        + [dma((2, 2, 2))] * 4
        + [dma((2, 2))] * 2
        + carry_bufs
        + carry_bufs
        + carry_sems
        + carry_sems
        + [
            pltpu.VMEM((count, width), bf16),
            pltpu.VMEM((count, width), bf16),
            pltpu.VMEM((LANES, width), bf16),
            pltpu.VMEM((256, width), bf16),
            pltpu.VMEM((count + 8, LANES), f32),
            pltpu.VMEM((count, LANES), bf16),
            pltpu.VMEM((count, 256), f32),
            pltpu.VMEM((count, 256), f32),
            pltpu.VMEM((count, 256), bf16),
            pltpu.VMEM((HEADS, count, EXP), bf16),
            pltpu.VMEM((HEADS, count, EXP), bf16),
            pltpu.VMEM((NCH, HEADS) + state, f32),
            pltpu.VMEM((NCH, HEADS) + state, f32),
            pltpu.VMEM((NCH, HEADS) + state, bf16),
            pltpu.VMEM((HEADS,) + state, f32),
            pltpu.VMEM((HEADS,) + state, f32),
            pltpu.VMEM((HEADS,) + state, f32),
            pltpu.VMEM((HEADS,) + state, f32),
            pltpu.VMEM((8, LANES), f32),
            pltpu.VMEM((8, LANES), f32),
            pltpu.VMEM((4, 128, EXP), bf16),
            pltpu.VMEM((4, 128, EXP), bf16),
            pltpu.VMEM((4, 128, 128), bf16),
            dma((NCH,)),
            dma((NCH,)),
            dma((4,)),
            dma((1,)),
            dma((2,)),
            dma((4,)),
            dma((3,)),
        ],
        compiler_params=pltpu.CompilerParams(
            collective_id=0, has_side_effects=True, vmem_limit_bytes=67043328
        ),
    )(
        inputs,
        cotangent,
        w_in.T,
        w_out,
        *consts,
        conv_w,
        norm_gain.reshape(1, HEADS * DV),
        jnp.asarray(rows),
        keep_flags,
    )
    return settle(*results)


def solution(mesh):
    placed = (
        P("seq", None),
        P("seq", None),
        P(None, "tp"),
        P(None, "tp"),
        P("tp"),
        P("tp", None),
        P("tp"),
    )
    return jax.shard_map(
        per_device,
        mesh=mesh,
        in_specs=placed,
        out_specs=(P("seq", "tp"), P("seq", "tp")),
        check_vma=False,
    )
```

```python
from functools import partial

import jax
import jax.numpy as jnp
import numpy as np
from jax import lax
from jax.experimental import pallas as pl
from jax.experimental.pallas import tpu as pltpu
from jax.sharding import PartitionSpec as P

FEAT = 16
DV = 128
LANES = 384
EXP = 256
HEADS = 2
epsilon = 1e-06

CH = 256
NCH = 4
MESH = pl.DeviceIdType.MESH
NT = (((1,), (1,)), ((), ()))
NN = (((1,), (0,)), ((), ()))
TN = (((0,), (0,)), ((), ()))
f32 = jnp.float32
bf16 = jnp.bfloat16


def neighbour(along, step):
    place = lax.axis_index("tp")
    column, row = lax.rem(place, 4), lax.div(place, 4)
    if along == "x":
        return row * 4 + lax.rem(column + step, 4)
    return lax.rem(row + step, 4) * 4 + column


def block_at(a_along, a_step, r_along, r_step):
    place = lax.axis_index("tp")
    column, row = lax.rem(place, 4), lax.div(place, 4)
    x_step = a_step if a_along == "x" else r_step
    y_step = a_step if a_along == "y" else r_step
    return lax.rem(row + y_step, 4) * 4 + lax.rem(column + x_step, 4)


def to_device(src, dst, send_sem, recv_sem, place):
    return pltpu.make_async_remote_copy(
        src_ref=src,
        dst_ref=dst,
        send_sem=send_sem,
        recv_sem=recv_sem,
        device_id={"tp": place},
        device_id_type=MESH,
    )


def to_seq(src, dst, send_sem, recv_sem, place):
    return pltpu.make_async_remote_copy(
        src_ref=src,
        dst_ref=dst,
        send_sem=send_sem,
        recv_sem=recv_sem,
        device_id={"seq": place},
        device_id_type=MESH,
    )


def dot(a, b, dims=NN):
    return lax.dot_general(a, b, dims, preferred_element_type=f32)


def rows_of(c, size=CH):
    return pl.ds(pl.multiple_of(c * size, size), size)


def way(c):
    return jnp.where(c < NCH // 2, 1, 3)


class Ring:
    def __init__(self, flip, streams, weight, part, landed, relay, keep, res, out, sems):
        self.flip, self.streams, self.weight = flip, streams, weight
        self.part, self.landed, self.relay = part, landed, relay
        self.keep, self.res, self.out = keep, res, out
        (self.ts, self.tr, self.ps, self.pr, self.os) = sems

    def turn(self, c):
        return lax.rem(c + self.flip, 2)

    def gather_to(self, c, d):
        return jnp.where(self.turn(c) == 0, neighbour("x", d), neighbour("y", d))

    def scatter_to(self, c, d):
        return jnp.where(self.turn(c) == 0, neighbour("y", d), neighbour("x", d))

    def direct(self, c, d):
        return [
            to_device(
                held.at[0, rows_of(c, size)],
                held.at[d, rows_of(c, size)],
                send.at[d - 1, c],
                recv.at[d - 1, c],
                self.gather_to(c, d),
            )
            for held, size, send, recv in self.streams
        ]

    def passed_on(self, c):
        return [
            to_device(
                held.at[way(c), rows_of(c, size)],
                held.at[2, rows_of(c, size)],
                send.at[1, c],
                recv.at[1, c],
                self.gather_to(c, way(c)),
            )
            for held, size, send, recv in self.streams
        ]

    def send_own(self, c):
        for d in (1, 3):
            for copy in self.direct(c, d):
                copy.start()

    def forward(self, c):
        for d in (1, 3):
            for copy in self.direct(c, d):
                copy.wait_recv()
        for copy in self.passed_on(c):
            copy.start()

    def tie(self, c):
        return to_device(
            self.part.at[2, rows_of(c)],
            self.relay.at[rows_of(c)],
            self.ts.at[c],
            self.tr.at[c],
            self.scatter_to(c, way(c)),
        )

    def side(self, c, d):
        return to_device(
            self.part.at[d, rows_of(c)],
            self.landed.at[d // 2, rows_of(c)],
            self.ps.at[d // 2, c],
            self.pr.at[d // 2, c],
            self.scatter_to(c, d),
        )

    def prepare(self, c):
        pass

    def product(self, c, k):
        held = self.streams[0][0]
        total = None
        for o in range(4):
            term = dot(held[o, rows_of(c)], self.weight[self.turn(c), k, o])
            total = term if total is None else total + term
        return total

    def compute(self, c):
        for copy in self.passed_on(c):
            copy.wait_recv()
        self.prepare(c)
        near, far = way(c), 4 - way(c)
        self.part[2, rows_of(c)] = self.product(c, 2).astype(bf16)
        self.part[far, rows_of(c)] = self.product(c, far).astype(bf16)
        self.keep[1, rows_of(c)] = self.product(c, near)
        self.keep[0, rows_of(c)] = self.product(c, 0) + self.res[rows_of(c)].astype(f32)

    def send(self, c):
        self.tie(c).start()
        self.side(c, 4 - way(c)).start()

    def multiply(self, c):
        for copy in self.passed_on(c):
            copy.wait_recv()
        self.prepare(c)
        near, far = way(c), 4 - way(c)
        self.part[2, rows_of(c)] = self.product(c, 2).astype(bf16)
        self.tie(c).start()
        self.keep[1, rows_of(c)] = self.product(c, near)
        self.part[far, rows_of(c)] = self.product(c, far).astype(bf16)
        self.side(c, far).start()
        self.keep[0, rows_of(c)] = self.product(c, 0) + self.res[rows_of(c)].astype(f32)

    def relayed(self, c):
        self.tie(c).wait_recv()
        near = way(c)
        total = self.keep[1, rows_of(c)] + self.relay[rows_of(c)].astype(f32)
        self.part[near, rows_of(c)] = total.astype(bf16)
        self.side(c, near).start()

    def finish(self, c):
        self.side(c, 1).wait_recv()
        self.side(c, 3).wait_recv()
        total = self.keep[0, rows_of(c)] + (
            self.landed[0, rows_of(c)].astype(f32) + self.landed[1, rows_of(c)].astype(f32)
        )
        self.part[0, rows_of(c)] = total.astype(bf16)
        self.leave(c).start()

    def leave(self, c):
        return pltpu.make_async_copy(
            self.part.at[0, rows_of(c)], self.out.at[rows_of(c)], self.os.at[c]
        )

    def drain(self, c):
        for copy in self.direct(c, 1) + self.direct(c, 3) + self.passed_on(c):
            copy.wait_send()
        self.tie(c).wait_send()
        self.side(c, 1).wait_send()
        self.side(c, 3).wait_send()
        self.leave(c).wait()


class SplitRing(Ring):
    def prepare(self, c):
        packed = self.streams[1][0]
        low = lax.broadcasted_iota(jnp.int32, (CH // 2, 128), 1) < 64
        for pair in range(2):
            one = packed[2 * pair, rows_of(c, CH // 2)].astype(f32)
            two = packed[2 * pair + 1, rows_of(c, CH // 2)].astype(f32)
            top = jnp.where(low, one, pltpu.roll(two, 64, 1))
            bottom = jnp.where(low, pltpu.roll(one, 64, 1), two)
            lanes = slice(pair * 128, pair * 128 + 128)
            self.flat[0 : CH // 2, lanes] = top.astype(bf16)
            self.flat[CH // 2 : CH, lanes] = bottom.astype(bf16)

    def product(self, c, k):
        return super().product(c, k) + dot(self.flat[...], self.weight_qk[self.turn(c), k].reshape(256, 256))


def ring_semaphores():
    dma = pltpu.SemaphoreType.DMA
    return [dma((NCH,)), dma((NCH,)), dma((2, NCH)), dma((2, NCH)), dma((NCH,))]


def ring_buffers(rows):
    return [
        pltpu.VMEM((2, 4, 4, 256, 256), bf16),
        pltpu.VMEM((4, rows, 256), bf16),
        pltpu.VMEM((2, rows, 256), bf16),
        pltpu.VMEM((rows, 256), bf16),
        pltpu.VMEM((2, rows, 256), f32),
        pltpu.VMEM((rows, 256), bf16),
    ]


def selectors():
    first = np.zeros((4, 128, EXP), np.float32)
    second = np.zeros((4, 128, EXP), np.float32)
    rows = np.zeros((8, EXP), np.float32)
    rows[0, 0] = rows[1, 0] = rows[2, 0] = 1.0
    for group in range(4):
        base = group * FEAT
        for i in range(FEAT):
            first[group, base + i, 1 + i] = 1.0
            rows[1, 1 + i] = 1.0
            rows[2, 1 + i] = 0.25
        e = 1 + FEAT
        for i in range(FEAT):
            for j in range(i, FEAT):
                first[group, base + i, e] = 1.0
                second[group, base + j, e] = 1.0
                rows[2, e] = 1 / 32 if i == j else 1 / 16
                e += 1
    moves = np.zeros((4, 128, 128), np.float32)
    for h in range(HEADS):
        for i in range(FEAT):
            q, k = 2 * h * FEAT + i, (2 * h + 1) * FEAT + i
            moves[2 * h, q, k] = 1.0
            moves[2 * h + 1, k, q] = 1.0
    return first, second, rows, moves


def one_if(condition):
    return jnp.where(condition, 1.0, 0.0).astype(f32)


def packed_state(state):
    rest = state[:32, DV:]
    for g in range(1, 4):
        rest = rest + pltpu.roll(state[32 * g : 32 * g + 32, DV:], 32 * g, 1)
    return jnp.concatenate([state[:, :DV], rest], 0)


def whole_state(packed):
    low = lax.broadcasted_iota(jnp.int32, (32, DV), 1) < 32
    rest = packed[DV:]
    parts = [rest] + [pltpu.roll(rest, DV - 32 * g, 1) for g in range(1, 4)]
    parts = [jnp.where(low, part, 0.0) for part in parts]
    return jnp.concatenate([packed[:DV], jnp.concatenate(parts, 0)], 1)


class Carry:
    def __init__(self, earlier, local, state, bufs, sems):
        self.earlier, self.local, self.state = earlier, local, state
        self.sa, self.ra, self.sb, self.rb, self.sc, self.rc = bufs
        self.pair_sems, self.zs, self.zr = sems
        place = lax.axis_index("seq")
        self.core, self.z = lax.rem(place, 2), lax.div(place, 2)
        self.partner = self.z * 2 + (1 - self.core)

    def swap(self):
        return to_seq(self.sa, self.ra, self.pair_sems.at[0], self.pair_sems.at[1], self.partner)

    def give(self):
        return to_seq(self.sc, self.rc, self.pair_sems.at[2], self.pair_sems.at[3], self.partner)

    def along(self, step):
        there = lax.rem(self.z + step, 4) * 2 + self.core
        return to_seq(
            self.sb, self.rb.at[step - 1], self.zs.at[step - 1], self.zr.at[step - 1], there
        )

    def start(self):
        self.sa[...] = packed_state(self.local[1 - self.core]).astype(bf16)
        self.swap().start()

    def middle(self):
        self.swap().wait_recv()
        self.sb[...] = (packed_state(self.local[self.core]) + self.ra[...].astype(f32)).astype(bf16)
        for step in (1, 2, 3):
            self.along(step).start()

    def late(self):
        total = jnp.zeros(self.sb.shape, f32)
        for step in (1, 2, 3):
            self.along(step).wait_recv()
            counts = one_if(self.z >= step if self.earlier else self.z < step)
            total = total + self.rb[step - 1].astype(f32) * counts
        takes = self.core if self.earlier else 1 - self.core
        own = packed_state(self.local[self.core]) * one_if(takes == 0)
        self.sc[...] = (total + own).astype(bf16)
        self.give().start()
        self.state[self.core] = whole_state(total + self.ra[...].astype(f32) * one_if(takes == 1))

    def end(self):
        self.give().wait_recv()
        self.state[1 - self.core] = whole_state(self.rc[...].astype(f32))

    def drain(self):
        self.swap().wait_send()
        self.give().wait_send()
        for step in (1, 2, 3):
            self.along(step).wait_send()


def layer_kernel(
    inputs, cotangent, w_t, w_out, first_any, second_any, moves_any, conv, gains, rows, keep,
    layer_out, input_grad, *scratch,
):
    take = list(scratch)

    def pop(n):
        got = take[:n]
        del take[:n]
        return got

    fwd_bufs, bwd_bufs = pop(6), pop(6)
    fwd_sems, bwd_sems = pop(5), pop(5)
    (held_h, held_v, held_qk, weight_qk, flat, saved_w, saved_l, moved_q) = pop(8)
    (gs_h, gr_h, gs_v, gr_v, gs_q, gr_q) = pop(6)
    (ws, wr, us, ur, w_own, q_own) = pop(6)
    (fs, fr, zcs, zcr, rys, ryr, ss, sr) = pop(8)
    early_bufs, late_bufs = pop(6), pop(6)
    early_sems, late_sems = pop(3), pop(3)
    (xin, cot, weights_t, weights_o) = pop(4)
    (pp, cv, mix, gh, dn, phi_q, phi_k, states, grads, scaled) = pop(10)
    dconv = pp
    (state_in, state_out, local_in, local_out, halo_in, halo_out) = pop(6)
    (first, second, moves) = pop(3)
    (x_sem, c_sem, w_sem, o_sem, r_sem, h_sem, k_sem) = pop(7)

    tp, place = lax.axis_index("tp"), lax.axis_index("seq")

    core, z = lax.rem(place, 2), lax.div(place, 2)
    fwd = Ring(1, [(held_h, CH, gs_h, gr_h)], *fwd_bufs, layer_out, fwd_sems)
    streams = [(held_v, CH, gs_v, gr_v), (held_qk, CH // 2, gs_q, gr_q)]
    bwd = SplitRing(0, streams, *bwd_bufs, input_grad, bwd_sems)
    bwd.flat, bwd.weight_qk = flat, weight_qk
    early = Carry(True, local_in, state_in, early_bufs, early_sems)
    later = Carry(False, local_out, state_out, late_bufs, late_sems)
    heads = held_h.at[0]

    def columns(t):
        return pl.ds(pl.multiple_of(t * 256, 256), 256)

    def out_block(t):
        return w_out.at[:, columns(t)]

    def swap_device():
        return place + 1 - 2 * core

    sides = ((bwd.weight, 128, 0), (weight_qk, 32, 256))
    fwd_weights, fwd_swaps, fwd_own, bwd_own = [], [], [], []
    bwd_weights, spreads, relays, bwd_swaps = [], ([], []), ([], []), ([], [])
    for p, (a, r) in enumerate((("x", "y"), ("y", "x"))):
        for d in (1, 2, 3):
            for j in range(2):
                k = core * 2 + j
                block = fwd.weight.at[p, k, d]
                at = (p, d - 1, j)
                wanted = out_block(block_at(a, d, r, k))
                fwd_weights.append(to_device(wanted, block, ws.at[at], wr.at[at], neighbour(a, d)))
                fwd_swaps.append(to_seq(block, block, us.at[at], ur.at[at], swap_device()))
        for n, (array, size, start) in enumerate(sides):
            half = rows_of(core, size)
            theirs = pl.ds(pl.multiple_of(start + core * size, size), size)
            for d in (1, 2, 3):
                at = (p, n, d - 1)
                wanted = weights_t.at[theirs, columns(block_at(a, d, r, z))]
                bwd_weights.append(
                    to_device(wanted, array.at[p, z, d, half], fs.at[at], fr.at[at], neighbour(a, d))
                )
            for n_way, step in enumerate((1, 3)):
                at = (p, n, n_way)
                there = lax.rem(z + step, 4) * 2 + core
                mine = array.at[p, z, pl.ds(1, 3), half]
                spreads[p].append(to_seq(mine, mine, zcs.at[at], zcr.at[at], there))
                near = lax.rem(z + 4 - step, 4)
                rows_in = pl.ds(
                    pl.multiple_of(core * size + n_way * (size // 2), size // 2), size // 2
                )
                passing = array.at[p, near, pl.ds(1, 3), rows_in]
                relays[p].append(to_seq(passing, passing, rys.at[at], ryr.at[at], there))
            ours = array.at[p, :, pl.ds(1, 3), half]
            bwd_swaps[p].append(to_seq(ours, ours, ss.at[p, n], sr.at[p, n], swap_device()))
        for k in range(4):
            t = block_at(a, 0, r, k)
            fwd_own.append(
                pltpu.make_async_copy(out_block(t), fwd.weight.at[p, k, 0], w_own.at[p, k])
            )
            for n, (array, size, start) in enumerate(sides):
                wanted = weights_t.at[pl.ds(start, 2 * size), columns(t)]
                bwd_own.append(
                    pltpu.make_async_copy(wanted, array.at[p, k, 0], q_own.at[p, n, k])
                )

    pieces = ((32, 128, 0), (192, 128, 128), (0, 32, 256), (160, 32, 288))
    w_loads = [
        pltpu.make_async_copy(
            w_t.at[pl.ds(src, size)], weights_t.at[pl.ds(dst, size)], w_sem.at[n]
        )
        for n, (src, size, dst) in enumerate(pieces)
    ]
    for copy in w_loads:
        copy.start()

    def x_load(c):
        return pltpu.make_async_copy(inputs.at[rows_of(c)], xin.at[rows_of(c)], x_sem.at[c])

    def c_load(c):
        return pltpu.make_async_copy(cotangent.at[rows_of(c)], cot.at[rows_of(c)], c_sem.at[c])

    x_load(3).start()
    barrier = pltpu.get_barrier_semaphore()
    for d in (1, 2, 3):
        for along in ("x", "y"):
            pl.semaphore_signal(
                barrier, inc=1, device_id={"tp": neighbour(along, d)}, device_id_type=MESH
            )
    for d in (1, 2, 4, 6, 7):
        pl.semaphore_signal(
            barrier, inc=1, device_id={"seq": lax.rem(place + d, 8)}, device_id_type=MESH
        )
    weights_t[pl.ds(320, 64)] = jnp.zeros((64, weights_t.shape[1]), bf16)
    const_loads = [
        pltpu.make_async_copy(src, dst, k_sem.at[n])
        for n, (src, dst) in enumerate(
            ((first_any, first), (second_any, second), (moves_any, moves))
        )
    ]
    o_load = pltpu.make_async_copy(w_out, weights_o, o_sem.at[0])
    res_loads = [
        pltpu.make_async_copy(inputs.at[:, columns(tp)], fwd.res, r_sem.at[0]),
        pltpu.make_async_copy(cotangent.at[:, columns(tp)], bwd.res, r_sem.at[1]),
    ]
    src = lax.broadcasted_iota(jnp.int32, (320, LANES), 0)
    dst = lax.broadcasted_iota(jnp.int32, (320, LANES), 1)
    from_high = jnp.where(dst < 288, dst - 256, jnp.where(dst < 320, dst - 128, -1))
    source = jnp.where(dst < 128, dst + 32, jnp.where(dst < 256, dst + 64, from_high))
    taps = lax.dot_general(
        conv[...],
        jnp.where(src == source, 1.0, 0.0).astype(f32),
        NN,
        precision=lax.Precision.HIGHEST,
        preferred_element_type=f32,
    )
    lane = lax.broadcasted_iota(jnp.int32, (1, HEADS * DV), 1)
    gain = gains[...] * jnp.where(lane < DV, keep[0].astype(f32), keep[1].astype(f32))

    for copy in w_loads:
        copy.wait()
    for c in (0, 1, 2):
        x_load(c).start()
    for copy in const_loads + [o_load] + res_loads + fwd_own + bwd_own:
        copy.start()

    ahead = to_seq(
        pp.at[pl.ds(NCH * CH, 8)], halo_in, h_sem.at[0], h_sem.at[1], lax.rem(place + 1, 8)
    )
    behind = to_seq(
        dconv.at[pl.ds(0, 8)], halo_out, h_sem.at[2], h_sem.at[3], lax.rem(place + 7, 8)
    )

    @pl.loop(0, NCH)
    def _(i):
        c = lax.rem(i + NCH - 1, NCH)
        x_load(c).wait()
        c_load(c).start()
        projected = dot(xin[rows_of(c)], weights_t[...], NT).astype(bf16).astype(f32)
        pp[pl.ds(pl.multiple_of(c * CH + 8, 8), CH)] = projected

        @pl.when(i == 0)
        def _():
            pl.semaphore_wait(barrier, 11)
            ahead.start()
            for copy in bwd_weights + fwd_weights:
                copy.start()

    for copy in const_loads:
        copy.wait()
    ahead.wait()
    pp[pl.ds(0, 8)] = halo_in[...] * one_if(place > 0)

    t0, t1, t2 = taps[0:1], taps[1:2], taps[2:3]
    bias_a, bias_b, scale = rows[0:1], rows[1:2], rows[2:3]

    def factors(qk, group):
        return dot(qk, first[group]) + bias_a, dot(qk, second[group]) + bias_b

    def lanes(h):
        return slice(h * DV, (h + 1) * DV)

    def qk_of(c):
        return cv[rows_of(c), 2 * DV : LANES]

    local_in[...] = jnp.zeros(local_in.shape, f32)

    @pl.loop(0, NCH)
    def _(c):
        window = pp[pl.ds(pl.multiple_of(c * CH, CH), CH + 8)]
        mixed = t0 * window[8:] + (
            t1 * pltpu.roll(window, 1, 0)[8:] + t2 * pltpu.roll(window, 2, 0)[8:]
        )
        cv[rows_of(c)] = mixed.astype(bf16)
        qk = qk_of(c)
        for h in range(HEADS):
            a, b = factors(qk, 2 * h + 1)
            features = (a * b).astype(bf16)
            phi_k[h, rows_of(c)] = features
            local = dot(cv[rows_of(c), lanes(h)], features, TN)
            states[c, h] = local
            local_in[h] = local_in[h] + local

    early.start()

    causal = lax.broadcasted_iota(jnp.int32, (CH, CH), 0) >= lax.broadcasted_iota(
        jnp.int32, (CH, CH), 1
    )

    @pl.loop(0, NCH)
    def _(c):
        qk = qk_of(c)
        for h in range(HEADS):
            moved = dot(qk, moves[2 * h]).astype(bf16)
            moved_q[h, rows_of(c)] = moved
            logits = dot(moved, qk, NT) * 0.25
            weight = jnp.where(causal, 1.0 + logits + 0.5 * logits * logits, 0.0).astype(bf16)
            saved_w[h, rows_of(c)] = weight
            saved_l[h, rows_of(c)] = jnp.where(causal, 0.25 + 0.25 * logits, 0.0)
            mix[rows_of(c), lanes(h)] = dot(weight, cv[rows_of(c), lanes(h)])

        @pl.when(c == 1)
        def _():
            early.middle()

    o_load.wait()

    @pl.loop(0, NCH)
    def _(c):
        c_load(c).wait()
        gh[rows_of(c)] = dot(cot[rows_of(c)], weights_o[...], NT) * gain

    @pl.loop(0, NCH)
    def _(c):
        qk = qk_of(c)
        for h in range(HEADS):
            a, b = factors(qk, 2 * h)
            phi_q[h, rows_of(c)] = (a * b).astype(bf16)

    early.late()
    for copy in bwd_weights:
        copy.wait()
    for copy in spreads[0]:
        copy.start()
    early.end()
    local_out[...] = jnp.zeros(local_out.shape, f32)

    @pl.loop(0, NCH)
    def _(c):
        for h in range(HEADS):
            entering = state_in[h]
            state_in[h] = entering + states[c, h]
            scaled[c, h] = (entering * scale).astype(bf16)
            numerator = mix[rows_of(c), lanes(h)] + dot(phi_q[h, rows_of(c)], scaled[c, h], NT)
            inverse = lax.rsqrt(jnp.mean(numerator * numerator, -1, keepdims=True) + epsilon)
            normed = numerator * inverse
            heads[rows_of(c), lanes(h)] = (normed * gain[:, lanes(h)]).astype(bf16)
            grad = gh[rows_of(c), lanes(h)]
            d_numer = (grad - normed * jnp.mean(grad * normed, -1, keepdims=True)) * inverse
            rounded = d_numer.astype(bf16)
            dn[rows_of(c), lanes(h)] = rounded
            local = dot(rounded, phi_q[h, rows_of(c)], TN)
            grads[c, h] = local
            local_out[h] = local_out[h] + local
        fwd.send_own(c)

    later.start()
    for copy in fwd_weights:
        copy.wait()
    for copy in fwd_swaps:
        copy.start()

    @pl.loop(0, NCH)
    def _(c):
        qk = qk_of(c)
        d_qk = jnp.zeros((CH, 128), f32)
        for h in range(HEADS):
            rounded = dn[rows_of(c), lanes(h)]
            dconv[rows_of(c), lanes(h)] = dot(saved_w[h, rows_of(c)], rounded, TN)
            d_weight = dot(rounded, cv[rows_of(c), lanes(h)], NT)
            d_logits = (d_weight * saved_l[h, rows_of(c)]).astype(bf16)
            d_qk = d_qk + dot(d_logits, dot(qk, moves[2 * h + 1]).astype(bf16))
            d_qk = d_qk + dot(d_logits, moved_q[h, rows_of(c)], TN)
            a, b = factors(qk, 2 * h)
            d_phi = dot(rounded, scaled[c, h])
            d_qk = d_qk + dot((d_phi * b).astype(bf16), first[2 * h], NT)
            d_qk = d_qk + dot((d_phi * a).astype(bf16), second[2 * h], NT)
        dconv[rows_of(c), 2 * DV : LANES] = d_qk

        @pl.when(c == 0)
        def _():
            later.middle()

        @pl.when(c >= 1)
        def _():
            fwd.forward(c - 1)

    fwd.forward(NCH - 1)
    for copy in spreads[0]:
        copy.wait()
    for copy in relays[0]:
        copy.start()
    later.late()
    later.end()
    state_out[...] = state_out[...] + local_out[...]

    def project_back(c):
        window = dconv[pl.ds(pl.multiple_of(c * CH, CH), CH + 8)]
        mixed = t0 * window[:CH] + (
            t1 * pltpu.roll(window, CH + 7, 0)[:CH] + t2 * pltpu.roll(window, CH + 6, 0)[:CH]
        )
        held_v[0, rows_of(c)] = mixed[:, : 2 * DV].astype(bf16)
        packed = mixed[: CH // 2, 2 * DV :] + pltpu.roll(mixed[CH // 2 :, 2 * DV :], 64, 1)
        held_qk[0, rows_of(c, CH // 2)] = packed.astype(bf16)

    @pl.loop(0, NCH)
    def _(c):
        qk = qk_of(c)
        d_qk = dconv[rows_of(c), 2 * DV : LANES]
        for h in range(HEADS):
            remaining = state_out[h] - grads[c, h]
            state_out[h] = remaining
            suffix = (remaining * scale).astype(bf16)
            dconv[rows_of(c), lanes(h)] = dconv[rows_of(c), lanes(h)] + dot(
                phi_k[h, rows_of(c)], suffix, NT
            )
            a, b = factors(qk, 2 * h + 1)
            d_phi = dot(cv[rows_of(c), lanes(h)], suffix)
            d_qk = d_qk + dot((d_phi * b).astype(bf16), first[2 * h + 1], NT)
            d_qk = d_qk + dot((d_phi * a).astype(bf16), second[2 * h + 1], NT)
        dconv[rows_of(c), 2 * DV : LANES] = d_qk

        @pl.when(c == 0)
        def _():
            behind.start()

        @pl.when(c == 1)
        def _():
            for copy in spreads[1]:
                copy.start()

        @pl.when(c > 0)
        def _():
            project_back(c - 1)

        @pl.when(c > 0)
        def _():
            bwd.send_own(c - 1)

    behind.wait()
    dconv[pl.ds(NCH * CH, 8)] = halo_out[...] * one_if(place < 7)
    project_back(NCH - 1)
    bwd.send_own(NCH - 1)

    for copy in fwd_swaps + fwd_own + bwd_own + res_loads:
        copy.wait()

    @pl.loop(0, NCH)
    def _(j):
        fwd.compute(j)

    @pl.loop(0, NCH)
    def _(j):
        bwd.forward(j)
        fwd.send(j)

        @pl.when(j == 1)
        def _():
            for copy in relays[0] + spreads[1]:
                copy.wait()
            for copy in bwd_swaps[0] + relays[1]:
                copy.start()

    for copy in bwd_swaps[0] + relays[1]:
        copy.wait()
    for copy in bwd_swaps[1]:
        copy.start()

    @pl.loop(0, NCH + 3)
    def _(i):
        @pl.when(i < NCH)
        def _():
            bwd.multiply(i)

        @pl.when(i == 0)
        def _():
            for copy in bwd_swaps[1]:
                copy.wait()

        @pl.when((i >= 1) & (i < NCH + 1))
        def _():
            fwd.relayed(i - 1)

        @pl.when(i >= 3)
        def _():
            bwd.relayed(i - 3)

    @pl.loop(0, NCH)
    def _(i):
        fwd.finish(i)
        bwd.finish(i)

    @pl.loop(0, NCH)
    def _(c):
        fwd.drain(c)
        bwd.drain(c)

    early.drain()
    later.drain()


def settle_kernel(first, second, first_out, second_out, held, in_sem, out_sem):
    pairs = ((first, first_out), (second, second_out))
    ins = [pltpu.make_async_copy(p[0], held.at[n], in_sem.at[n]) for n, p in enumerate(pairs)]
    outs = [pltpu.make_async_copy(held.at[n], p[1], out_sem.at[n]) for n, p in enumerate(pairs)]
    for copy in ins:
        copy.start()
    for n in range(2):
        ins[n].wait()
        outs[n].start()
    for copy in outs:
        copy.wait()


def settle(first, second):
    whole = pl.BlockSpec(memory_space=pl.ANY)
    result = jax.ShapeDtypeStruct(first.shape, first.dtype)
    dma = pltpu.SemaphoreType.DMA
    return pl.pallas_call(
        settle_kernel,
        out_shape=(result, result),
        in_specs=[whole] * 2,
        out_specs=(whole, whole),
        scratch_shapes=[pltpu.VMEM((2,) + first.shape, first.dtype), dma((2,)), dma((2,))],
    )(first, second)


def per_device(inputs, cotangent, w_in, conv_w, norm_gain, w_out, keep_flags):
    count, width = inputs.shape
    first, second, rows, moves = selectors()
    consts = [jnp.asarray(part, bf16) for part in (first, second, moves)]
    whole, near = pl.BlockSpec(memory_space=pl.ANY), pl.BlockSpec(memory_space=pltpu.VMEM)
    result = jax.ShapeDtypeStruct((count, 256), bf16)
    dma = pltpu.SemaphoreType.DMA
    state = (DV, EXP)
    lump = (160, DV)
    carry_bufs = [pltpu.VMEM((n,) + lump if n > 1 else lump, bf16) for n in (1, 1, 1, 3, 1, 1)]
    carry_sems = [dma((4,)), dma((3,)), dma((3,))]
    results = pl.pallas_call(
        layer_kernel,
        out_shape=(result, result),
        in_specs=[whole] * 7 + [near] * 3 + [pl.BlockSpec(memory_space=pltpu.SMEM)],
        out_specs=(whole, whole),
        scratch_shapes=ring_buffers(count)
        + ring_buffers(count)
        + ring_semaphores()
        + ring_semaphores()
        + [
            pltpu.VMEM((4, count, 256), bf16),
            pltpu.VMEM((4, count, 256), bf16),
            pltpu.VMEM((4, count // 2, 128), bf16),
            pltpu.VMEM((2, 4, 4, 64, 256), bf16),
            pltpu.VMEM((CH, 256), bf16),
            pltpu.VMEM((HEADS, count, CH), bf16),
            pltpu.VMEM((HEADS, count, CH), f32),
            pltpu.VMEM((HEADS, count, 128), bf16),
        ]
        + [dma((3, NCH))] * 6
        + [dma((2, 3, 2))] * 4
        + [dma((2, 4)), dma((2, 2, 4))]
        + [dma((2, 2, 3))] * 2
        + [dma((2, 2, 2))] * 4
        + [dma((2, 2))] * 2
        + carry_bufs
        + carry_bufs
        + carry_sems
        + carry_sems
        + [
            pltpu.VMEM((count, width), bf16),
            pltpu.VMEM((count, width), bf16),
            pltpu.VMEM((LANES, width), bf16),
            pltpu.VMEM((256, width), bf16),
            pltpu.VMEM((count + 8, LANES), f32),
            pltpu.VMEM((count, LANES), bf16),
            pltpu.VMEM((count, 256), f32),
            pltpu.VMEM((count, 256), f32),
            pltpu.VMEM((count, 256), bf16),
            pltpu.VMEM((HEADS, count, EXP), bf16),
            pltpu.VMEM((HEADS, count, EXP), bf16),
            pltpu.VMEM((NCH, HEADS) + state, f32),
            pltpu.VMEM((NCH, HEADS) + state, f32),
            pltpu.VMEM((NCH, HEADS) + state, bf16),
            pltpu.VMEM((HEADS,) + state, f32),
            pltpu.VMEM((HEADS,) + state, f32),
            pltpu.VMEM((HEADS,) + state, f32),
            pltpu.VMEM((HEADS,) + state, f32),
            pltpu.VMEM((8, LANES), f32),
            pltpu.VMEM((8, LANES), f32),
            pltpu.VMEM((4, 128, EXP), bf16),
            pltpu.VMEM((4, 128, EXP), bf16),
            pltpu.VMEM((4, 128, 128), bf16),
            dma((NCH,)),
            dma((NCH,)),
            dma((4,)),
            dma((1,)),
            dma((2,)),
            dma((4,)),
            dma((3,)),
        ],
        compiler_params=pltpu.CompilerParams(
            collective_id=0, has_side_effects=True, vmem_limit_bytes=67043328
        ),
    )(
        inputs,
        cotangent,
        w_in.T,
        w_out,
        *consts,
        conv_w,
        norm_gain.reshape(1, HEADS * DV),
        jnp.asarray(rows),
        keep_flags,
    )
    return settle(*results)


def solution(mesh):
    placed = (
        P("seq", None),
        P("seq", None),
        P(None, "tp"),
        P(None, "tp"),
        P("tp"),
        P("tp", None),
        P("tp"),
    )
    return jax.shard_map(
        per_device,
        mesh=mesh,
        in_specs=placed,
        out_specs=(P("seq", "tp"), P("seq", "tp")),
        check_vma=False,
    )
```

```python
from functools import partial

import jax
import jax.numpy as jnp
import numpy as np
from jax import lax
from jax.experimental import pallas as pl
from jax.experimental.pallas import tpu as pltpu
from jax.sharding import PartitionSpec as P

FEAT = 16
DV = 128
LANES = 384
EXP = 256
HEADS = 2
epsilon = 1e-06

CH = 256
NCH = 4
MESH = pl.DeviceIdType.MESH
NT = (((1,), (1,)), ((), ()))
NN = (((1,), (0,)), ((), ()))
TN = (((0,), (0,)), ((), ()))
f32 = jnp.float32
bf16 = jnp.bfloat16


def neighbour(along, step):
    place = lax.axis_index("tp")
    column, row = lax.rem(place, 4), lax.div(place, 4)
    if along == "x":
        return row * 4 + lax.rem(column + step, 4)
    return lax.rem(row + step, 4) * 4 + column


def block_at(a_along, a_step, r_along, r_step):
    place = lax.axis_index("tp")
    column, row = lax.rem(place, 4), lax.div(place, 4)
    x_step = a_step if a_along == "x" else r_step
    y_step = a_step if a_along == "y" else r_step
    return lax.rem(row + y_step, 4) * 4 + lax.rem(column + x_step, 4)


def to_device(src, dst, send_sem, recv_sem, place):
    return pltpu.make_async_remote_copy(
        src_ref=src,
        dst_ref=dst,
        send_sem=send_sem,
        recv_sem=recv_sem,
        device_id={"tp": place},
        device_id_type=MESH,
    )


def to_seq(src, dst, send_sem, recv_sem, place):
    return pltpu.make_async_remote_copy(
        src_ref=src,
        dst_ref=dst,
        send_sem=send_sem,
        recv_sem=recv_sem,
        device_id={"seq": place},
        device_id_type=MESH,
    )


def dot(a, b, dims=NN):
    return lax.dot_general(a, b, dims, preferred_element_type=f32)


def rows_of(c, size=CH):
    return pl.ds(pl.multiple_of(c * size, size), size)


def way(c):
    return jnp.where(c < NCH // 2, 1, 3)


class Ring:
    def __init__(self, flip, streams, weight, part, landed, relay, keep, res, out, sems):
        self.flip, self.streams, self.weight = flip, streams, weight
        self.part, self.landed, self.relay = part, landed, relay
        self.keep, self.res, self.out = keep, res, out
        (self.ps, self.tr, self.pr, self.os) = sems

    def turn(self, c):
        return lax.rem(c + self.flip, 2)

    def gather_to(self, c, d):
        return jnp.where(self.turn(c) == 0, neighbour("x", d), neighbour("y", d))

    def scatter_to(self, c, d):
        return jnp.where(self.turn(c) == 0, neighbour("y", d), neighbour("x", d))

    def direct(self, c, d):
        return [
            to_device(
                held.at[0, rows_of(c, size)],
                held.at[d, rows_of(c, size)],
                send.at[0],
                recv.at[d - 1, c],
                self.gather_to(c, d),
            )
            for held, size, send, recv in self.streams
        ]

    def passed_on(self, c):
        return [
            to_device(
                held.at[way(c), rows_of(c, size)],
                held.at[2, rows_of(c, size)],
                send.at[0],
                recv.at[1, c],
                self.gather_to(c, way(c)),
            )
            for held, size, send, recv in self.streams
        ]

    def send_own(self, c):
        for d in (1, 3):
            for copy in self.direct(c, d):
                copy.start()

    def forward(self, c):
        for d in (1, 3):
            for copy in self.direct(c, d):
                copy.wait_recv()
        for copy in self.passed_on(c):
            copy.start()

    def tie(self, c):
        return to_device(
            self.part.at[2, rows_of(c)],
            self.relay.at[rows_of(c)],
            self.ps.at[0],
            self.tr.at[c],
            self.scatter_to(c, way(c)),
        )

    def side(self, c, d):
        return to_device(
            self.part.at[d, rows_of(c)],
            self.landed.at[d // 2, rows_of(c)],
            self.ps.at[0],
            self.pr.at[d // 2, c],
            self.scatter_to(c, d),
        )

    def prepare(self, c):
        pass

    def product(self, c, k):
        held = self.streams[0][0]
        total = None
        for o in range(4):
            term = dot(held[o, rows_of(c)], self.weight[self.turn(c), k, o])
            total = term if total is None else total + term
        return total

    def compute(self, c):
        for copy in self.passed_on(c):
            copy.wait_recv()
        self.prepare(c)
        near, far = way(c), 4 - way(c)
        self.part[2, rows_of(c)] = self.product(c, 2).astype(bf16)
        self.part[far, rows_of(c)] = self.product(c, far).astype(bf16)
        self.keep[1, rows_of(c)] = self.product(c, near)
        self.keep[0, rows_of(c)] = self.product(c, 0) + self.res[rows_of(c)].astype(f32)

    def send(self, c):
        self.tie(c).start()
        self.side(c, 4 - way(c)).start()

    def multiply(self, c):
        for copy in self.passed_on(c):
            copy.wait_recv()
        self.prepare(c)
        near, far = way(c), 4 - way(c)
        self.part[2, rows_of(c)] = self.product(c, 2).astype(bf16)
        self.tie(c).start()
        self.keep[1, rows_of(c)] = self.product(c, near)
        self.part[far, rows_of(c)] = self.product(c, far).astype(bf16)
        self.side(c, far).start()
        self.keep[0, rows_of(c)] = self.product(c, 0) + self.res[rows_of(c)].astype(f32)

    def relayed(self, c):
        self.tie(c).wait_recv()
        near = way(c)
        total = self.keep[1, rows_of(c)] + self.relay[rows_of(c)].astype(f32)
        self.part[near, rows_of(c)] = total.astype(bf16)
        self.side(c, near).start()

    def finish(self, c):
        self.side(c, 1).wait_recv()
        self.side(c, 3).wait_recv()
        total = self.keep[0, rows_of(c)] + (
            self.landed[0, rows_of(c)].astype(f32) + self.landed[1, rows_of(c)].astype(f32)
        )
        self.part[0, rows_of(c)] = total.astype(bf16)
        self.leave(c).start()

    def leave(self, c):
        return pltpu.make_async_copy(
            self.part.at[0, rows_of(c)], self.out.at[rows_of(c)], self.os.at[0]
        )

    def drain(self):
        for held, _, send, recv in self.streams:
            sent = held.at[pl.ds(1, 3)]
            to_device(sent, sent, send.at[0], recv.at[0, 0], self.gather_to(0, 1)).wait_send()
        sent = self.part.at[pl.ds(1, 3)]
        to_device(sent, sent, self.ps.at[0], self.tr.at[0], self.scatter_to(0, 1)).wait_send()
        pltpu.make_async_copy(self.part.at[0], self.out, self.os.at[0]).wait()


class SplitRing(Ring):
    def prepare(self, c):
        packed = self.streams[1][0]
        low = lax.broadcasted_iota(jnp.int32, (CH // 2, 128), 1) < 64
        for pair in range(2):
            one = packed[2 * pair, rows_of(c, CH // 2)].astype(f32)
            two = packed[2 * pair + 1, rows_of(c, CH // 2)].astype(f32)
            top = jnp.where(low, one, pltpu.roll(two, 64, 1))
            bottom = jnp.where(low, pltpu.roll(one, 64, 1), two)
            lanes = slice(pair * 128, pair * 128 + 128)
            self.flat[0 : CH // 2, lanes] = top.astype(bf16)
            self.flat[CH // 2 : CH, lanes] = bottom.astype(bf16)

    def product(self, c, k):
        return super().product(c, k) + dot(self.flat[...], self.weight_qk[self.turn(c), k].reshape(256, 256))


def ring_semaphores():
    dma = pltpu.SemaphoreType.DMA
    return [dma((1,)), dma((NCH,)), dma((2, NCH)), dma((1,))]


def ring_buffers(rows):
    return [
        pltpu.VMEM((2, 4, 4, 256, 256), bf16),
        pltpu.VMEM((4, rows, 256), bf16),
        pltpu.VMEM((2, rows, 256), bf16),
        pltpu.VMEM((rows, 256), bf16),
        pltpu.VMEM((2, rows, 256), f32),
        pltpu.VMEM((rows, 256), bf16),
    ]


def selectors():
    first = np.zeros((4, 128, EXP), np.float32)
    second = np.zeros((4, 128, EXP), np.float32)
    rows = np.zeros((8, EXP), np.float32)
    rows[0, 0] = rows[1, 0] = rows[2, 0] = 1.0
    for group in range(4):
        base = group * FEAT
        for i in range(FEAT):
            first[group, base + i, 1 + i] = 1.0
            rows[1, 1 + i] = 1.0
            rows[2, 1 + i] = 0.25
        e = 1 + FEAT
        for i in range(FEAT):
            for j in range(i, FEAT):
                first[group, base + i, e] = 1.0
                second[group, base + j, e] = 1.0
                rows[2, e] = 1 / 32 if i == j else 1 / 16
                e += 1
    moves = np.zeros((4, 128, 128), np.float32)
    for h in range(HEADS):
        for i in range(FEAT):
            q, k = 2 * h * FEAT + i, (2 * h + 1) * FEAT + i
            moves[2 * h, q, k] = 1.0
            moves[2 * h + 1, k, q] = 1.0
    return first, second, rows, moves


def one_if(condition):
    return jnp.where(condition, 1.0, 0.0).astype(f32)


def packed_state(state):
    rest = state[:32, DV:]
    for g in range(1, 4):
        rest = rest + pltpu.roll(state[32 * g : 32 * g + 32, DV:], 32 * g, 1)
    return jnp.concatenate([state[:, :DV], rest], 0)


def whole_state(packed):
    low = lax.broadcasted_iota(jnp.int32, (32, DV), 1) < 32
    rest = packed[DV:]
    parts = [rest] + [pltpu.roll(rest, DV - 32 * g, 1) for g in range(1, 4)]
    parts = [jnp.where(low, part, 0.0) for part in parts]
    return jnp.concatenate([packed[:DV], jnp.concatenate(parts, 0)], 1)


class Carry:
    def __init__(self, earlier, local, state, bufs, sems):
        self.earlier, self.local, self.state = earlier, local, state
        self.sa, self.ra, self.sb, self.rb, self.sc, self.rc = bufs
        self.pair_sems, self.zs, self.zr = sems
        place = lax.axis_index("seq")
        self.core, self.z = lax.rem(place, 2), lax.div(place, 2)
        self.partner = self.z * 2 + (1 - self.core)

    def swap(self):
        return to_seq(self.sa, self.ra, self.pair_sems.at[0], self.pair_sems.at[1], self.partner)

    def give(self):
        return to_seq(self.sc, self.rc, self.pair_sems.at[2], self.pair_sems.at[3], self.partner)

    def along(self, step):
        there = lax.rem(self.z + step, 4) * 2 + self.core
        return to_seq(
            self.sb, self.rb.at[step - 1], self.zs.at[step - 1], self.zr.at[step - 1], there
        )

    def start(self):
        self.sa[...] = packed_state(self.local[1 - self.core]).astype(bf16)
        self.swap().start()

    def middle(self):
        self.swap().wait_recv()
        self.sb[...] = (packed_state(self.local[self.core]) + self.ra[...].astype(f32)).astype(bf16)
        for step in (1, 2, 3):
            self.along(step).start()

    def late(self):
        total = jnp.zeros(self.sb.shape, f32)
        for step in (1, 2, 3):
            self.along(step).wait_recv()
            counts = one_if(self.z >= step if self.earlier else self.z < step)
            total = total + self.rb[step - 1].astype(f32) * counts
        takes = self.core if self.earlier else 1 - self.core
        own = packed_state(self.local[self.core]) * one_if(takes == 0)
        self.sc[...] = (total + own).astype(bf16)
        self.give().start()
        self.state[self.core] = whole_state(total + self.ra[...].astype(f32) * one_if(takes == 1))

    def end(self):
        self.give().wait_recv()
        self.state[1 - self.core] = whole_state(self.rc[...].astype(f32))

    def drain(self):
        self.swap().wait_send()
        self.give().wait_send()
        for step in (1, 2, 3):
            self.along(step).wait_send()


def layer_kernel(
    inputs, cotangent, w_t, w_out, first_any, second_any, moves_any, conv, gains, rows, keep,
    layer_out, input_grad, *scratch,
):
    take = list(scratch)

    def pop(n):
        got = take[:n]
        del take[:n]
        return got

    fwd_bufs, bwd_bufs = pop(6), pop(6)
    fwd_sems, bwd_sems = pop(4), pop(4)
    (held_h, held_v, held_qk, weight_qk, flat, saved_w, saved_l, moved_q) = pop(8)
    (gs_h, gr_h, gs_v, gr_v, gs_q, gr_q) = pop(6)
    (ws, wr, us, ur, w_own, q_own) = pop(6)
    (fs, fr, zcs, zcr, rys, ryr, ss, sr) = pop(8)
    early_bufs, late_bufs = pop(6), pop(6)
    early_sems, late_sems = pop(3), pop(3)
    (xin, cot, weights_t, weights_o) = pop(4)
    (pp, cv, mix, gh, dn, phi_q, phi_k, states, grads, scaled) = pop(10)
    dconv = pp
    (state_in, state_out, local_in, local_out, halo_in, halo_out) = pop(6)
    (first, second, moves) = pop(3)
    (x_sem, c_sem, w_sem, o_sem, r_sem, h_sem, k_sem) = pop(7)

    tp, place = lax.axis_index("tp"), lax.axis_index("seq")

    core, z = lax.rem(place, 2), lax.div(place, 2)
    fwd = Ring(1, [(held_h, CH, gs_h, gr_h)], *fwd_bufs, layer_out, fwd_sems)
    streams = [(held_v, CH, gs_v, gr_v), (held_qk, CH // 2, gs_q, gr_q)]
    bwd = SplitRing(0, streams, *bwd_bufs, input_grad, bwd_sems)
    bwd.flat, bwd.weight_qk = flat, weight_qk
    early = Carry(True, local_in, state_in, early_bufs, early_sems)
    later = Carry(False, local_out, state_out, late_bufs, late_sems)
    heads = held_h.at[0]

    def columns(t):
        return pl.ds(pl.multiple_of(t * 256, 256), 256)

    def out_block(t):
        return w_out.at[:, columns(t)]

    def swap_device():
        return place + 1 - 2 * core

    sides = ((bwd.weight, 128, 0), (weight_qk, 32, 256))
    fwd_weights, fwd_swaps, fwd_own, bwd_own = [], [], [], []
    bwd_weights, spreads, relays, bwd_swaps = [], ([], []), ([], []), ([], [])
    for p, (a, r) in enumerate((("x", "y"), ("y", "x"))):
        for d in (1, 2, 3):
            for j in range(2):
                k = core * 2 + j
                block = fwd.weight.at[p, k, d]
                wanted = out_block(block_at(a, d, r, k))
                fwd_weights.append(to_device(wanted, block, ws.at[0], wr.at[0], neighbour(a, d)))
        for n, (array, size, start) in enumerate(sides):
            half = rows_of(core, size)
            theirs = pl.ds(pl.multiple_of(start + core * size, size), size)
            for d in (1, 2, 3):
                wanted = weights_t.at[theirs, columns(block_at(a, d, r, z))]
                bwd_weights.append(
                    to_device(wanted, array.at[p, z, d, half], fs.at[n], fr.at[n], neighbour(a, d))
                )
            for n_way, step in enumerate((1, 3)):
                at = (p, n)
                there = lax.rem(z + step, 4) * 2 + core
                mine = array.at[p, z, pl.ds(1, 3), half]
                spreads[p].append(to_seq(mine, mine, zcs.at[at], zcr.at[at], there))
                near = lax.rem(z + 4 - step, 4)
                rows_in = pl.ds(
                    pl.multiple_of(core * size + n_way * (size // 2), size // 2), size // 2
                )
                passing = array.at[p, near, pl.ds(1, 3), rows_in]
                relays[p].append(to_seq(passing, passing, rys.at[at], ryr.at[at], there))
            ours = array.at[p, :, pl.ds(1, 3), half]
            bwd_swaps[p].append(to_seq(ours, ours, ss.at[p, n], sr.at[p, n], swap_device()))
        for k in range(4):
            t = block_at(a, 0, r, k)
            fwd_own.append(
                pltpu.make_async_copy(out_block(t), fwd.weight.at[p, k, 0], w_own.at[0])
            )
            for n, (array, size, start) in enumerate(sides):
                wanted = weights_t.at[pl.ds(start, 2 * size), columns(t)]
                bwd_own.append(
                    pltpu.make_async_copy(wanted, array.at[p, k, 0], q_own.at[n])
                )

    fetched = fwd.weight.at[:, pl.ds(core * 2, 2), pl.ds(1, 3)]
    fwd_fetch = to_device(fetched, fetched, ws.at[0], wr.at[0], neighbour("x", 1))
    fwd_swaps.append(to_seq(fetched, fetched, us.at[0], ur.at[0], swap_device()))
    owned = fwd.weight.at[:, :, 0]
    own_waits = [pltpu.make_async_copy(owned, owned, w_own.at[0])]
    bwd_fetch, spread_waits, relay_waits = [], ([], []), ([], [])
    for n, (array, size, start) in enumerate(sides):
        owned = array.at[:, :, 0]
        own_waits.append(pltpu.make_async_copy(owned, owned, q_own.at[n]))
        fetched = array.at[:, z, pl.ds(1, 3), rows_of(core, size)]
        bwd_fetch.append(to_device(fetched, fetched, fs.at[n], fr.at[n], neighbour("x", 1)))
        for p in range(2):
            both = array.at[p, pl.ds(0, 2), pl.ds(1, 3), rows_of(core, size)]
            one = array.at[p, z, pl.ds(1, 3), rows_of(core, size)]
            there = lax.rem(z + 1, 4) * 2 + core
            spread_waits[p].append(to_seq(both, both, zcs.at[p, n], zcr.at[p, n], there))
            relay_waits[p].append(to_seq(one, one, rys.at[p, n], ryr.at[p, n], there))

    pieces = ((32, 128, 0), (192, 128, 128), (0, 32, 256), (160, 32, 288))
    w_loads = [
        pltpu.make_async_copy(
            w_t.at[pl.ds(src, size)], weights_t.at[pl.ds(dst, size)], w_sem.at[n]
        )
        for n, (src, size, dst) in enumerate(pieces)
    ]
    for copy in w_loads:
        copy.start()

    def x_load(c):
        return pltpu.make_async_copy(inputs.at[rows_of(c)], xin.at[rows_of(c)], x_sem.at[c])

    def c_load(c):
        return pltpu.make_async_copy(cotangent.at[rows_of(c)], cot.at[rows_of(c)], c_sem.at[c])

    x_load(3).start()
    barrier = pltpu.get_barrier_semaphore()
    for d in (1, 2, 3):
        for along in ("x", "y"):
            pl.semaphore_signal(
                barrier, inc=1, device_id={"tp": neighbour(along, d)}, device_id_type=MESH
            )
    for d in (1, 2, 4, 6, 7):
        pl.semaphore_signal(
            barrier, inc=1, device_id={"seq": lax.rem(place + d, 8)}, device_id_type=MESH
        )
    weights_t[pl.ds(320, 64)] = jnp.zeros((64, weights_t.shape[1]), bf16)
    const_loads = [
        pltpu.make_async_copy(src, dst, k_sem.at[n])
        for n, (src, dst) in enumerate(
            ((first_any, first), (second_any, second), (moves_any, moves))
        )
    ]
    o_load = pltpu.make_async_copy(w_out, weights_o, o_sem.at[0])
    res_loads = [
        pltpu.make_async_copy(inputs.at[:, columns(tp)], fwd.res, r_sem.at[0]),
        pltpu.make_async_copy(cotangent.at[:, columns(tp)], bwd.res, r_sem.at[1]),
    ]
    src = lax.broadcasted_iota(jnp.int32, (320, LANES), 0)
    dst = lax.broadcasted_iota(jnp.int32, (320, LANES), 1)
    from_high = jnp.where(dst < 288, dst - 256, jnp.where(dst < 320, dst - 128, -1))
    source = jnp.where(dst < 128, dst + 32, jnp.where(dst < 256, dst + 64, from_high))
    taps = lax.dot_general(
        conv[...],
        jnp.where(src == source, 1.0, 0.0).astype(f32),
        NN,
        precision=lax.Precision.HIGHEST,
        preferred_element_type=f32,
    )
    lane = lax.broadcasted_iota(jnp.int32, (1, HEADS * DV), 1)
    gain = gains[...] * jnp.where(lane < DV, keep[0].astype(f32), keep[1].astype(f32))

    for copy in w_loads:
        copy.wait()
    for c in (0, 1, 2):
        x_load(c).start()
    for copy in const_loads + [o_load] + res_loads + fwd_own + bwd_own:
        copy.start()

    ahead = to_seq(
        pp.at[pl.ds(NCH * CH, 8)], halo_in, h_sem.at[0], h_sem.at[1], lax.rem(place + 1, 8)
    )
    behind = to_seq(
        dconv.at[pl.ds(0, 8)], halo_out, h_sem.at[2], h_sem.at[3], lax.rem(place + 7, 8)
    )

    @pl.loop(0, NCH)
    def _(i):
        c = lax.rem(i + NCH - 1, NCH)
        x_load(c).wait()
        c_load(c).start()
        projected = dot(xin[rows_of(c)], weights_t[...], NT).astype(bf16).astype(f32)
        pp[pl.ds(pl.multiple_of(c * CH + 8, 8), CH)] = projected

        @pl.when(i == 0)
        def _():
            pl.semaphore_wait(barrier, 11)
            ahead.start()
            for copy in bwd_weights + fwd_weights:
                copy.start()

    for copy in const_loads:
        copy.wait()
    ahead.wait()
    pp[pl.ds(0, 8)] = halo_in[...] * one_if(place > 0)

    t0, t1, t2 = taps[0:1], taps[1:2], taps[2:3]
    bias_a, bias_b, scale = rows[0:1], rows[1:2], rows[2:3]

    def factors(qk, group):
        return dot(qk, first[group]) + bias_a, dot(qk, second[group]) + bias_b

    def lanes(h):
        return slice(h * DV, (h + 1) * DV)

    def qk_of(c):
        return cv[rows_of(c), 2 * DV : LANES]

    local_in[...] = jnp.zeros(local_in.shape, f32)

    @pl.loop(0, NCH)
    def _(c):
        window = pp[pl.ds(pl.multiple_of(c * CH, CH), CH + 8)]
        mixed = t0 * window[8:] + (
            t1 * pltpu.roll(window, 1, 0)[8:] + t2 * pltpu.roll(window, 2, 0)[8:]
        )
        cv[rows_of(c)] = mixed.astype(bf16)
        qk = qk_of(c)
        for h in range(HEADS):
            a, b = factors(qk, 2 * h + 1)
            features = (a * b).astype(bf16)
            phi_k[h, rows_of(c)] = features
            local = dot(cv[rows_of(c), lanes(h)], features, TN)
            states[c, h] = local
            local_in[h] = local_in[h] + local

    early.start()

    causal = lax.broadcasted_iota(jnp.int32, (CH, CH), 0) >= lax.broadcasted_iota(
        jnp.int32, (CH, CH), 1
    )

    @pl.loop(0, NCH)
    def _(c):
        qk = qk_of(c)
        for h in range(HEADS):
            moved = dot(qk, moves[2 * h]).astype(bf16)
            moved_q[h, rows_of(c)] = moved
            logits = dot(moved, qk, NT) * 0.25
            weight = jnp.where(causal, 1.0 + logits + 0.5 * logits * logits, 0.0).astype(bf16)
            saved_w[h, rows_of(c)] = weight
            saved_l[h, rows_of(c)] = jnp.where(causal, 0.25 + 0.25 * logits, 0.0)
            mix[rows_of(c), lanes(h)] = dot(weight, cv[rows_of(c), lanes(h)])

        @pl.when(c == 1)
        def _():
            early.middle()

    o_load.wait()

    @pl.loop(0, NCH)
    def _(c):
        c_load(c).wait()
        gh[rows_of(c)] = dot(cot[rows_of(c)], weights_o[...], NT) * gain

    @pl.loop(0, NCH)
    def _(c):
        qk = qk_of(c)
        for h in range(HEADS):
            a, b = factors(qk, 2 * h)
            phi_q[h, rows_of(c)] = (a * b).astype(bf16)

    early.late()
    for copy in bwd_fetch:
        copy.wait()
    for copy in spreads[0]:
        copy.start()
    early.end()
    local_out[...] = jnp.zeros(local_out.shape, f32)

    @pl.loop(0, NCH)
    def _(c):
        for h in range(HEADS):
            entering = state_in[h]
            state_in[h] = entering + states[c, h]
            scaled[c, h] = (entering * scale).astype(bf16)
            numerator = mix[rows_of(c), lanes(h)] + dot(phi_q[h, rows_of(c)], scaled[c, h], NT)
            inverse = lax.rsqrt(jnp.mean(numerator * numerator, -1, keepdims=True) + epsilon)
            normed = numerator * inverse
            heads[rows_of(c), lanes(h)] = (normed * gain[:, lanes(h)]).astype(bf16)
            grad = gh[rows_of(c), lanes(h)]
            d_numer = (grad - normed * jnp.mean(grad * normed, -1, keepdims=True)) * inverse
            rounded = d_numer.astype(bf16)
            dn[rows_of(c), lanes(h)] = rounded
            local = dot(rounded, phi_q[h, rows_of(c)], TN)
            grads[c, h] = local
            local_out[h] = local_out[h] + local
        fwd.send_own(c)

    later.start()
    fwd_fetch.wait()
    for copy in fwd_swaps:
        copy.start()

    @pl.loop(0, NCH)
    def _(c):
        qk = qk_of(c)
        d_qk = jnp.zeros((CH, 128), f32)
        for h in range(HEADS):
            rounded = dn[rows_of(c), lanes(h)]
            dconv[rows_of(c), lanes(h)] = dot(saved_w[h, rows_of(c)], rounded, TN)
            d_weight = dot(rounded, cv[rows_of(c), lanes(h)], NT)
            d_logits = (d_weight * saved_l[h, rows_of(c)]).astype(bf16)
            d_qk = d_qk + dot(d_logits, dot(qk, moves[2 * h + 1]).astype(bf16))
            d_qk = d_qk + dot(d_logits, moved_q[h, rows_of(c)], TN)
            a, b = factors(qk, 2 * h)
            d_phi = dot(rounded, scaled[c, h])
            d_qk = d_qk + dot((d_phi * b).astype(bf16), first[2 * h], NT)
            d_qk = d_qk + dot((d_phi * a).astype(bf16), second[2 * h], NT)
        dconv[rows_of(c), 2 * DV : LANES] = d_qk

        @pl.when(c == 0)
        def _():
            later.middle()

        @pl.when(c >= 1)
        def _():
            fwd.forward(c - 1)

    fwd.forward(NCH - 1)
    for copy in spread_waits[0]:
        copy.wait()
    for copy in relays[0]:
        copy.start()
    later.late()
    later.end()
    state_out[...] = state_out[...] + local_out[...]

    def project_back(c):
        window = dconv[pl.ds(pl.multiple_of(c * CH, CH), CH + 8)]
        mixed = t0 * window[:CH] + (
            t1 * pltpu.roll(window, CH + 7, 0)[:CH] + t2 * pltpu.roll(window, CH + 6, 0)[:CH]
        )
        held_v[0, rows_of(c)] = mixed[:, : 2 * DV].astype(bf16)
        packed = mixed[: CH // 2, 2 * DV :] + pltpu.roll(mixed[CH // 2 :, 2 * DV :], 64, 1)
        held_qk[0, rows_of(c, CH // 2)] = packed.astype(bf16)

    @pl.loop(0, NCH)
    def _(c):
        qk = qk_of(c)
        d_qk = dconv[rows_of(c), 2 * DV : LANES]
        for h in range(HEADS):
            remaining = state_out[h] - grads[c, h]
            state_out[h] = remaining
            suffix = (remaining * scale).astype(bf16)
            dconv[rows_of(c), lanes(h)] = dconv[rows_of(c), lanes(h)] + dot(
                phi_k[h, rows_of(c)], suffix, NT
            )
            a, b = factors(qk, 2 * h + 1)
            d_phi = dot(cv[rows_of(c), lanes(h)], suffix)
            d_qk = d_qk + dot((d_phi * b).astype(bf16), first[2 * h + 1], NT)
            d_qk = d_qk + dot((d_phi * a).astype(bf16), second[2 * h + 1], NT)
        dconv[rows_of(c), 2 * DV : LANES] = d_qk

        @pl.when(c == 0)
        def _():
            behind.start()

        @pl.when(c == 1)
        def _():
            for copy in spreads[1]:
                copy.start()

        @pl.when(c > 0)
        def _():
            project_back(c - 1)

        @pl.when(c > 0)
        def _():
            bwd.send_own(c - 1)

    behind.wait()
    dconv[pl.ds(NCH * CH, 8)] = halo_out[...] * one_if(place < 7)
    project_back(NCH - 1)
    bwd.send_own(NCH - 1)

    for copy in fwd_swaps + own_waits + res_loads:
        copy.wait()

    @pl.loop(0, NCH)
    def _(j):
        fwd.compute(j)

    @pl.loop(0, NCH)
    def _(j):
        bwd.forward(j)
        fwd.send(j)

        @pl.when(j == 1)
        def _():
            for copy in relay_waits[0] + spread_waits[1]:
                copy.wait()
            for copy in bwd_swaps[0] + relays[1]:
                copy.start()

    for copy in bwd_swaps[0]:
        copy.wait()

    @pl.loop(0, NCH + 3)
    def _(i):
        @pl.when(i < NCH)
        def _():
            bwd.multiply(i)

        @pl.when(i == 0)
        def _():
            for copy in relay_waits[1]:
                copy.wait()
            for copy in bwd_swaps[1]:
                copy.start()
            for copy in bwd_swaps[1]:
                copy.wait()

        @pl.when((i >= 1) & (i < NCH + 1))
        def _():
            fwd.relayed(i - 1)

        @pl.when(i >= 3)
        def _():
            bwd.relayed(i - 3)

    @pl.loop(0, NCH)
    def _(i):
        fwd.finish(i)
        bwd.finish(i)

    fwd.drain()
    bwd.drain()

    early.drain()
    later.drain()


def settle_kernel(first, second, first_out, second_out, held, in_sem, out_sem):
    pairs = ((first, first_out), (second, second_out))
    ins = [pltpu.make_async_copy(p[0], held.at[n], in_sem.at[n]) for n, p in enumerate(pairs)]
    outs = [pltpu.make_async_copy(held.at[n], p[1], out_sem.at[n]) for n, p in enumerate(pairs)]
    for copy in ins:
        copy.start()
    for n in range(2):
        ins[n].wait()
        outs[n].start()
    for copy in outs:
        copy.wait()


def settle(first, second):
    whole = pl.BlockSpec(memory_space=pl.ANY)
    result = jax.ShapeDtypeStruct(first.shape, first.dtype)
    dma = pltpu.SemaphoreType.DMA
    return pl.pallas_call(
        settle_kernel,
        out_shape=(result, result),
        in_specs=[whole] * 2,
        out_specs=(whole, whole),
        scratch_shapes=[pltpu.VMEM((2,) + first.shape, first.dtype), dma((2,)), dma((2,))],
    )(first, second)


def per_device(inputs, cotangent, w_in, conv_w, norm_gain, w_out, keep_flags):
    count, width = inputs.shape
    first, second, rows, moves = selectors()
    consts = [jnp.asarray(part, bf16) for part in (first, second, moves)]
    whole, near = pl.BlockSpec(memory_space=pl.ANY), pl.BlockSpec(memory_space=pltpu.VMEM)
    result = jax.ShapeDtypeStruct((count, 256), bf16)
    dma = pltpu.SemaphoreType.DMA
    state = (DV, EXP)
    lump = (160, DV)
    carry_bufs = [pltpu.VMEM((n,) + lump if n > 1 else lump, bf16) for n in (1, 1, 1, 3, 1, 1)]
    carry_sems = [dma((4,)), dma((3,)), dma((3,))]
    results = pl.pallas_call(
        layer_kernel,
        out_shape=(result, result),
        in_specs=[whole] * 7 + [near] * 3 + [pl.BlockSpec(memory_space=pltpu.SMEM)],
        out_specs=(whole, whole),
        scratch_shapes=ring_buffers(count)
        + ring_buffers(count)
        + ring_semaphores()
        + ring_semaphores()
        + [
            pltpu.VMEM((4, count, 256), bf16),
            pltpu.VMEM((4, count, 256), bf16),
            pltpu.VMEM((4, count // 2, 128), bf16),
            pltpu.VMEM((2, 4, 4, 64, 256), bf16),
            pltpu.VMEM((CH, 256), bf16),
            pltpu.VMEM((HEADS, count, CH), bf16),
            pltpu.VMEM((HEADS, count, CH), f32),
            pltpu.VMEM((HEADS, count, 128), bf16),
        ]
        + [dma((1,)), dma((3, NCH))] * 3
        + [dma((1,))] * 4
        + [dma((1,)), dma((2,))]
        + [dma((2,))] * 2
        + [dma((2, 2))] * 4
        + [dma((2, 2))] * 2
        + carry_bufs
        + carry_bufs
        + carry_sems
        + carry_sems
        + [
            pltpu.VMEM((count, width), bf16),
            pltpu.VMEM((count, width), bf16),
            pltpu.VMEM((LANES, width), bf16),
            pltpu.VMEM((256, width), bf16),
            pltpu.VMEM((count + 8, LANES), f32),
            pltpu.VMEM((count, LANES), bf16),
            pltpu.VMEM((count, 256), f32),
            pltpu.VMEM((count, 256), f32),
            pltpu.VMEM((count, 256), bf16),
            pltpu.VMEM((HEADS, count, EXP), bf16),
            pltpu.VMEM((HEADS, count, EXP), bf16),
            pltpu.VMEM((NCH, HEADS) + state, f32),
            pltpu.VMEM((NCH, HEADS) + state, f32),
            pltpu.VMEM((NCH, HEADS) + state, bf16),
            pltpu.VMEM((HEADS,) + state, f32),
            pltpu.VMEM((HEADS,) + state, f32),
            pltpu.VMEM((HEADS,) + state, f32),
            pltpu.VMEM((HEADS,) + state, f32),
            pltpu.VMEM((8, LANES), f32),
            pltpu.VMEM((8, LANES), f32),
            pltpu.VMEM((4, 128, EXP), bf16),
            pltpu.VMEM((4, 128, EXP), bf16),
            pltpu.VMEM((4, 128, 128), bf16),
            dma((NCH,)),
            dma((NCH,)),
            dma((4,)),
            dma((1,)),
            dma((2,)),
            dma((4,)),
            dma((3,)),
        ],
        compiler_params=pltpu.CompilerParams(
            collective_id=0, has_side_effects=True, vmem_limit_bytes=67043328
        ),
    )(
        inputs,
        cotangent,
        w_in.T,
        w_out,
        *consts,
        conv_w,
        norm_gain.reshape(1, HEADS * DV),
        jnp.asarray(rows),
        keep_flags,
    )
    return settle(*results)


def solution(mesh):
    placed = (
        P("seq", None),
        P("seq", None),
        P(None, "tp"),
        P(None, "tp"),
        P("tp"),
        P("tp", None),
        P("tp"),
    )
    return jax.shard_map(
        per_device,
        mesh=mesh,
        in_specs=placed,
        out_specs=(P("seq", "tp"), P("seq", "tp")),
        check_vma=False,
    )
```

```python
from functools import partial

import jax
import jax.numpy as jnp
import numpy as np
from jax import lax
from jax.experimental import pallas as pl
from jax.experimental.pallas import tpu as pltpu
from jax.sharding import PartitionSpec as P

FEAT = 16
DV = 128
LANES = 384
EXP = 256
HEADS = 2
epsilon = 1e-06

CH = 256
NCH = 4
MESH = pl.DeviceIdType.MESH
NT = (((1,), (1,)), ((), ()))
NN = (((1,), (0,)), ((), ()))
TN = (((0,), (0,)), ((), ()))
f32 = jnp.float32
bf16 = jnp.bfloat16


def neighbour(along, step):
    place = lax.axis_index("tp")
    column, row = lax.rem(place, 4), lax.div(place, 4)
    if along == "x":
        return row * 4 + lax.rem(column + step, 4)
    return lax.rem(row + step, 4) * 4 + column


def block_at(a_along, a_step, r_along, r_step):
    place = lax.axis_index("tp")
    column, row = lax.rem(place, 4), lax.div(place, 4)
    x_step = a_step if a_along == "x" else r_step
    y_step = a_step if a_along == "y" else r_step
    return lax.rem(row + y_step, 4) * 4 + lax.rem(column + x_step, 4)


def to_device(src, dst, send_sem, recv_sem, place):
    return pltpu.make_async_remote_copy(
        src_ref=src,
        dst_ref=dst,
        send_sem=send_sem,
        recv_sem=recv_sem,
        device_id={"tp": place},
        device_id_type=MESH,
    )


def to_seq(src, dst, send_sem, recv_sem, place):
    return pltpu.make_async_remote_copy(
        src_ref=src,
        dst_ref=dst,
        send_sem=send_sem,
        recv_sem=recv_sem,
        device_id={"seq": place},
        device_id_type=MESH,
    )


def dot(a, b, dims=NN):
    return lax.dot_general(a, b, dims, preferred_element_type=f32)


def rows_of(c, size=CH):
    return pl.ds(pl.multiple_of(c * size, size), size)


def way(c):
    return jnp.where(c < NCH // 2, 1, 3)


class Ring:
    def __init__(self, flip, streams, weight, part, landed, relay, keep, res, out, sems):
        self.flip, self.streams, self.weight = flip, streams, weight
        self.part, self.landed, self.relay = part, landed, relay
        self.keep, self.res, self.out = keep, res, out
        (self.ps, self.tr, self.pr, self.os) = sems

    def turn(self, c):
        return lax.rem(c + self.flip, 2)

    def gather_to(self, c, d):
        return jnp.where(self.turn(c) == 0, neighbour("x", d), neighbour("y", d))

    def scatter_to(self, c, d):
        return jnp.where(self.turn(c) == 0, neighbour("y", d), neighbour("x", d))

    def direct(self, c, d):
        return [
            to_device(
                held.at[0, rows_of(c, size)],
                held.at[d, rows_of(c, size)],
                send.at[0],
                recv.at[d - 1, c],
                self.gather_to(c, d),
            )
            for held, size, send, recv in self.streams
        ]

    def passed_on(self, c):
        return [
            to_device(
                held.at[way(c), rows_of(c, size)],
                held.at[2, rows_of(c, size)],
                send.at[0],
                recv.at[1, c],
                self.gather_to(c, way(c)),
            )
            for held, size, send, recv in self.streams
        ]

    def send_own(self, c):
        for d in (1, 3):
            for copy in self.direct(c, d):
                copy.start()

    def forward(self, c):
        for d in (1, 3):
            for copy in self.direct(c, d):
                copy.wait_recv()
        for copy in self.passed_on(c):
            copy.start()

    def tie(self, c):
        return to_device(
            self.part.at[2, rows_of(c)],
            self.relay.at[rows_of(c)],
            self.ps.at[0],
            self.tr.at[c],
            self.scatter_to(c, way(c)),
        )

    def side(self, c, d):
        return to_device(
            self.part.at[d, rows_of(c)],
            self.landed.at[d // 2, rows_of(c)],
            self.ps.at[0],
            self.pr.at[d // 2, c],
            self.scatter_to(c, d),
        )

    def prepare(self, c):
        pass

    def product(self, c, k):
        held = self.streams[0][0]
        total = None
        for o in range(4):
            term = dot(held[o, rows_of(c)], self.weight[self.turn(c), k, o])
            total = term if total is None else total + term
        return total

    def compute(self, c):
        for copy in self.passed_on(c):
            copy.wait_recv()
        self.prepare(c)
        near, far = way(c), 4 - way(c)
        self.part[2, rows_of(c)] = self.product(c, 2).astype(bf16)
        self.part[far, rows_of(c)] = self.product(c, far).astype(bf16)
        self.keep[1, rows_of(c)] = self.product(c, near)
        self.keep[0, rows_of(c)] = self.product(c, 0) + self.res[rows_of(c)].astype(f32)

    def send(self, c):
        self.tie(c).start()
        self.side(c, 4 - way(c)).start()

    def multiply(self, c):
        for copy in self.passed_on(c):
            copy.wait_recv()
        self.prepare(c)
        near, far = way(c), 4 - way(c)
        self.part[2, rows_of(c)] = self.product(c, 2).astype(bf16)
        self.tie(c).start()
        self.keep[1, rows_of(c)] = self.product(c, near)
        self.part[far, rows_of(c)] = self.product(c, far).astype(bf16)
        self.side(c, far).start()
        self.keep[0, rows_of(c)] = self.product(c, 0) + self.res[rows_of(c)].astype(f32)

    def relayed(self, c):
        self.tie(c).wait_recv()
        near = way(c)
        total = self.keep[1, rows_of(c)] + self.relay[rows_of(c)].astype(f32)
        self.part[near, rows_of(c)] = total.astype(bf16)
        self.side(c, near).start()

    def finish(self, c):
        self.side(c, 1).wait_recv()
        self.side(c, 3).wait_recv()
        total = self.keep[0, rows_of(c)] + (
            self.landed[0, rows_of(c)].astype(f32) + self.landed[1, rows_of(c)].astype(f32)
        )
        self.part[0, rows_of(c)] = total.astype(bf16)
        self.leave(c).start()

    def leave(self, c):
        return pltpu.make_async_copy(
            self.part.at[0, rows_of(c)], self.out.at[rows_of(c)], self.os.at[0]
        )

    def drain(self):
        for held, _, send, recv in self.streams:
            sent = held.at[pl.ds(1, 3)]
            to_device(sent, sent, send.at[0], recv.at[0, 0], self.gather_to(0, 1)).wait_send()
        sent = self.part.at[pl.ds(1, 3)]
        to_device(sent, sent, self.ps.at[0], self.tr.at[0], self.scatter_to(0, 1)).wait_send()
        pltpu.make_async_copy(self.part.at[0], self.out, self.os.at[0]).wait()


class SplitRing(Ring):
    def prepare(self, c):
        packed = self.streams[1][0]
        low = lax.broadcasted_iota(jnp.int32, (CH // 2, 128), 1) < 64
        for pair in range(2):
            one = packed[2 * pair, rows_of(c, CH // 2)].astype(f32)
            two = packed[2 * pair + 1, rows_of(c, CH // 2)].astype(f32)
            top = jnp.where(low, one, pltpu.roll(two, 64, 1))
            bottom = jnp.where(low, pltpu.roll(one, 64, 1), two)
            lanes = slice(pair * 128, pair * 128 + 128)
            self.flat[0 : CH // 2, lanes] = top.astype(bf16)
            self.flat[CH // 2 : CH, lanes] = bottom.astype(bf16)

    def product(self, c, k):
        return super().product(c, k) + dot(self.flat[...], self.weight_qk[self.turn(c), k].reshape(256, 256))


def ring_semaphores():
    dma = pltpu.SemaphoreType.DMA
    return [dma((1,)), dma((NCH,)), dma((2, NCH)), dma((1,))]


def ring_buffers(rows):
    return [
        pltpu.VMEM((2, 4, 4, 256, 256), bf16),
        pltpu.VMEM((4, rows, 256), bf16),
        pltpu.VMEM((2, rows, 256), bf16),
        pltpu.VMEM((rows, 256), bf16),
        pltpu.VMEM((2, rows, 256), f32),
        pltpu.VMEM((rows, 256), bf16),
    ]


def selectors():
    first = np.zeros((4, 128, EXP), np.float32)
    second = np.zeros((4, 128, EXP), np.float32)
    rows = np.zeros((8, EXP), np.float32)
    rows[0, 0] = rows[1, 0] = rows[2, 0] = 1.0
    for group in range(4):
        base = group * FEAT
        for i in range(FEAT):
            first[group, base + i, 1 + i] = 1.0
            rows[1, 1 + i] = 1.0
            rows[2, 1 + i] = 0.25
        e = 1 + FEAT
        for i in range(FEAT):
            for j in range(i, FEAT):
                first[group, base + i, e] = 1.0
                second[group, base + j, e] = 1.0
                rows[2, e] = 1 / 32 if i == j else 1 / 16
                e += 1
    moves = np.zeros((4, 128, 128), np.float32)
    for h in range(HEADS):
        for i in range(FEAT):
            q, k = 2 * h * FEAT + i, (2 * h + 1) * FEAT + i
            moves[2 * h, q, k] = 1.0
            moves[2 * h + 1, k, q] = 1.0
    return first, second, rows, moves


def one_if(condition):
    return jnp.where(condition, 1.0, 0.0).astype(f32)


def packed_state(state):
    rest = state[:32, DV:]
    for g in range(1, 4):
        rest = rest + pltpu.roll(state[32 * g : 32 * g + 32, DV:], 32 * g, 1)
    return jnp.concatenate([state[:, :DV], rest], 0)


def whole_state(packed):
    low = lax.broadcasted_iota(jnp.int32, (32, DV), 1) < 32
    rest = packed[DV:]
    parts = [rest] + [pltpu.roll(rest, DV - 32 * g, 1) for g in range(1, 4)]
    parts = [jnp.where(low, part, 0.0) for part in parts]
    return jnp.concatenate([packed[:DV], jnp.concatenate(parts, 0)], 1)


class Carry:
    def __init__(self, earlier, local, state, bufs, sems):
        self.earlier, self.local, self.state = earlier, local, state
        self.sa, self.ra, self.sb, self.rb, self.sc, self.rc = bufs
        self.pair_sems, self.zs, self.zr = sems
        place = lax.axis_index("seq")
        self.core, self.z = lax.rem(place, 2), lax.div(place, 2)
        self.partner = self.z * 2 + (1 - self.core)

    def swap(self):
        return to_seq(self.sa, self.ra, self.pair_sems.at[0], self.pair_sems.at[1], self.partner)

    def give(self):
        return to_seq(self.sc, self.rc, self.pair_sems.at[2], self.pair_sems.at[3], self.partner)

    def along(self, step):
        there = lax.rem(self.z + step, 4) * 2 + self.core
        return to_seq(
            self.sb, self.rb.at[step - 1], self.zs.at[step - 1], self.zr.at[step - 1], there
        )

    def start(self):
        self.sa[...] = packed_state(self.local[1 - self.core]).astype(bf16)
        self.swap().start()

    def middle(self):
        self.swap().wait_recv()
        self.sb[...] = (packed_state(self.local[self.core]) + self.ra[...].astype(f32)).astype(bf16)
        for step in (1, 2, 3):
            self.along(step).start()

    def late(self):
        total = jnp.zeros(self.sb.shape, f32)
        for step in (1, 2, 3):
            self.along(step).wait_recv()
            counts = one_if(self.z >= step if self.earlier else self.z < step)
            total = total + self.rb[step - 1].astype(f32) * counts
        takes = self.core if self.earlier else 1 - self.core
        own = packed_state(self.local[self.core]) * one_if(takes == 0)
        self.sc[...] = (total + own).astype(bf16)
        self.give().start()
        self.state[self.core] = whole_state(total + self.ra[...].astype(f32) * one_if(takes == 1))

    def end(self):
        self.give().wait_recv()
        self.state[1 - self.core] = whole_state(self.rc[...].astype(f32))

    def drain(self):
        self.swap().wait_send()
        self.give().wait_send()
        for step in (1, 2, 3):
            self.along(step).wait_send()


def layer_kernel(
    inputs, cotangent, w_t, w_out, first_any, second_any, moves_any, conv, gains, rows, keep,
    layer_out, input_grad, *scratch,
):
    take = list(scratch)

    def pop(n):
        got = take[:n]
        del take[:n]
        return got

    fwd_bufs, bwd_bufs = pop(6), pop(6)
    fwd_sems, bwd_sems = pop(4), pop(4)
    (held_h, held_v, held_qk, weight_qk, flat, saved_w, saved_l, moved_q) = pop(8)
    (gs_h, gr_h, gs_v, gr_v, gs_q, gr_q) = pop(6)
    (ws, wr, us, ur, w_own, q_own) = pop(6)
    (fs, fr, zcs, zcr, rys, ryr, ss, sr) = pop(8)
    early_bufs, late_bufs = pop(6), pop(6)
    early_sems, late_sems = pop(3), pop(3)
    (xin, cot, weights_t, weights_o) = pop(4)
    (pp, cv, mix, gh, dn, phi_q, phi_k, states, grads, scaled) = pop(10)
    dconv = pp
    (state_in, state_out, local_in, local_out, halo_in, halo_out) = pop(6)
    (first, second, moves) = pop(3)
    (x_sem, c_sem, w_sem, o_sem, r_sem, h_sem, k_sem) = pop(7)

    tp, place = lax.axis_index("tp"), lax.axis_index("seq")

    core, z = lax.rem(place, 2), lax.div(place, 2)
    fwd = Ring(1, [(held_h, CH, gs_h, gr_h)], *fwd_bufs, layer_out, fwd_sems)
    streams = [(held_v, CH, gs_v, gr_v), (held_qk, CH // 2, gs_q, gr_q)]
    bwd = SplitRing(0, streams, *bwd_bufs, input_grad, bwd_sems)
    bwd.flat, bwd.weight_qk = flat, weight_qk
    early = Carry(True, local_in, state_in, early_bufs, early_sems)
    later = Carry(False, local_out, state_out, late_bufs, late_sems)
    heads = held_h.at[0]

    def columns(t):
        return pl.ds(pl.multiple_of(t * 256, 256), 256)

    def out_block(t):
        return w_out.at[:, columns(t)]

    def swap_device():
        return place + 1 - 2 * core

    sides = ((bwd.weight, 128, 0), (weight_qk, 32, 256))
    fwd_weights, fwd_swaps, fwd_own, bwd_own = [], [], [], []
    bwd_weights, spreads, relays, bwd_swaps = [], ([], []), ([], []), ([], [])
    for p, (a, r) in enumerate((("x", "y"), ("y", "x"))):
        for d in (1, 2, 3):
            for j in range(2):
                k = core * 2 + j
                block = fwd.weight.at[p, k, d]
                wanted = out_block(block_at(a, d, r, k))
                fwd_weights.append(to_device(wanted, block, ws.at[0], wr.at[0], neighbour(a, d)))
        for n, (array, size, start) in enumerate(sides):
            half = rows_of(core, size)
            theirs = pl.ds(pl.multiple_of(start + core * size, size), size)
            for d in (1, 2, 3):
                wanted = weights_t.at[theirs, columns(block_at(a, d, r, z))]
                bwd_weights.append(
                    to_device(wanted, array.at[p, z, d, half], fs.at[n], fr.at[n], neighbour(a, d))
                )
            for n_way, step in enumerate((1, 3)):
                at = (p, n)
                there = lax.rem(z + step, 4) * 2 + core
                mine = array.at[p, z, pl.ds(1, 3), half]
                spreads[p].append(to_seq(mine, mine, zcs.at[at], zcr.at[at], there))
                near = lax.rem(z + 4 - step, 4)
                rows_in = pl.ds(
                    pl.multiple_of(core * size + n_way * (size // 2), size // 2), size // 2
                )
                passing = array.at[p, near, pl.ds(1, 3), rows_in]
                relays[p].append(to_seq(passing, passing, rys.at[at], ryr.at[at], there))
            ours = array.at[p, :, pl.ds(1, 3), half]
            bwd_swaps[p].append(to_seq(ours, ours, ss.at[p, n], sr.at[p, n], swap_device()))
        for k in range(4):
            t = block_at(a, 0, r, k)
            fwd_own.append(
                pltpu.make_async_copy(out_block(t), fwd.weight.at[p, k, 0], w_own.at[0])
            )
            for n, (array, size, start) in enumerate(sides):
                wanted = weights_t.at[pl.ds(start, 2 * size), columns(t)]
                bwd_own.append(
                    pltpu.make_async_copy(wanted, array.at[p, k, 0], q_own.at[n])
                )

    fetched = fwd.weight.at[:, pl.ds(core * 2, 2), pl.ds(1, 3)]
    fwd_fetch = to_device(fetched, fetched, ws.at[0], wr.at[0], neighbour("x", 1))
    fwd_swaps.append(to_seq(fetched, fetched, us.at[0], ur.at[0], swap_device()))
    owned = fwd.weight.at[:, :, 0]
    own_waits = [pltpu.make_async_copy(owned, owned, w_own.at[0])]
    bwd_fetch, spread_waits, relay_waits = [], ([], []), ([], [])
    for n, (array, size, start) in enumerate(sides):
        owned = array.at[:, :, 0]
        own_waits.append(pltpu.make_async_copy(owned, owned, q_own.at[n]))
        fetched = array.at[:, z, pl.ds(1, 3), rows_of(core, size)]
        bwd_fetch.append(to_device(fetched, fetched, fs.at[n], fr.at[n], neighbour("x", 1)))
        for p in range(2):
            both = array.at[p, pl.ds(0, 2), pl.ds(1, 3), rows_of(core, size)]
            one = array.at[p, z, pl.ds(1, 3), rows_of(core, size)]
            there = lax.rem(z + 1, 4) * 2 + core
            spread_waits[p].append(to_seq(both, both, zcs.at[p, n], zcr.at[p, n], there))
            relay_waits[p].append(to_seq(one, one, rys.at[p, n], ryr.at[p, n], there))

    pieces = ((32, 128, 0), (192, 128, 128), (0, 32, 256), (160, 32, 288))
    w_loads = [
        pltpu.make_async_copy(
            w_t.at[pl.ds(src, size)], weights_t.at[pl.ds(dst, size)], w_sem.at[n]
        )
        for n, (src, size, dst) in enumerate(pieces)
    ]
    for copy in w_loads:
        copy.start()

    def x_load(c):
        return pltpu.make_async_copy(inputs.at[rows_of(c)], xin.at[rows_of(c)], x_sem.at[c])

    def c_load(c):
        return pltpu.make_async_copy(cotangent.at[rows_of(c)], cot.at[rows_of(c)], c_sem.at[c])

    x_load(3).start()
    barrier = pltpu.get_barrier_semaphore()
    for d in (1, 2, 3):
        for along in ("x", "y"):
            pl.semaphore_signal(
                barrier, inc=1, device_id={"tp": neighbour(along, d)}, device_id_type=MESH
            )
    for d in (1, 2, 4, 6, 7):
        pl.semaphore_signal(
            barrier, inc=1, device_id={"seq": lax.rem(place + d, 8)}, device_id_type=MESH
        )
    weights_t[pl.ds(320, 64)] = jnp.zeros((64, weights_t.shape[1]), bf16)
    const_loads = [
        pltpu.make_async_copy(src, dst, k_sem.at[n])
        for n, (src, dst) in enumerate(
            ((first_any, first), (second_any, second), (moves_any, moves))
        )
    ]
    o_load = pltpu.make_async_copy(w_out, weights_o, o_sem.at[0])
    res_loads = [
        pltpu.make_async_copy(inputs.at[:, columns(tp)], fwd.res, r_sem.at[0]),
        pltpu.make_async_copy(cotangent.at[:, columns(tp)], bwd.res, r_sem.at[1]),
    ]
    src = lax.broadcasted_iota(jnp.int32, (320, LANES), 0)
    dst = lax.broadcasted_iota(jnp.int32, (320, LANES), 1)
    from_high = jnp.where(dst < 288, dst - 256, jnp.where(dst < 320, dst - 128, -1))
    source = jnp.where(dst < 128, dst + 32, jnp.where(dst < 256, dst + 64, from_high))
    taps = lax.dot_general(
        conv[...],
        jnp.where(src == source, 1.0, 0.0).astype(f32),
        NN,
        precision=lax.Precision.HIGHEST,
        preferred_element_type=f32,
    )
    lane = lax.broadcasted_iota(jnp.int32, (1, HEADS * DV), 1)
    gain = gains[...] * jnp.where(lane < DV, keep[0].astype(f32), keep[1].astype(f32))

    for copy in w_loads:
        copy.wait()
    for c in (0, 1, 2):
        x_load(c).start()
    for copy in const_loads + [o_load] + res_loads + fwd_own + bwd_own:
        copy.start()

    ahead = to_seq(
        pp.at[pl.ds(NCH * CH, 8)], halo_in, h_sem.at[0], h_sem.at[1], lax.rem(place + 1, 8)
    )
    behind = to_seq(
        dconv.at[pl.ds(0, 8)], halo_out, h_sem.at[2], h_sem.at[3], lax.rem(place + 7, 8)
    )

    @pl.loop(0, NCH)
    def _(i):
        c = lax.rem(i + NCH - 1, NCH)
        x_load(c).wait()
        c_load(c).start()
        projected = dot(xin[rows_of(c)], weights_t[...], NT).astype(bf16).astype(f32)
        pp[pl.ds(pl.multiple_of(c * CH + 8, 8), CH)] = projected

        @pl.when(i == 0)
        def _():
            pl.semaphore_wait(barrier, 11)
            ahead.start()
            for copy in bwd_weights + fwd_weights:
                copy.start()

    for copy in const_loads:
        copy.wait()
    ahead.wait()
    pp[pl.ds(0, 8)] = halo_in[...] * one_if(place > 0)

    t0, t1, t2 = taps[0:1], taps[1:2], taps[2:3]
    bias_a, bias_b, scale = rows[0:1], rows[1:2], rows[2:3]

    def factors(qk, group):
        return dot(qk, first[group]) + bias_a, dot(qk, second[group]) + bias_b

    def lanes(h):
        return slice(h * DV, (h + 1) * DV)

    def qk_of(c):
        return cv[rows_of(c), 2 * DV : LANES]

    local_in[...] = jnp.zeros(local_in.shape, f32)

    @pl.loop(0, NCH)
    def _(c):
        window = pp[pl.ds(pl.multiple_of(c * CH, CH), CH + 8)]
        mixed = t0 * window[8:] + (
            t1 * pltpu.roll(window, 1, 0)[8:] + t2 * pltpu.roll(window, 2, 0)[8:]
        )
        cv[rows_of(c)] = mixed.astype(bf16)
        qk = qk_of(c)
        for h in range(HEADS):
            a, b = factors(qk, 2 * h + 1)
            features = (a * b).astype(bf16)
            phi_k[h, rows_of(c)] = features
            local = dot(cv[rows_of(c), lanes(h)], features, TN)
            states[c, h] = local
            local_in[h] = local_in[h] + local

    early.start()

    causal = lax.broadcasted_iota(jnp.int32, (CH, CH), 0) >= lax.broadcasted_iota(
        jnp.int32, (CH, CH), 1
    )

    @pl.loop(0, NCH)
    def _(c):
        qk = qk_of(c)
        for h in range(HEADS):
            moved = dot(qk, moves[2 * h]).astype(bf16)
            moved_q[h, rows_of(c)] = moved
            logits = dot(moved, qk, NT) * 0.25
            weight = jnp.where(causal, 1.0 + logits + 0.5 * logits * logits, 0.0).astype(bf16)
            saved_w[h, rows_of(c)] = weight
            saved_l[h, rows_of(c)] = jnp.where(causal, 0.25 + 0.25 * logits, 0.0)
            mix[rows_of(c), lanes(h)] = dot(weight, cv[rows_of(c), lanes(h)])

        @pl.when(c == 1)
        def _():
            early.middle()

    o_load.wait()

    @pl.loop(0, NCH)
    def _(c):
        c_load(c).wait()
        gh[rows_of(c)] = dot(cot[rows_of(c)], weights_o[...], NT) * gain

    @pl.loop(0, NCH)
    def _(c):
        qk = qk_of(c)
        for h in range(HEADS):
            a, b = factors(qk, 2 * h)
            phi_q[h, rows_of(c)] = (a * b).astype(bf16)

    early.late()
    for copy in bwd_fetch:
        copy.wait()
    for copy in spreads[0]:
        copy.start()
    early.end()
    local_out[...] = jnp.zeros(local_out.shape, f32)

    @pl.loop(0, NCH)
    def _(c):
        for h in range(HEADS):
            entering = state_in[h]
            state_in[h] = entering + states[c, h]
            scaled[c, h] = (entering * scale).astype(bf16)
            numerator = mix[rows_of(c), lanes(h)] + dot(phi_q[h, rows_of(c)], scaled[c, h], NT)
            inverse = lax.rsqrt(jnp.mean(numerator * numerator, -1, keepdims=True) + epsilon)
            normed = numerator * inverse
            heads[rows_of(c), lanes(h)] = (normed * gain[:, lanes(h)]).astype(bf16)
            grad = gh[rows_of(c), lanes(h)]
            d_numer = (grad - normed * jnp.mean(grad * normed, -1, keepdims=True)) * inverse
            rounded = d_numer.astype(bf16)
            dn[rows_of(c), lanes(h)] = rounded
            local = dot(rounded, phi_q[h, rows_of(c)], TN)
            grads[c, h] = local
            local_out[h] = local_out[h] + local
        fwd.send_own(c)

    later.start()
    fwd_fetch.wait()
    for copy in fwd_swaps:
        copy.start()

    @pl.loop(0, NCH)
    def _(c):
        qk = qk_of(c)
        d_qk = jnp.zeros((CH, 128), f32)
        for h in range(HEADS):
            rounded = dn[rows_of(c), lanes(h)]
            dconv[rows_of(c), lanes(h)] = dot(saved_w[h, rows_of(c)], rounded, TN)
            d_weight = dot(rounded, cv[rows_of(c), lanes(h)], NT)
            d_logits = (d_weight * saved_l[h, rows_of(c)]).astype(bf16)
            d_qk = d_qk + dot(d_logits, dot(qk, moves[2 * h + 1]).astype(bf16))
            d_qk = d_qk + dot(d_logits, moved_q[h, rows_of(c)], TN)
            a, b = factors(qk, 2 * h)
            d_phi = dot(rounded, scaled[c, h])
            d_qk = d_qk + dot((d_phi * b).astype(bf16), first[2 * h], NT)
            d_qk = d_qk + dot((d_phi * a).astype(bf16), second[2 * h], NT)
        dconv[rows_of(c), 2 * DV : LANES] = d_qk

        @pl.when(c == 0)
        def _():
            later.middle()

        @pl.when(c >= 1)
        def _():
            fwd.forward(c - 1)

    fwd.forward(NCH - 1)
    for copy in spread_waits[0]:
        copy.wait()
    for copy in relays[0]:
        copy.start()
    later.late()
    later.end()
    state_out[...] = state_out[...] + local_out[...]

    def project_back(c):
        window = dconv[pl.ds(pl.multiple_of(c * CH, CH), CH + 8)]
        mixed = t0 * window[:CH] + (
            t1 * pltpu.roll(window, CH + 7, 0)[:CH] + t2 * pltpu.roll(window, CH + 6, 0)[:CH]
        )
        held_v[0, rows_of(c)] = mixed[:, : 2 * DV].astype(bf16)
        packed = mixed[: CH // 2, 2 * DV :] + pltpu.roll(mixed[CH // 2 :, 2 * DV :], 64, 1)
        held_qk[0, rows_of(c, CH // 2)] = packed.astype(bf16)

    @pl.loop(0, NCH)
    def _(c):
        qk = qk_of(c)
        d_qk = dconv[rows_of(c), 2 * DV : LANES]
        for h in range(HEADS):
            remaining = state_out[h] - grads[c, h]
            state_out[h] = remaining
            suffix = (remaining * scale).astype(bf16)
            dconv[rows_of(c), lanes(h)] = dconv[rows_of(c), lanes(h)] + dot(
                phi_k[h, rows_of(c)], suffix, NT
            )
            a, b = factors(qk, 2 * h + 1)
            d_phi = dot(cv[rows_of(c), lanes(h)], suffix)
            d_qk = d_qk + dot((d_phi * b).astype(bf16), first[2 * h + 1], NT)
            d_qk = d_qk + dot((d_phi * a).astype(bf16), second[2 * h + 1], NT)
        dconv[rows_of(c), 2 * DV : LANES] = d_qk

        @pl.when(c == 0)
        def _():
            behind.start()
            for copy in spreads[1]:
                copy.start()

        @pl.when(c > 0)
        def _():
            project_back(c - 1)

        @pl.when(c > 0)
        def _():
            bwd.send_own(c - 1)

    behind.wait()
    dconv[pl.ds(NCH * CH, 8)] = halo_out[...] * one_if(place < 7)
    project_back(NCH - 1)
    bwd.send_own(NCH - 1)

    for copy in fwd_swaps + own_waits + res_loads:
        copy.wait()

    @pl.loop(0, NCH)
    def _(j):
        fwd.compute(j)

    @pl.loop(0, NCH)
    def _(j):
        bwd.forward(j)
        fwd.send(j)

        @pl.when(j == 0)
        def _():
            for copy in relay_waits[0] + spread_waits[1]:
                copy.wait()
            for copy in bwd_swaps[0] + relays[1]:
                copy.start()

    for copy in bwd_swaps[0]:
        copy.wait()

    @pl.loop(0, NCH + 3)
    def _(i):
        @pl.when(i < NCH)
        def _():
            bwd.multiply(i)

        @pl.when(i == 0)
        def _():
            for copy in relay_waits[1]:
                copy.wait()
            for copy in bwd_swaps[1]:
                copy.start()
            for copy in bwd_swaps[1]:
                copy.wait()

        @pl.when((i >= 1) & (i < NCH + 1))
        def _():
            fwd.relayed(i - 1)

        @pl.when(i >= 3)
        def _():
            bwd.relayed(i - 3)

    @pl.loop(0, NCH)
    def _(i):
        fwd.finish(i)
        bwd.finish(i)

    fwd.drain()
    bwd.drain()

    early.drain()
    later.drain()


def settle_kernel(first, second, first_out, second_out, held, in_sem, out_sem):
    pairs = ((first, first_out), (second, second_out))
    ins = [pltpu.make_async_copy(p[0], held.at[n], in_sem.at[n]) for n, p in enumerate(pairs)]
    outs = [pltpu.make_async_copy(held.at[n], p[1], out_sem.at[n]) for n, p in enumerate(pairs)]
    for copy in ins:
        copy.start()
    for n in range(2):
        ins[n].wait()
        outs[n].start()
    for copy in outs:
        copy.wait()


def settle(first, second):
    whole = pl.BlockSpec(memory_space=pl.ANY)
    result = jax.ShapeDtypeStruct(first.shape, first.dtype)
    dma = pltpu.SemaphoreType.DMA
    return pl.pallas_call(
        settle_kernel,
        out_shape=(result, result),
        in_specs=[whole] * 2,
        out_specs=(whole, whole),
        scratch_shapes=[pltpu.VMEM((2,) + first.shape, first.dtype), dma((2,)), dma((2,))],
    )(first, second)


def per_device(inputs, cotangent, w_in, conv_w, norm_gain, w_out, keep_flags):
    count, width = inputs.shape
    first, second, rows, moves = selectors()
    consts = [jnp.asarray(part, bf16) for part in (first, second, moves)]
    whole, near = pl.BlockSpec(memory_space=pl.ANY), pl.BlockSpec(memory_space=pltpu.VMEM)
    result = jax.ShapeDtypeStruct((count, 256), bf16)
    dma = pltpu.SemaphoreType.DMA
    state = (DV, EXP)
    lump = (160, DV)
    carry_bufs = [pltpu.VMEM((n,) + lump if n > 1 else lump, bf16) for n in (1, 1, 1, 3, 1, 1)]
    carry_sems = [dma((4,)), dma((3,)), dma((3,))]
    results = pl.pallas_call(
        layer_kernel,
        out_shape=(result, result),
        in_specs=[whole] * 7 + [near] * 3 + [pl.BlockSpec(memory_space=pltpu.SMEM)],
        out_specs=(whole, whole),
        scratch_shapes=ring_buffers(count)
        + ring_buffers(count)
        + ring_semaphores()
        + ring_semaphores()
        + [
            pltpu.VMEM((4, count, 256), bf16),
            pltpu.VMEM((4, count, 256), bf16),
            pltpu.VMEM((4, count // 2, 128), bf16),
            pltpu.VMEM((2, 4, 4, 64, 256), bf16),
            pltpu.VMEM((CH, 256), bf16),
            pltpu.VMEM((HEADS, count, CH), bf16),
            pltpu.VMEM((HEADS, count, CH), f32),
            pltpu.VMEM((HEADS, count, 128), bf16),
        ]
        + [dma((1,)), dma((3, NCH))] * 3
        + [dma((1,))] * 4
        + [dma((1,)), dma((2,))]
        + [dma((2,))] * 2
        + [dma((2, 2))] * 4
        + [dma((2, 2))] * 2
        + carry_bufs
        + carry_bufs
        + carry_sems
        + carry_sems
        + [
            pltpu.VMEM((count, width), bf16),
            pltpu.VMEM((count, width), bf16),
            pltpu.VMEM((LANES, width), bf16),
            pltpu.VMEM((256, width), bf16),
            pltpu.VMEM((count + 8, LANES), f32),
            pltpu.VMEM((count, LANES), bf16),
            pltpu.VMEM((count, 256), f32),
            pltpu.VMEM((count, 256), f32),
            pltpu.VMEM((count, 256), bf16),
            pltpu.VMEM((HEADS, count, EXP), bf16),
            pltpu.VMEM((HEADS, count, EXP), bf16),
            pltpu.VMEM((NCH, HEADS) + state, f32),
            pltpu.VMEM((NCH, HEADS) + state, f32),
            pltpu.VMEM((NCH, HEADS) + state, bf16),
            pltpu.VMEM((HEADS,) + state, f32),
            pltpu.VMEM((HEADS,) + state, f32),
            pltpu.VMEM((HEADS,) + state, f32),
            pltpu.VMEM((HEADS,) + state, f32),
            pltpu.VMEM((8, LANES), f32),
            pltpu.VMEM((8, LANES), f32),
            pltpu.VMEM((4, 128, EXP), bf16),
            pltpu.VMEM((4, 128, EXP), bf16),
            pltpu.VMEM((4, 128, 128), bf16),
            dma((NCH,)),
            dma((NCH,)),
            dma((4,)),
            dma((1,)),
            dma((2,)),
            dma((4,)),
            dma((3,)),
        ],
        compiler_params=pltpu.CompilerParams(
            collective_id=0, has_side_effects=True, vmem_limit_bytes=67043328
        ),
    )(
        inputs,
        cotangent,
        w_in.T,
        w_out,
        *consts,
        conv_w,
        norm_gain.reshape(1, HEADS * DV),
        jnp.asarray(rows),
        keep_flags,
    )
    return settle(*results)


def solution(mesh):
    placed = (
        P("seq", None),
        P("seq", None),
        P(None, "tp"),
        P(None, "tp"),
        P("tp"),
        P("tp", None),
        P("tp"),
    )
    return jax.shard_map(
        per_device,
        mesh=mesh,
        in_specs=placed,
        out_specs=(P("seq", "tp"), P("seq", "tp")),
        check_vma=False,
    )
```

```python
from functools import partial

import jax
import jax.numpy as jnp
import numpy as np
from jax import lax
from jax.experimental import pallas as pl
from jax.experimental.pallas import tpu as pltpu
from jax.sharding import PartitionSpec as P

FEAT = 16
DV = 128
LANES = 384
EXP = 256
HEADS = 2
epsilon = 1e-06

CH = 256
NCH = 4
MESH = pl.DeviceIdType.MESH
NT = (((1,), (1,)), ((), ()))
NN = (((1,), (0,)), ((), ()))
TN = (((0,), (0,)), ((), ()))
f32 = jnp.float32
bf16 = jnp.bfloat16


def neighbour(along, step):
    place = lax.axis_index("tp")
    column, row = lax.rem(place, 4), lax.div(place, 4)
    if along == "x":
        return row * 4 + lax.rem(column + step, 4)
    return lax.rem(row + step, 4) * 4 + column


def block_at(a_along, a_step, r_along, r_step):
    place = lax.axis_index("tp")
    column, row = lax.rem(place, 4), lax.div(place, 4)
    x_step = a_step if a_along == "x" else r_step
    y_step = a_step if a_along == "y" else r_step
    return lax.rem(row + y_step, 4) * 4 + lax.rem(column + x_step, 4)


def to_device(src, dst, send_sem, recv_sem, place):
    return pltpu.make_async_remote_copy(
        src_ref=src,
        dst_ref=dst,
        send_sem=send_sem,
        recv_sem=recv_sem,
        device_id={"tp": place},
        device_id_type=MESH,
    )


def to_seq(src, dst, send_sem, recv_sem, place):
    return pltpu.make_async_remote_copy(
        src_ref=src,
        dst_ref=dst,
        send_sem=send_sem,
        recv_sem=recv_sem,
        device_id={"seq": place},
        device_id_type=MESH,
    )


def dot(a, b, dims=NN):
    return lax.dot_general(a, b, dims, preferred_element_type=f32)


def rows_of(c, size=CH):
    return pl.ds(pl.multiple_of(c * size, size), size)


def way(c):
    return jnp.where(c < NCH // 2, 1, 3)


class Ring:
    def __init__(self, flip, streams, weight, part, landed, relay, keep, res, out, sems):
        self.flip, self.streams, self.weight = flip, streams, weight
        self.part, self.landed, self.relay = part, landed, relay
        self.keep, self.res, self.out = keep, res, out
        (self.ps, self.tr, self.pr, self.os) = sems

    def turn(self, c):
        return lax.rem(c + self.flip, 2)

    def gather_to(self, c, d):
        return jnp.where(self.turn(c) == 0, neighbour("x", d), neighbour("y", d))

    def scatter_to(self, c, d):
        return jnp.where(self.turn(c) == 0, neighbour("y", d), neighbour("x", d))

    def direct(self, c, d):
        return [
            to_device(
                held.at[0, rows_of(c, size)],
                held.at[d, rows_of(c, size)],
                send.at[0],
                recv.at[d - 1, c],
                self.gather_to(c, d),
            )
            for held, size, send, recv in self.streams
        ]

    def passed_on(self, c):
        return [
            to_device(
                held.at[way(c), rows_of(c, size)],
                held.at[2, rows_of(c, size)],
                send.at[0],
                recv.at[1, c],
                self.gather_to(c, way(c)),
            )
            for held, size, send, recv in self.streams
        ]

    def send_own(self, c):
        for d in (1, 3):
            for copy in self.direct(c, d):
                copy.start()

    def forward(self, c):
        for d in (1, 3):
            for copy in self.direct(c, d):
                copy.wait_recv()
        for copy in self.passed_on(c):
            copy.start()

    def tie(self, c):
        return to_device(
            self.part.at[2, rows_of(c)],
            self.relay.at[rows_of(c)],
            self.ps.at[0],
            self.tr.at[c],
            self.scatter_to(c, way(c)),
        )

    def side(self, c, d):
        return to_device(
            self.part.at[d, rows_of(c)],
            self.landed.at[d // 2, rows_of(c)],
            self.ps.at[0],
            self.pr.at[d // 2, c],
            self.scatter_to(c, d),
        )

    def prepare(self, c):
        pass

    def product(self, c, k):
        held = self.streams[0][0]
        total = None
        for o in range(4):
            term = dot(held[o, rows_of(c)], self.weight[self.turn(c), k, o])
            total = term if total is None else total + term
        return total

    def compute(self, c):
        for copy in self.passed_on(c):
            copy.wait_recv()
        self.prepare(c)
        near, far = way(c), 4 - way(c)
        self.part[2, rows_of(c)] = self.product(c, 2).astype(bf16)
        self.part[far, rows_of(c)] = self.product(c, far).astype(bf16)
        self.keep[1, rows_of(c)] = self.product(c, near)
        self.keep[0, rows_of(c)] = self.product(c, 0) + self.res[rows_of(c)].astype(f32)

    def send(self, c):
        self.tie(c).start()
        self.side(c, 4 - way(c)).start()

    def multiply(self, c):
        for copy in self.passed_on(c):
            copy.wait_recv()
        self.prepare(c)
        near, far = way(c), 4 - way(c)
        self.part[2, rows_of(c)] = self.product(c, 2).astype(bf16)
        self.tie(c).start()
        self.keep[1, rows_of(c)] = self.product(c, near)
        self.part[far, rows_of(c)] = self.product(c, far).astype(bf16)
        self.side(c, far).start()
        self.keep[0, rows_of(c)] = self.product(c, 0) + self.res[rows_of(c)].astype(f32)

    def relayed(self, c):
        self.tie(c).wait_recv()
        near = way(c)
        total = self.keep[1, rows_of(c)] + self.relay[rows_of(c)].astype(f32)
        self.part[near, rows_of(c)] = total.astype(bf16)
        self.side(c, near).start()

    def finish(self, c):
        self.side(c, 1).wait_recv()
        self.side(c, 3).wait_recv()
        total = self.keep[0, rows_of(c)] + (
            self.landed[0, rows_of(c)].astype(f32) + self.landed[1, rows_of(c)].astype(f32)
        )
        self.part[0, rows_of(c)] = total.astype(bf16)
        self.leave(c).start()

    def leave(self, c):
        return pltpu.make_async_copy(
            self.part.at[0, rows_of(c)], self.out.at[rows_of(c)], self.os.at[0]
        )

    def drain(self):
        for held, _, send, recv in self.streams:
            sent = held.at[pl.ds(1, 3)]
            to_device(sent, sent, send.at[0], recv.at[0, 0], self.gather_to(0, 1)).wait_send()
        sent = self.part.at[pl.ds(1, 3)]
        to_device(sent, sent, self.ps.at[0], self.tr.at[0], self.scatter_to(0, 1)).wait_send()
        pltpu.make_async_copy(self.part.at[0], self.out, self.os.at[0]).wait()


class SplitRing(Ring):
    def prepare(self, c):
        packed = self.streams[1][0]
        low = lax.broadcasted_iota(jnp.int32, (CH // 2, 128), 1) < 64
        for pair in range(2):
            one = packed[2 * pair, rows_of(c, CH // 2)].astype(f32)
            two = packed[2 * pair + 1, rows_of(c, CH // 2)].astype(f32)
            top = jnp.where(low, one, pltpu.roll(two, 64, 1))
            bottom = jnp.where(low, pltpu.roll(one, 64, 1), two)
            lanes = slice(pair * 128, pair * 128 + 128)
            self.flat[0 : CH // 2, lanes] = top.astype(bf16)
            self.flat[CH // 2 : CH, lanes] = bottom.astype(bf16)

    def product(self, c, k):
        return super().product(c, k) + dot(self.flat[...], self.weight_qk[self.turn(c), k].reshape(256, 256))


def ring_semaphores():
    dma = pltpu.SemaphoreType.DMA
    return [dma((1,)), dma((NCH,)), dma((2, NCH)), dma((1,))]


def ring_buffers(rows):
    return [
        pltpu.VMEM((2, 4, 4, 256, 256), bf16),
        pltpu.VMEM((4, rows, 256), bf16),
        pltpu.VMEM((2, rows, 256), bf16),
        pltpu.VMEM((rows, 256), bf16),
        pltpu.VMEM((2, rows, 256), f32),
        pltpu.VMEM((rows, 256), bf16),
    ]


def selectors():
    first = np.zeros((4, 128, EXP), np.float32)
    second = np.zeros((4, 128, EXP), np.float32)
    rows = np.zeros((8, EXP), np.float32)
    rows[0, 0] = rows[1, 0] = rows[2, 0] = 1.0
    for group in range(4):
        base = group * FEAT
        for i in range(FEAT):
            first[group, base + i, 1 + i] = 1.0
            rows[1, 1 + i] = 1.0
            rows[2, 1 + i] = 0.25
        e = 1 + FEAT
        for i in range(FEAT):
            for j in range(i, FEAT):
                first[group, base + i, e] = 1.0
                second[group, base + j, e] = 1.0
                rows[2, e] = 1 / 32 if i == j else 1 / 16
                e += 1
    moves = np.zeros((4, 128, 128), np.float32)
    for h in range(HEADS):
        for i in range(FEAT):
            q, k = 2 * h * FEAT + i, (2 * h + 1) * FEAT + i
            moves[2 * h, q, k] = 1.0
            moves[2 * h + 1, k, q] = 1.0
    return first, second, rows, moves


def one_if(condition):
    return jnp.where(condition, 1.0, 0.0).astype(f32)


def packed_state(state):
    rest = state[:32, DV:]
    for g in range(1, 4):
        rest = rest + pltpu.roll(state[32 * g : 32 * g + 32, DV:], 32 * g, 1)
    return jnp.concatenate([state[:, :DV], rest], 0)


def whole_state(packed):
    low = lax.broadcasted_iota(jnp.int32, (32, DV), 1) < 32
    rest = packed[DV:]
    parts = [rest] + [pltpu.roll(rest, DV - 32 * g, 1) for g in range(1, 4)]
    parts = [jnp.where(low, part, 0.0) for part in parts]
    return jnp.concatenate([packed[:DV], jnp.concatenate(parts, 0)], 1)


class Carry:
    def __init__(self, earlier, local, state, bufs, sems):
        self.earlier, self.local, self.state = earlier, local, state
        self.sa, self.ra, self.sb, self.rb, self.sc, self.rc = bufs
        self.pair_sems, self.zs, self.zr = sems
        place = lax.axis_index("seq")
        self.core, self.z = lax.rem(place, 2), lax.div(place, 2)
        self.partner = self.z * 2 + (1 - self.core)

    def swap(self):
        return to_seq(self.sa, self.ra, self.pair_sems.at[0], self.pair_sems.at[1], self.partner)

    def give(self):
        return to_seq(self.sc, self.rc, self.pair_sems.at[2], self.pair_sems.at[3], self.partner)

    def along(self, step):
        there = lax.rem(self.z + step, 4) * 2 + self.core
        return to_seq(
            self.sb, self.rb.at[step - 1], self.zs.at[step - 1], self.zr.at[step - 1], there
        )

    def start(self):
        self.sa[...] = packed_state(self.local[1 - self.core]).astype(bf16)
        self.swap().start()

    def middle(self):
        self.swap().wait_recv()
        self.sb[...] = (packed_state(self.local[self.core]) + self.ra[...].astype(f32)).astype(bf16)
        for step in (1, 2, 3):
            self.along(step).start()

    def late(self):
        total = jnp.zeros(self.sb.shape, f32)
        for step in (1, 2, 3):
            self.along(step).wait_recv()
            counts = one_if(self.z >= step if self.earlier else self.z < step)
            total = total + self.rb[step - 1].astype(f32) * counts
        takes = self.core if self.earlier else 1 - self.core
        own = packed_state(self.local[self.core]) * one_if(takes == 0)
        self.sc[...] = (total + own).astype(bf16)
        self.give().start()
        self.state[self.core] = whole_state(total + self.ra[...].astype(f32) * one_if(takes == 1))

    def end(self):
        self.give().wait_recv()
        self.state[1 - self.core] = whole_state(self.rc[...].astype(f32))

    def drain(self):
        self.swap().wait_send()
        self.give().wait_send()
        for step in (1, 2, 3):
            self.along(step).wait_send()


def layer_kernel(
    inputs, cotangent, w_t, w_out, first_any, second_any, moves_any, conv, gains, rows, keep,
    layer_out, input_grad, *scratch,
):
    take = list(scratch)

    def pop(n):
        got = take[:n]
        del take[:n]
        return got

    fwd_bufs, bwd_bufs = pop(6), pop(6)
    fwd_sems, bwd_sems = pop(4), pop(4)
    (held_h, held_v, held_qk, weight_qk, flat, saved_w, saved_l, moved_q) = pop(8)
    (gs_h, gr_h, gs_v, gr_v, gs_q, gr_q) = pop(6)
    (ws, wr, us, ur, w_own, q_own) = pop(6)
    (fs, fr, zcs, zcr, rys, ryr, ss, sr) = pop(8)
    early_bufs, late_bufs = pop(6), pop(6)
    early_sems, late_sems = pop(3), pop(3)
    (xin, cot, weights_t, weights_o) = pop(4)
    (pp, cv, mix, gh, dn, phi_q, phi_k, states, grads, scaled) = pop(10)
    dconv = pp
    (state_in, state_out, local_in, local_out, halo_in, halo_out) = pop(6)
    (first, second, moves) = pop(3)
    (x_sem, c_sem, w_sem, o_sem, r_sem, h_sem, k_sem) = pop(7)

    tp, place = lax.axis_index("tp"), lax.axis_index("seq")

    core, z = lax.rem(place, 2), lax.div(place, 2)
    fwd = Ring(1, [(held_h, CH, gs_h, gr_h)], *fwd_bufs, layer_out, fwd_sems)
    streams = [(held_v, CH, gs_v, gr_v), (held_qk, CH // 2, gs_q, gr_q)]
    bwd = SplitRing(0, streams, *bwd_bufs, input_grad, bwd_sems)
    bwd.flat, bwd.weight_qk = flat, weight_qk
    early = Carry(True, local_in, state_in, early_bufs, early_sems)
    later = Carry(False, local_out, state_out, late_bufs, late_sems)
    heads = held_h.at[0]

    def columns(t):
        return pl.ds(pl.multiple_of(t * 256, 256), 256)

    def out_block(t):
        return w_out.at[:, columns(t)]

    def swap_device():
        return place + 1 - 2 * core

    sides = ((bwd.weight, 128, 0), (weight_qk, 32, 256))
    fwd_weights, fwd_swaps, fwd_own, bwd_own = [], [], [], []
    bwd_weights, spreads, relays, bwd_swaps = [], ([], []), ([], []), ([], [])
    for p, (a, r) in enumerate((("x", "y"), ("y", "x"))):
        for d in (1, 2, 3):
            for j in range(2):
                k = core * 2 + j
                block = fwd.weight.at[p, k, d]
                wanted = out_block(block_at(a, d, r, k))
                fwd_weights.append(to_device(wanted, block, ws.at[0], wr.at[0], neighbour(a, d)))
        for n, (array, size, start) in enumerate(sides):
            half = rows_of(core, size)
            theirs = pl.ds(pl.multiple_of(start + core * size, size), size)
            for d in (1, 2, 3):
                wanted = weights_t.at[theirs, columns(block_at(a, d, r, z))]
                bwd_weights.append(
                    to_device(wanted, array.at[p, z, d, half], fs.at[n], fr.at[n], neighbour(a, d))
                )
            for n_way, step in enumerate((1, 3)):
                at = (p, n)
                there = lax.rem(z + step, 4) * 2 + core
                mine = array.at[p, z, pl.ds(1, 3), half]
                spreads[p].append(to_seq(mine, mine, zcs.at[at], zcr.at[at], there))
                near = lax.rem(z + 4 - step, 4)
                rows_in = pl.ds(
                    pl.multiple_of(core * size + n_way * (size // 2), size // 2), size // 2
                )
                passing = array.at[p, near, pl.ds(1, 3), rows_in]
                relays[p].append(to_seq(passing, passing, rys.at[at], ryr.at[at], there))
            ours = array.at[p, :, pl.ds(1, 3), half]
            bwd_swaps[p].append(to_seq(ours, ours, ss.at[p, n], sr.at[p, n], swap_device()))
        for k in range(4):
            t = block_at(a, 0, r, k)
            fwd_own.append(
                pltpu.make_async_copy(out_block(t), fwd.weight.at[p, k, 0], w_own.at[0])
            )
            for n, (array, size, start) in enumerate(sides):
                wanted = weights_t.at[pl.ds(start, 2 * size), columns(t)]
                bwd_own.append(
                    pltpu.make_async_copy(wanted, array.at[p, k, 0], q_own.at[n])
                )

    fetched = fwd.weight.at[:, pl.ds(core * 2, 2), pl.ds(1, 3)]
    fwd_fetch = to_device(fetched, fetched, ws.at[0], wr.at[0], neighbour("x", 1))
    fwd_swaps.append(to_seq(fetched, fetched, us.at[0], ur.at[0], swap_device()))
    owned = fwd.weight.at[:, :, 0]
    own_waits = [pltpu.make_async_copy(owned, owned, w_own.at[0])]
    bwd_fetch, spread_waits, relay_waits = [], ([], []), ([], [])
    for n, (array, size, start) in enumerate(sides):
        owned = array.at[:, :, 0]
        own_waits.append(pltpu.make_async_copy(owned, owned, q_own.at[n]))
        fetched = array.at[:, z, pl.ds(1, 3), rows_of(core, size)]
        bwd_fetch.append(to_device(fetched, fetched, fs.at[n], fr.at[n], neighbour("x", 1)))
        for p in range(2):
            both = array.at[p, pl.ds(0, 2), pl.ds(1, 3), rows_of(core, size)]
            one = array.at[p, z, pl.ds(1, 3), rows_of(core, size)]
            there = lax.rem(z + 1, 4) * 2 + core
            spread_waits[p].append(to_seq(both, both, zcs.at[p, n], zcr.at[p, n], there))
            relay_waits[p].append(to_seq(one, one, rys.at[p, n], ryr.at[p, n], there))

    pieces = ((32, 128, 0), (192, 128, 128), (0, 32, 256), (160, 32, 288))
    w_loads = [
        pltpu.make_async_copy(
            w_t.at[pl.ds(src, size)], weights_t.at[pl.ds(dst, size)], w_sem.at[n]
        )
        for n, (src, size, dst) in enumerate(pieces)
    ]
    for copy in w_loads:
        copy.start()

    def x_load(c):
        return pltpu.make_async_copy(inputs.at[rows_of(c)], xin.at[rows_of(c)], x_sem.at[c])

    def c_load(c):
        return pltpu.make_async_copy(cotangent.at[rows_of(c)], cot.at[rows_of(c)], c_sem.at[c])

    x_load(3).start()
    barrier = pltpu.get_barrier_semaphore()
    for d in (1, 2, 3):
        for along in ("x", "y"):
            pl.semaphore_signal(
                barrier, inc=1, device_id={"tp": neighbour(along, d)}, device_id_type=MESH
            )
    for d in (1, 2, 4, 6, 7):
        pl.semaphore_signal(
            barrier, inc=1, device_id={"seq": lax.rem(place + d, 8)}, device_id_type=MESH
        )
    weights_t[pl.ds(320, 64)] = jnp.zeros((64, weights_t.shape[1]), bf16)
    const_loads = [
        pltpu.make_async_copy(src, dst, k_sem.at[n])
        for n, (src, dst) in enumerate(
            ((first_any, first), (second_any, second), (moves_any, moves))
        )
    ]
    o_load = pltpu.make_async_copy(w_out, weights_o, o_sem.at[0])
    res_loads = [
        pltpu.make_async_copy(inputs.at[:, columns(tp)], fwd.res, r_sem.at[0]),
        pltpu.make_async_copy(cotangent.at[:, columns(tp)], bwd.res, r_sem.at[1]),
    ]
    src = lax.broadcasted_iota(jnp.int32, (320, LANES), 0)
    dst = lax.broadcasted_iota(jnp.int32, (320, LANES), 1)
    from_high = jnp.where(dst < 288, dst - 256, jnp.where(dst < 320, dst - 128, -1))
    source = jnp.where(dst < 128, dst + 32, jnp.where(dst < 256, dst + 64, from_high))
    taps = lax.dot_general(
        conv[...],
        jnp.where(src == source, 1.0, 0.0).astype(f32),
        NN,
        precision=lax.Precision.HIGHEST,
        preferred_element_type=f32,
    )
    lane = lax.broadcasted_iota(jnp.int32, (1, HEADS * DV), 1)
    gain = gains[...] * jnp.where(lane < DV, keep[0].astype(f32), keep[1].astype(f32))

    for copy in w_loads:
        copy.wait()
    for c in (0, 1, 2):
        x_load(c).start()
    for copy in const_loads + [o_load] + res_loads + fwd_own + bwd_own:
        copy.start()

    ahead = to_seq(
        pp.at[pl.ds(NCH * CH, 8)], halo_in, h_sem.at[0], h_sem.at[1], lax.rem(place + 1, 8)
    )
    behind = to_seq(
        dconv.at[pl.ds(0, 8)], halo_out, h_sem.at[2], h_sem.at[3], lax.rem(place + 7, 8)
    )

    @pl.loop(0, NCH)
    def _(i):
        c = lax.rem(i + NCH - 1, NCH)
        x_load(c).wait()
        c_load(c).start()
        projected = dot(xin[rows_of(c)], weights_t[...], NT).astype(bf16).astype(f32)
        pp[pl.ds(pl.multiple_of(c * CH + 8, 8), CH)] = projected

        @pl.when(i == 0)
        def _():
            pl.semaphore_wait(barrier, 11)
            ahead.start()
            for copy in bwd_weights + fwd_weights:
                copy.start()

    for copy in const_loads:
        copy.wait()
    ahead.wait()
    pp[pl.ds(0, 8)] = halo_in[...] * one_if(place > 0)

    t0, t1, t2 = taps[0:1], taps[1:2], taps[2:3]
    bias_a, bias_b, scale = rows[0:1], rows[1:2], rows[2:3]

    def factors(qk, group):
        return dot(qk, first[group]) + bias_a, dot(qk, second[group]) + bias_b

    def lanes(h):
        return slice(h * DV, (h + 1) * DV)

    def qk_of(c):
        return cv[rows_of(c), 2 * DV : LANES]

    local_in[...] = jnp.zeros(local_in.shape, f32)

    @pl.loop(0, NCH)
    def _(c):
        window = pp[pl.ds(pl.multiple_of(c * CH, CH), CH + 8)]
        mixed = t0 * window[8:] + (
            t1 * pltpu.roll(window, 1, 0)[8:] + t2 * pltpu.roll(window, 2, 0)[8:]
        )
        cv[rows_of(c)] = mixed.astype(bf16)
        qk = qk_of(c)
        for h in range(HEADS):
            a, b = factors(qk, 2 * h + 1)
            features = (a * b).astype(bf16)
            phi_k[h, rows_of(c)] = features
            local = dot(cv[rows_of(c), lanes(h)], features, TN)
            states[c, h] = local
            local_in[h] = local_in[h] + local

    early.start()

    causal = lax.broadcasted_iota(jnp.int32, (CH, CH), 0) >= lax.broadcasted_iota(
        jnp.int32, (CH, CH), 1
    )

    @pl.loop(0, NCH)
    def _(c):
        qk = qk_of(c)
        for h in range(HEADS):
            moved = dot(qk, moves[2 * h]).astype(bf16)
            moved_q[h, rows_of(c)] = moved
            logits = dot(moved, qk, NT) * 0.25
            weight = jnp.where(causal, 1.0 + logits + 0.5 * logits * logits, 0.0).astype(bf16)
            saved_w[h, rows_of(c)] = weight
            saved_l[h, rows_of(c)] = jnp.where(causal, 0.25 + 0.25 * logits, 0.0)
            mix[rows_of(c), lanes(h)] = dot(weight, cv[rows_of(c), lanes(h)])

        @pl.when(c == 1)
        def _():
            early.middle()

    o_load.wait()

    @pl.loop(0, NCH)
    def _(c):
        c_load(c).wait()
        gh[rows_of(c)] = dot(cot[rows_of(c)], weights_o[...], NT) * gain

    @pl.loop(0, NCH)
    def _(c):
        qk = qk_of(c)
        for h in range(HEADS):
            a, b = factors(qk, 2 * h)
            phi_q[h, rows_of(c)] = (a * b).astype(bf16)

    early.late()
    for copy in bwd_fetch:
        copy.wait()
    for copy in spreads[0]:
        copy.start()
    early.end()
    local_out[...] = jnp.zeros(local_out.shape, f32)

    @pl.loop(0, NCH)
    def _(c):
        for h in range(HEADS):
            entering = state_in[h]
            state_in[h] = entering + states[c, h]
            scaled[c, h] = (entering * scale).astype(bf16)
            numerator = mix[rows_of(c), lanes(h)] + dot(phi_q[h, rows_of(c)], scaled[c, h], NT)
            inverse = lax.rsqrt(jnp.mean(numerator * numerator, -1, keepdims=True) + epsilon)
            normed = numerator * inverse
            heads[rows_of(c), lanes(h)] = (normed * gain[:, lanes(h)]).astype(bf16)
            grad = gh[rows_of(c), lanes(h)]
            d_numer = (grad - normed * jnp.mean(grad * normed, -1, keepdims=True)) * inverse
            rounded = d_numer.astype(bf16)
            dn[rows_of(c), lanes(h)] = rounded
            local = dot(rounded, phi_q[h, rows_of(c)], TN)
            grads[c, h] = local
            local_out[h] = local_out[h] + local
        fwd.send_own(c)

    later.start()
    fwd_fetch.wait()
    for copy in fwd_swaps:
        copy.start()

    @pl.loop(0, NCH)
    def _(c):
        qk = qk_of(c)
        d_qk = jnp.zeros((CH, 128), f32)
        for h in range(HEADS):
            rounded = dn[rows_of(c), lanes(h)]
            dconv[rows_of(c), lanes(h)] = dot(saved_w[h, rows_of(c)], rounded, TN)
            d_weight = dot(rounded, cv[rows_of(c), lanes(h)], NT)
            d_logits = (d_weight * saved_l[h, rows_of(c)]).astype(bf16)
            d_qk = d_qk + dot(d_logits, dot(qk, moves[2 * h + 1]).astype(bf16))
            d_qk = d_qk + dot(d_logits, moved_q[h, rows_of(c)], TN)
            a, b = factors(qk, 2 * h)
            d_phi = dot(rounded, scaled[c, h])
            d_qk = d_qk + dot((d_phi * b).astype(bf16), first[2 * h], NT)
            d_qk = d_qk + dot((d_phi * a).astype(bf16), second[2 * h], NT)
        dconv[rows_of(c), 2 * DV : LANES] = d_qk

        @pl.when(c == 0)
        def _():
            later.middle()

        @pl.when(c >= 1)
        def _():
            fwd.forward(c - 1)

    fwd.forward(NCH - 1)
    for copy in spread_waits[0]:
        copy.wait()
    for copy in relays[0]:
        copy.start()
    later.late()
    later.end()
    state_out[...] = state_out[...] + local_out[...]

    def project_back(c):
        window = dconv[pl.ds(pl.multiple_of(c * CH, CH), CH + 8)]
        mixed = t0 * window[:CH] + (
            t1 * pltpu.roll(window, CH + 7, 0)[:CH] + t2 * pltpu.roll(window, CH + 6, 0)[:CH]
        )
        held_v[0, rows_of(c)] = mixed[:, : 2 * DV].astype(bf16)
        packed = mixed[: CH // 2, 2 * DV :] + pltpu.roll(mixed[CH // 2 :, 2 * DV :], 64, 1)
        held_qk[0, rows_of(c, CH // 2)] = packed.astype(bf16)

    @pl.loop(0, NCH)
    def _(c):
        qk = qk_of(c)
        d_qk = dconv[rows_of(c), 2 * DV : LANES]
        for h in range(HEADS):
            remaining = state_out[h] - grads[c, h]
            state_out[h] = remaining
            suffix = (remaining * scale).astype(bf16)
            dconv[rows_of(c), lanes(h)] = dconv[rows_of(c), lanes(h)] + dot(
                phi_k[h, rows_of(c)], suffix, NT
            )
            a, b = factors(qk, 2 * h + 1)
            d_phi = dot(cv[rows_of(c), lanes(h)], suffix)
            d_qk = d_qk + dot((d_phi * b).astype(bf16), first[2 * h + 1], NT)
            d_qk = d_qk + dot((d_phi * a).astype(bf16), second[2 * h + 1], NT)
        dconv[rows_of(c), 2 * DV : LANES] = d_qk

        @pl.when(c == 0)
        def _():
            behind.start()
            for copy in spreads[1]:
                copy.start()

        @pl.when(c > 0)
        def _():
            project_back(c - 1)

        @pl.when(c > 0)
        def _():
            bwd.send_own(c - 1)

    behind.wait()
    dconv[pl.ds(NCH * CH, 8)] = halo_out[...] * one_if(place < 7)
    project_back(NCH - 1)
    bwd.send_own(NCH - 1)

    for copy in fwd_swaps + own_waits + res_loads:
        copy.wait()

    @pl.loop(0, NCH)
    def _(j):
        fwd.compute(j)

    @pl.loop(0, NCH)
    def _(j):
        bwd.forward(j)
        fwd.send(j)

        @pl.when(j == 0)
        def _():
            for copy in relay_waits[0] + spread_waits[1]:
                copy.wait()
            for copy in bwd_swaps[0] + relays[1]:
                copy.start()

    for copy in bwd_swaps[0]:
        copy.wait()

    @pl.loop(0, NCH + 3)
    def _(i):
        @pl.when((i >= 1) & (i < NCH + 1))
        def _():
            fwd.relayed(i - 1)

        @pl.when(i < NCH)
        def _():
            bwd.multiply(i)

        @pl.when(i == 0)
        def _():
            for copy in relay_waits[1]:
                copy.wait()
            for copy in bwd_swaps[1]:
                copy.start()
            for copy in bwd_swaps[1]:
                copy.wait()

        @pl.when(i >= 3)
        def _():
            bwd.relayed(i - 3)

    @pl.loop(0, NCH)
    def _(i):
        fwd.finish(i)
        bwd.finish(i)

    fwd.drain()
    bwd.drain()

    early.drain()
    later.drain()


def settle_kernel(first, second, first_out, second_out, held, in_sem, out_sem):
    pairs = ((first, first_out), (second, second_out))
    ins = [pltpu.make_async_copy(p[0], held.at[n], in_sem.at[n]) for n, p in enumerate(pairs)]
    outs = [pltpu.make_async_copy(held.at[n], p[1], out_sem.at[n]) for n, p in enumerate(pairs)]
    for copy in ins:
        copy.start()
    for n in range(2):
        ins[n].wait()
        outs[n].start()
    for copy in outs:
        copy.wait()


def settle(first, second):
    whole = pl.BlockSpec(memory_space=pl.ANY)
    result = jax.ShapeDtypeStruct(first.shape, first.dtype)
    dma = pltpu.SemaphoreType.DMA
    return pl.pallas_call(
        settle_kernel,
        out_shape=(result, result),
        in_specs=[whole] * 2,
        out_specs=(whole, whole),
        scratch_shapes=[pltpu.VMEM((2,) + first.shape, first.dtype), dma((2,)), dma((2,))],
    )(first, second)


def per_device(inputs, cotangent, w_in, conv_w, norm_gain, w_out, keep_flags):
    count, width = inputs.shape
    first, second, rows, moves = selectors()
    consts = [jnp.asarray(part, bf16) for part in (first, second, moves)]
    whole, near = pl.BlockSpec(memory_space=pl.ANY), pl.BlockSpec(memory_space=pltpu.VMEM)
    result = jax.ShapeDtypeStruct((count, 256), bf16)
    dma = pltpu.SemaphoreType.DMA
    state = (DV, EXP)
    lump = (160, DV)
    carry_bufs = [pltpu.VMEM((n,) + lump if n > 1 else lump, bf16) for n in (1, 1, 1, 3, 1, 1)]
    carry_sems = [dma((4,)), dma((3,)), dma((3,))]
    results = pl.pallas_call(
        layer_kernel,
        out_shape=(result, result),
        in_specs=[whole] * 7 + [near] * 3 + [pl.BlockSpec(memory_space=pltpu.SMEM)],
        out_specs=(whole, whole),
        scratch_shapes=ring_buffers(count)
        + ring_buffers(count)
        + ring_semaphores()
        + ring_semaphores()
        + [
            pltpu.VMEM((4, count, 256), bf16),
            pltpu.VMEM((4, count, 256), bf16),
            pltpu.VMEM((4, count // 2, 128), bf16),
            pltpu.VMEM((2, 4, 4, 64, 256), bf16),
            pltpu.VMEM((CH, 256), bf16),
            pltpu.VMEM((HEADS, count, CH), bf16),
            pltpu.VMEM((HEADS, count, CH), f32),
            pltpu.VMEM((HEADS, count, 128), bf16),
        ]
        + [dma((1,)), dma((3, NCH))] * 3
        + [dma((1,))] * 4
        + [dma((1,)), dma((2,))]
        + [dma((2,))] * 2
        + [dma((2, 2))] * 4
        + [dma((2, 2))] * 2
        + carry_bufs
        + carry_bufs
        + carry_sems
        + carry_sems
        + [
            pltpu.VMEM((count, width), bf16),
            pltpu.VMEM((count, width), bf16),
            pltpu.VMEM((LANES, width), bf16),
            pltpu.VMEM((256, width), bf16),
            pltpu.VMEM((count + 8, LANES), f32),
            pltpu.VMEM((count, LANES), bf16),
            pltpu.VMEM((count, 256), f32),
            pltpu.VMEM((count, 256), f32),
            pltpu.VMEM((count, 256), bf16),
            pltpu.VMEM((HEADS, count, EXP), bf16),
            pltpu.VMEM((HEADS, count, EXP), bf16),
            pltpu.VMEM((NCH, HEADS) + state, f32),
            pltpu.VMEM((NCH, HEADS) + state, f32),
            pltpu.VMEM((NCH, HEADS) + state, bf16),
            pltpu.VMEM((HEADS,) + state, f32),
            pltpu.VMEM((HEADS,) + state, f32),
            pltpu.VMEM((HEADS,) + state, f32),
            pltpu.VMEM((HEADS,) + state, f32),
            pltpu.VMEM((8, LANES), f32),
            pltpu.VMEM((8, LANES), f32),
            pltpu.VMEM((4, 128, EXP), bf16),
            pltpu.VMEM((4, 128, EXP), bf16),
            pltpu.VMEM((4, 128, 128), bf16),
            dma((NCH,)),
            dma((NCH,)),
            dma((4,)),
            dma((1,)),
            dma((2,)),
            dma((4,)),
            dma((3,)),
        ],
        compiler_params=pltpu.CompilerParams(
            collective_id=0, has_side_effects=True, vmem_limit_bytes=67043328
        ),
    )(
        inputs,
        cotangent,
        w_in.T,
        w_out,
        *consts,
        conv_w,
        norm_gain.reshape(1, HEADS * DV),
        jnp.asarray(rows),
        keep_flags,
    )
    return settle(*results)


def solution(mesh):
    placed = (
        P("seq", None),
        P("seq", None),
        P(None, "tp"),
        P(None, "tp"),
        P("tp"),
        P("tp", None),
        P("tp"),
    )
    return jax.shard_map(
        per_device,
        mesh=mesh,
        in_specs=placed,
        out_specs=(P("seq", "tp"), P("seq", "tp")),
        check_vma=False,
    )
```
